32 devices in a mesh: section: 2 (over x), dp: 16 (over z, y, core).
Axes of the slice: x: 2, y: 2, z: 4, core: 2. Of those that a mesh axis runs over, the one named last changes fastest.
Arguments:
- section_input: bfloat16 [6, 1920, 1024], P(None, 'dp'), may hold values from -6 to 6
- out_cotangent: bfloat16 [6, 1920, 1024], P(None, 'dp'), may hold values from -6 to 6
- series_counts: int32 [6, 16], P(None, 'dp'), may hold values from 4 to 8
- norm_gains: float32 [4, 2048], P('section'), may hold values from 0.1 to 1.9
- biases: float32 [4, 8192], P('section'), may hold values from -4 to 4
- qkv_weight: bfloat16 [4, 1024, 3072], P('section'), may hold values from -0.1875 to 0.1875
- out_weight: bfloat16 [4, 1024, 1024], P('section'), may hold values from -0.3125 to 0.3125
- up_weight: bfloat16 [4, 1024, 2048], P('section'), may hold values from -0.1875 to 0.1875
- down_weight: bfloat16 [4, 2048, 1024], P('section'), may hold values from -0.125 to 0.125
Outputs:
- section_outputs: bfloat16 [2, 6, 1920, 1024], P('section', None, 'dp')
- section_input_grads: bfloat16 [2, 6, 1920, 1024], P('section', None, 'dp')
- grad_norm_gains: float32 [4, 2048], P('section', 'dp')
- grad_biases: float32 [4, 8192], P('section', 'dp')
- grad_qkv: float32 [4, 1024, 3072], P('section', 'dp')
- grad_out: float32 [4, 1024, 1024], P('section', 'dp')
- grad_up: float32 [4, 1024, 2048], P('section', 'dp')
- grad_down: float32 [4, 2048, 1024], P('section', 'dp')
The draws below stay inside these ranges and needn't reach their ends.
Inputs may be any that keep to these rules, and one draw needn't show every extreme that they name: `series_counts`: live series in the 8 slots of one dp index's share of a micro-batch; slots from the count on hold padding.
All inputs are finite; a program needn't handle non-finite values.
Results may differ from the reference program's by a relative error of at most 0.025.
Values may be sent and summed in bfloat16 or wider, within the bound.
No kernel may reach another device: no remote copies, remote signals or barrier semaphores. Data moves between devices by JAX's collectives and lax.ppermute only.
A program may use at most 256 MiB of HBM per device.

```python
import jax
import jax.numpy as jnp
from jax import lax

D = 1024
HEADS = 8
HEAD_DIM = 128
FF = 2048
SEG = 15
LAYERS_DEV = 2
MICRO = 6
SLOTS = 8
LAYERS = 4
ROWS = 1920
N_SECTION = 2
N_DP = 16


def plant(values, stream_key, low, largest):
    dims = values.shape
    spot = [jax.random.randint(jax.random.fold_in(stream_key, axis), (), 0, dims[axis]) for axis in range(len(dims))]
    values = values.at[tuple(spot)].set(low)
    longest = dims.index(max(dims))
    spot[longest] = (spot[longest] + 1) % dims[longest]
    return values.at[tuple(spot)].set(largest)


def steps_of(own_key, shape, cuts, smallest, top_value):
    loudness, own = 1.0, jax.random.fold_in(own_key, 6)
    for dim, blocks in cuts:
        draws = jnp.exp(jax.random.uniform(jax.random.fold_in(own, dim), (blocks,), jnp.float32, smallest / len(cuts), top_value / len(cuts)))
        loudness = loudness * jnp.repeat(draws, shape[dim] // blocks).reshape([-1 if axis == dim else 1 for axis in range(len(shape))])
    return loudness


def scatter_about(rng, dims, scale, most, cuts=(), kind=jnp.bfloat16):
    drawn = scale * jax.random.normal(rng, dims, jnp.float32)
    if cuts:
        drawn = drawn * steps_of(rng, dims, cuts, -0.22, 0.18)
    return jnp.clip(drawn, -most, most).astype(kind)


def setup_inputs(seed: int = 0) -> dict:
    key_list = jax.random.split(jax.random.key(seed), 10)
    return {
        "section_input": scatter_about(key_list[0], (MICRO, ROWS, D), 1.0, 6.0, ((1, 16),)),
        "out_cotangent": scatter_about(key_list[1], (MICRO, ROWS, D), 1.0, 6.0, ((1, 16),)),
        "series_counts": plant(jax.random.randint(key_list[2], (MICRO, N_DP), max(1, SLOTS // 2), SLOTS + 1), jax.random.fold_in(key_list[2], 1), max(1, SLOTS // 2), SLOTS).astype(jnp.int32),
        "norm_gains": jnp.clip(1.0 + 0.18 * jax.random.normal(key_list[3], (LAYERS, 2 * D), jnp.float32), 0.1, 1.9),
        "biases": scatter_about(key_list[4], (LAYERS, 6 * D + FF), 0.3, 4.0, ((0, 2),), jnp.float32),
        "qkv_weight": scatter_about(key_list[5], (LAYERS, D, 3 * D), D ** -0.5, 0.1875, ((0, 2),)),
        "out_weight": scatter_about(key_list[6], (LAYERS, D, D), (D // 3) ** -0.5, 0.3125, ((0, 2),)),
        "up_weight": scatter_about(key_list[7], (LAYERS, D, FF), D ** -0.5, 0.1875, ((0, 2),)),
        "down_weight": scatter_about(key_list[8], (LAYERS, FF, D), FF ** -0.5, 0.125, ((0, 2),)),
    }


@jax.custom_vjp
def low(v):
    return lax.optimization_barrier(v.astype(jnp.bfloat16)).astype(jnp.float32)

@jax.custom_vjp
def low_back(v):
    return v

def low_keep(v):
    return (low(v), None)

def low_pass(kept, grad):
    return (grad,)

def back_keep(v):
    return (v, None)

def back_low(kept, grad):
    return (low(grad),)
low.defvjp(low_keep, low_pass)
low_back.defvjp(back_keep, back_low)
EPSILON = 1e-05
HIGHEST = lax.Precision.HIGHEST
NEGATIVE = -1e+30

def matmul(left_side, right_side):
    return jnp.dot(left_side, right_side, precision=HIGHEST, preferred_element_type=jnp.float32)

def norm_rows(values, gain, shift):
    centre = lax.optimization_barrier(jnp.mean(values, axis=-1, keepdims=True))
    centred = values - centre
    spread = lax.optimization_barrier(jnp.mean(centred * centred, axis=-1, keepdims=True))
    return centred * lax.rsqrt(spread + EPSILON) * gain + shift

def layer_apply(residual, layer_gains, layer_biases, w_qkv, w_out, w_up, w_down):
    model_width = residual.shape[1]
    entry_one = low(norm_rows(residual, layer_gains[:model_width], layer_biases[:model_width]))
    qkv_bias = jnp.concatenate([layer_biases[model_width:2 * model_width], jnp.zeros_like(layer_biases[:model_width]), layer_biases[2 * model_width:3 * model_width]])
    qkv_rows = low(low_back(matmul(entry_one, w_qkv) + qkv_bias))
    head_rows = qkv_rows.reshape(-1, SEG, 3, HEADS, HEAD_DIM)
    query_heads = head_rows[:, :, 0]
    key_heads = head_rows[:, :, 1]
    value_heads = head_rows[:, :, 2]
    positions = jnp.arange(SEG, dtype=jnp.int32)
    causal = positions[:, None] >= positions[None, :]
    scores = jnp.einsum('sqhd,skhd->shqk', query_heads, key_heads, precision=HIGHEST) * HEAD_DIM ** (-0.5)
    scores = low_back(jnp.where(causal, scores, NEGATIVE))
    soft_weights = low(jax.nn.softmax(scores, axis=-1))
    attended = jnp.einsum('shqk,skhd->sqhd', soft_weights, value_heads, precision=HIGHEST)
    attended = low(low_back(attended.reshape(-1, model_width)))
    residual = residual + low_back(matmul(attended, w_out) + layer_biases[3 * model_width:4 * model_width])
    entry_two = low(norm_rows(residual, layer_gains[model_width:], layer_biases[4 * model_width:5 * model_width]))
    hidden_in = low_back(matmul(entry_two, w_up) + layer_biases[6 * model_width:])
    hidden = low(low_back(jax.nn.gelu(hidden_in)))
    return residual + low_back(matmul(hidden, w_down) + layer_biases[5 * model_width:6 * model_width])

def reference(section_input, out_cotangent, series_counts, norm_gains, biases, qkv_weight, out_weight, up_weight, down_weight):
    row_ids = jnp.arange(ROWS, dtype=jnp.int32)
    slot_index = row_ids % (SLOTS * SEG) // SEG
    group_index = row_ids // (SLOTS * SEG)
    live = (slot_index[None, :] < series_counts[:, group_index]).astype(jnp.float32)[:, :, None]

    def forward(first_input, probes, gains_all, biases_all, qkv_all, out_all, up_all, down_all):
        current = first_input + probes[0]
        produced = []
        for section_id in range(N_SECTION):
            residual = current.reshape(-1, D)
            for sublayer in range(LAYERS_DEV):
                layer_id = LAYERS_DEV * section_id + sublayer
                residual = layer_apply(residual, gains_all[layer_id], biases_all[layer_id], qkv_all[layer_id], out_all[layer_id], up_all[layer_id], down_all[layer_id])
            emitted = low(low_back(live * residual.reshape(MICRO, ROWS, D)))
            produced.append(emitted)
            if section_id + 1 < N_SECTION:
                current = emitted + probes[section_id + 1]
        return jnp.stack(produced)
    primals = (section_input.astype(jnp.float32), jnp.zeros((N_SECTION, MICRO, ROWS, D), jnp.float32), norm_gains, biases, qkv_weight.astype(jnp.float32), out_weight.astype(jnp.float32), up_weight.astype(jnp.float32), down_weight.astype(jnp.float32))
    outputs, pullback = jax.vjp(forward, *primals)
    cotangent = jnp.zeros_like(outputs).at[N_SECTION - 1].set(out_cotangent.astype(jnp.float32))
    grads = pullback(cotangent)
    return (outputs.astype(jnp.bfloat16), grads[1].astype(jnp.bfloat16), grads[2], grads[3], grads[4], grads[5], grads[6], grads[7])
```

```python
import functools

import jax
import jax.numpy as jnp
from jax import lax
from jax.experimental import pallas as pl
from jax.experimental.pallas import tpu as pltpu
from jax.sharding import PartitionSpec as P

HEADS = 8
HEAD_DIM = 128
SEG = 15
LAYERS_DEV = 2
EPSILON = 1e-05
NEGATIVE = -1e30
SCALE = HEAD_DIM ** (-0.5)
GELU_A = 0.7978845608028654
GELU_B = 0.044715
TILE = 1024
F32 = jnp.float32
BF16 = jnp.bfloat16


def dot_nn(left, right):
    return jnp.dot(left, right, preferred_element_type=F32)


def dot_nt(left, right):
    return lax.dot_general(left, right, (((1,), (1,)), ((), ())), preferred_element_type=F32)


def dot_tn(left, right):
    return lax.dot_general(left, right, (((0,), (0,)), ((), ())), preferred_element_type=F32)


def query_blocks(rows):
    blocks = []
    for base in range(0, rows, 240):
        blocks += [(base, 128, base), (base + 128, 112, base + 112)]
    return blocks


def mask_table():
    tables = []
    for query_start, key_start in ((0, 0), (128, 112)):
        query = query_start + lax.broadcasted_iota(jnp.int32, (128, 128), 0)
        key = key_start + lax.broadcasted_iota(jnp.int32, (128, 128), 1)
        seen = (query // SEG == key // SEG) & (key <= query)
        tables.append(jnp.where(seen, 0.0, NEGATIVE).astype(F32))
    return jnp.stack(tables)


def fold_rows(values):
    rows, width = values.shape
    return jnp.sum(values.reshape(rows // 8, 8, width), axis=0)


def live_column(meta, tick, rows, per_micro):
    micros = rows // per_micro
    row = lax.broadcasted_iota(jnp.int32, (rows, 1), 0)
    live = None
    for micro in range(micros):
        count = meta[tick, 3 + meta[tick, 1] * micros + micro]
        inside = (row >= micro * per_micro) & (row < micro * per_micro + count * SEG)
        live = inside if live is None else live | inside
    return live.astype(F32)


def softmax_rows(query, key, mask):
    scores = dot_nt(query, key) + mask
    top = jnp.max(scores, axis=-1, keepdims=True)
    raised = jnp.exp((scores - top) * SCALE)
    return raised / jnp.sum(raised, axis=-1, keepdims=True)


def forward_kernel(
    tick, aliased, rows, block, per_micro, unroll,
    meta, first_in, recv, mask, gains, biases, wqkv, wout, wup, wdown,
    *refs,
):
    (y_ref, n1_o, e1_o, qkv_o, o_o, n2_o, e2_o, u_o, h_o, r1_o, r2_o, made_o) = refs[aliased:aliased + 12]
    (wq, wo, wu, wd, xb, xs, qb, n1_s, e1_s, qkv_s, o_s, n2_s, e2_s, u_s, h_s, r1_s, r2_s,
     wsem, ssem, xsem) = refs[aliased + 12:]
    width = xs.shape[1]
    hidden = wu.shape[2]
    layers = wq.shape[0]

    def weight_pieces(layer):
        pieces = []
        for tile in range(3 * width // TILE):
            cut = pl.ds(tile * TILE, TILE)
            pieces.append((wqkv.at[layer, :, cut], wq.at[layer, :, cut]))
        pieces.append((wout.at[layer], wo.at[layer]))
        for tile in range(hidden // TILE):
            cut = pl.ds(tile * TILE, TILE)
            pieces.append((wup.at[layer, :, cut], wu.at[layer, :, cut]))
        for tile in range(hidden // TILE):
            cut = pl.ds(tile * TILE, TILE)
            pieces.append((wdown.at[layer, cut, :], wd.at[layer, cut, :]))
        return pieces

    n_qkv = 3 * width // TILE
    n_hid = hidden // TILE
    at_out = n_qkv
    at_up = n_qkv + 1
    at_down = at_up + n_hid

    @pl.when(meta[tick, 0] == 1)
    def _():
        row0 = pl.multiple_of(meta[tick, 1] * rows, 16)

        @pl.when(meta[tick, 2] == 1)
        def _():
            copy = pltpu.make_async_copy(first_in.at[pl.ds(row0, rows)], xb, xsem)
            copy.start()
            copy.wait()

        @pl.when(meta[tick, 2] != 1)
        def _():
            copy = pltpu.make_async_copy(recv, xb, xsem)
            copy.start()
            copy.wait()

        for layer in range(layers):
            for spot, (source, target) in enumerate(weight_pieces(layer)):
                pltpu.make_async_copy(source, target, wsem.at[layer, spot]).start()

        def wait_weight(layer, spot, source, target):
            pltpu.make_async_copy(source, target, wsem.at[layer, spot]).wait()

        saves = ((n1_s, n1_o), (e1_s, e1_o), (qkv_s, qkv_o), (o_s, o_o), (n2_s, n2_o), (e2_s, e2_o),
                 (u_s, u_o), (h_s, h_o), (r1_s, r1_o), (r2_s, r2_o))

        def save(layer, spot):
            source, target = saves[spot]
            return pltpu.make_async_copy(
                source.at[layer], target.at[layer, pl.ds(row0, rows)], ssem.at[layer, spot])

        @pl.loop(0, rows // block)
        def _(step):
            cut = pl.ds(pl.multiple_of(step * block, 16), block)
            xs[cut, :] = xb[cut, :].astype(F32)

        def norm(layer, gain, shift, n_s, e_s, r_s):
            @pl.loop(0, rows // block)
            def _(step):
                cut = pl.ds(pl.multiple_of(step * block, 16), block)
                values = xs[cut, :]
                centred = values - jnp.mean(values, axis=-1, keepdims=True)
                inverse = lax.rsqrt(jnp.mean(centred * centred, axis=-1, keepdims=True) + EPSILON)
                normed = centred * inverse
                n_s[layer, cut, :] = normed.astype(BF16)
                e_s[layer, cut, :] = (normed * gain + shift).astype(BF16)
                r_s[layer, cut, :] = jnp.broadcast_to(inverse, (block, 128))

        @pl.loop(0, layers)
        def _(layer):
            norm(layer, gains[pl.ds(layer, 1), :width], biases[pl.ds(layer, 1), :width], n1_s, e1_s, r1_s)
            save(layer, 0).start()
            save(layer, 1).start()
            save(layer, 8).start()
            qb[:, :width] = biases[pl.ds(layer, 1), width:2 * width]
            qb[:, width:2 * width] = jnp.zeros((1, width), F32)
            qb[:, 2 * width:] = biases[pl.ds(layer, 1), 2 * width:3 * width]

            @pl.loop(0, n_qkv)
            def _(tile):
                cut = pl.ds(pl.multiple_of(tile * TILE, TILE), TILE)
                wait_weight(layer, tile, wqkv.at[layer, :, cut], wq.at[layer, :, cut])
                qkv_s[layer, :, cut] = (dot_nn(e1_s[layer], wq[layer, :, cut]) + qb[:, cut]).astype(BF16)

            save(layer, 2).start()

            @pl.loop(0, HEADS // unroll)
            def _(group):
                for inner in range(unroll):
                    col = pl.multiple_of((group * unroll + inner) * HEAD_DIM, HEAD_DIM)
                    for spot, (q0, nq, k0) in enumerate(query_blocks(rows)):
                        query = qkv_s[layer, q0:q0 + nq, pl.ds(col, HEAD_DIM)]
                        key = qkv_s[layer, k0:k0 + 128, pl.ds(width + col, HEAD_DIM)]
                        value = qkv_s[layer, k0:k0 + 128, pl.ds(2 * width + col, HEAD_DIM)]
                        soft = softmax_rows(query, key, mask[spot % 2, :nq, :])
                        o_s[layer, q0:q0 + nq, pl.ds(col, HEAD_DIM)] = dot_nn(soft.astype(BF16), value).astype(BF16)

            save(layer, 3).start()
            wait_weight(layer, at_out, wout.at[layer], wo.at[layer])
            xs[...] += dot_nn(o_s[layer], wo[layer]) + biases[pl.ds(layer, 1), 3 * width:4 * width]
            norm(layer, gains[pl.ds(layer, 1), width:], biases[pl.ds(layer, 1), 4 * width:5 * width], n2_s, e2_s, r2_s)
            save(layer, 4).start()
            save(layer, 5).start()
            save(layer, 9).start()

            @pl.loop(0, n_hid)
            def _(tile):
                cut = pl.ds(pl.multiple_of(tile * TILE, TILE), TILE)
                bias_cut = pl.ds(pl.multiple_of(6 * width + tile * TILE, TILE), TILE)
                wait_weight(layer, at_up + tile, wup.at[layer, :, cut], wu.at[layer, :, cut])
                pre = dot_nn(e2_s[layer], wu[layer, :, cut]) + biases[pl.ds(layer, 1), bias_cut]
                u_s[layer, :, cut] = pre.astype(BF16)
                turned = jnp.tanh(GELU_A * (pre + GELU_B * pre * pre * pre))
                h_s[layer, :, cut] = (0.5 * pre * (1.0 + turned)).astype(BF16)

            save(layer, 6).start()
            save(layer, 7).start()
            for tile in range(n_hid):
                cut = pl.ds(tile * TILE, TILE)
                wait_weight(layer, at_down + tile, wdown.at[layer, cut, :], wd.at[layer, cut, :])
            xs[...] += dot_nn(h_s[layer], wd[layer]) + biases[pl.ds(layer, 1), 5 * width:6 * width]

        y_ref[...] = (xs[...] * live_column(meta, tick, rows, per_micro)).astype(BF16)
        made = pltpu.make_async_copy(y_ref, made_o.at[pl.ds(row0, rows)], xsem)
        made.start()
        for layer in range(layers):
            for spot in range(len(saves)):
                save(layer, spot).wait()
        made.wait()


def backward_kernel(
    tick, aliased, rows, block, per_micro, unroll,
    meta, last_in, recv, mask, gains, wqkv, wout, wup, wdown,
    n1_i, qkv_i, n2_i, u_i, r1_i, r2_i,
    *refs,
):
    (gx_ref, dqkv_o, da_o, du_o, df_o, sums_o, made_o) = refs[aliased:aliased + 7]
    (wq, wo, wu, wd, gb, gs, de_s, do_s, n1_s, qkv_s, n2_s, u_s, r1_s, r2_s,
     dqkv_s, da_s, du_s, df_s, sums_s, wsem, lsem, ssem, xsem) = refs[aliased + 7:]
    width = gs.shape[1]
    hidden = wu.shape[2]
    layers = wq.shape[0]
    n_hid = hidden // TILE
    HALF = 512

    @pl.when(meta[tick, 0] == 1)
    def _():
        row0 = pl.multiple_of(meta[tick, 1] * rows, 16)

        @pl.when(meta[tick, 2] == 1)
        def _():
            copy = pltpu.make_async_copy(last_in.at[pl.ds(row0, rows)], gb, xsem)
            copy.start()
            copy.wait()

        @pl.when(meta[tick, 2] != 1)
        def _():
            copy = pltpu.make_async_copy(recv, gb, xsem)
            copy.start()
            copy.wait()

        def weight(layer, spot):
            if spot < n_hid:
                cut = pl.ds(spot * TILE, TILE)
                pair = (wdown.at[layer, cut, :], wd.at[layer, cut, :])
            else:
                pair = ((wup.at[layer], wu.at[layer]), (wout.at[layer], wo.at[layer]),
                        (wqkv.at[layer], wq.at[layer]))[spot - n_hid]
            return pltpu.make_async_copy(pair[0], pair[1], wsem.at[layer, spot])

        loads = ((u_i, u_s), (n2_i, n2_s), (r2_i, r2_s), (qkv_i, qkv_s), (n1_i, n1_s), (r1_i, r1_s))

        def load(layer, spot):
            source, target = loads[spot]
            return pltpu.make_async_copy(
                source.at[layer, pl.ds(row0, rows)], target.at[layer], lsem.at[layer, spot])

        saves = ((df_s, df_o), (du_s, du_o), (da_s, da_o), (dqkv_s, dqkv_o))

        def save(layer, spot):
            source, target = saves[spot]
            return pltpu.make_async_copy(
                source.at[layer], target.at[layer, pl.ds(row0, rows)], ssem.at[layer, spot])

        def save_sums(layer):
            return pltpu.make_async_copy(sums_s.at[layer], sums_o.at[meta[tick, 1], layer], ssem.at[layer, 4])

        for layer in reversed(range(layers)):
            for spot in range(n_hid):
                weight(layer, spot).start()
                if spot == 0:
                    load(layer, 0).start()
            weight(layer, n_hid).start()
            load(layer, 1).start()
            load(layer, 2).start()
            weight(layer, n_hid + 1).start()
            load(layer, 3).start()
            weight(layer, n_hid + 2).start()
            load(layer, 4).start()
            load(layer, 5).start()

        sums_s[...] = jnp.zeros(sums_s.shape, F32)
        live = live_column(meta, tick, rows, per_micro)
        gs[...] = gb[...].astype(F32) * live

        def add_sum(layer, start, size, values):
            sums_s[layer, :, pl.ds(start, size)] += fold_rows(values)

        def norm_back(layer, gain, n_s, r_s, shift_at, gain_at, narrow):
            @pl.loop(0, rows // block)
            def _(step):
                cut = pl.ds(pl.multiple_of(step * block, 16), block)
                grad = de_s[cut, :]
                normed = n_s[layer, cut, :].astype(F32)
                scaled = grad * gain
                along = grad * normed
                first = jnp.mean(scaled, axis=-1, keepdims=True)
                second = jnp.mean(along * gain, axis=-1, keepdims=True)
                inverse = r_s[layer, cut, :1]
                fresh = gs[cut, :] + inverse * (scaled - first - normed * second)
                gs[cut, :] = fresh
                add_sum(layer, shift_at, width, grad)
                add_sum(layer, gain_at, width, along)
                if narrow is not None:
                    rounded = fresh.astype(BF16)
                    narrow[layer, cut, :] = rounded
                    add_sum(layer, 3 * width, width, rounded.astype(F32))

        @pl.loop(0, layers)
        def _(turn):
            layer = layers - 1 - turn

            @pl.loop(0, rows // block)
            def _(step):
                cut = pl.ds(pl.multiple_of(step * block, 16), block)
                rounded = gs[cut, :].astype(BF16)
                df_s[layer, cut, :] = rounded
                add_sum(layer, 5 * width, width, rounded.astype(F32))

            save(layer, 0).start()
            load(layer, 0).wait()
            for spot in range(n_hid):
                weight(layer, spot).wait()

            @pl.loop(0, hidden // HALF)
            def _(tile):
                cut = pl.ds(pl.multiple_of(tile * HALF, HALF), HALF)
                back = dot_nt(df_s[layer], wd[layer, cut, :]).astype(BF16).astype(F32)
                pre = u_s[layer, :, cut].astype(F32)
                square = pre * pre
                turned = jnp.tanh(GELU_A * pre * (1.0 + GELU_B * square))
                slope = 0.5 * (1.0 + turned) + (0.5 * GELU_A) * pre * (1.0 - turned * turned) * (
                    1.0 + (3.0 * GELU_B) * square)
                rounded = (back * slope).astype(BF16)
                du_s[layer, :, cut] = rounded
                add_sum(layer, pl.multiple_of(6 * width + tile * HALF, HALF), HALF, rounded.astype(F32))

            save(layer, 1).start()
            weight(layer, n_hid).wait()

            @pl.loop(0, width // HALF)
            def _(tile):
                cut = pl.ds(pl.multiple_of(tile * HALF, HALF), HALF)
                de_s[:, cut] = dot_nt(du_s[layer], wu[layer, cut, :])

            load(layer, 1).wait()
            load(layer, 2).wait()
            norm_back(layer, gains[pl.ds(layer, 1), width:], n2_s, r2_s, 4 * width, 9 * width, da_s)
            save(layer, 2).start()
            weight(layer, n_hid + 1).wait()
            do_s[...] = dot_nt(da_s[layer], wo[layer]).astype(BF16)
            load(layer, 3).wait()

            @pl.loop(0, HEADS // unroll)
            def _(group):
                for inner in range(unroll):
                    col = pl.multiple_of((group * unroll + inner) * HEAD_DIM, HEAD_DIM)
                    q_cut = pl.ds(col, HEAD_DIM)
                    k_cut = pl.ds(width + col, HEAD_DIM)
                    v_cut = pl.ds(2 * width + col, HEAD_DIM)
                    q_sum = jnp.zeros((8, HEAD_DIM), F32)
                    v_sum = jnp.zeros((8, HEAD_DIM), F32)
                    tail_k = tail_v = None
                    for spot, (q0, nq, k0) in enumerate(query_blocks(rows)):
                        query = qkv_s[layer, q0:q0 + nq, q_cut]
                        key = qkv_s[layer, k0:k0 + 128, k_cut]
                        value = qkv_s[layer, k0:k0 + 128, v_cut]
                        grad = do_s[q0:q0 + nq, q_cut]
                        soft = softmax_rows(query, key, mask[spot % 2, :nq, :])
                        soft_grad = dot_nt(grad, value)
                        inner_sum = jnp.sum(soft_grad * soft, axis=-1, keepdims=True)
                        score_grad = (soft * (soft_grad - inner_sum)).astype(BF16)
                        dq = (dot_nn(score_grad, key) * SCALE).astype(BF16)
                        dqkv_s[layer, q0:q0 + nq, q_cut] = dq
                        q_sum += fold_rows(dq.astype(F32))
                        dk = dot_tn(score_grad, query) * SCALE
                        dv = dot_tn(soft.astype(BF16), grad)
                        if spot % 2 == 0:
                            tail_k, tail_v = dk[112:], dv[112:]
                            low, high = 0, 112
                            head_k, head_v = dk[:112], dv[:112]
                        else:
                            low, high = 0, 128
                            head_k = jnp.concatenate([dk[:16] + tail_k, dk[16:]], axis=0)
                            head_v = jnp.concatenate([dv[:16] + tail_v, dv[16:]], axis=0)
                        dqkv_s[layer, k0 + low:k0 + high, k_cut] = head_k.astype(BF16)
                        head_v = head_v.astype(BF16)
                        dqkv_s[layer, k0 + low:k0 + high, v_cut] = head_v
                        v_sum += fold_rows(head_v.astype(F32))
                    sums_s[layer, :, pl.ds(width + col, HEAD_DIM)] = q_sum
                    sums_s[layer, :, pl.ds(2 * width + col, HEAD_DIM)] = v_sum

            save(layer, 3).start()
            weight(layer, n_hid + 2).wait()

            @pl.loop(0, width // HALF)
            def _(tile):
                cut = pl.ds(pl.multiple_of(tile * HALF, HALF), HALF)
                de_s[:, cut] = dot_nt(dqkv_s[layer], wq[layer, cut, :])

            load(layer, 4).wait()
            load(layer, 5).wait()
            norm_back(layer, gains[pl.ds(layer, 1), :width], n1_s, r1_s, 0, 8 * width, None)
            save_sums(layer).start()

        gx_ref[...] = gs[...].astype(BF16)
        made = pltpu.make_async_copy(gx_ref, made_o.at[pl.ds(row0, rows)], xsem)
        made.start()
        for layer in range(layers):
            for spot in range(len(saves)):
                save(layer, spot).wait()
            save_sums(layer).wait()
        made.wait()


ANY = pl.BlockSpec(memory_space=pl.ANY)
VMEM = pl.BlockSpec(memory_space=pltpu.VMEM)
SMEM = pl.BlockSpec(memory_space=pltpu.SMEM)
LIMIT = 58 << 20


def forward_shapes(layers, total, width, hidden):
    sizes = (width, width, 3 * width, width, width, width, hidden, hidden)
    shapes = [((layers, total, size), BF16) for size in sizes]
    shapes += [((layers, total, 128), F32)] * 2
    shapes.append(((total, width), BF16))
    return shapes


def backward_shapes(layers, total, width, hidden, chunks):
    shapes = [((layers, total, size), BF16) for size in (3 * width, width, hidden, width)]
    shapes.append(((chunks, layers, 8, 8 * width + hidden), F32))
    shapes.append(((total, width), BF16))
    return shapes


def run_forward(tick, meta, first_in, recv, mask, gains, biases, weights, kept, rows, per_micro, block=48, unroll=2):
    wqkv, wout, wup, wdown = weights
    layers, width = wqkv.shape[0], wqkv.shape[1]
    hidden = wup.shape[2]
    sizes = (width, width, 3 * width, width, width, width, hidden, hidden)
    pieces = 3 * width // TILE + 1 + 2 * (hidden // TILE)
    scratch = [pltpu.VMEM(w.shape, BF16) for w in weights]
    scratch += [pltpu.VMEM((rows, width), BF16), pltpu.VMEM((rows, width), F32), pltpu.VMEM((1, 3 * width), F32)]
    scratch += [pltpu.VMEM((layers, rows, size), BF16) for size in sizes]
    scratch += [pltpu.VMEM((layers, rows, 128), F32)] * 2
    scratch += [pltpu.SemaphoreType.DMA((layers, pieces)), pltpu.SemaphoreType.DMA((layers, 10)), pltpu.SemaphoreType.DMA]
    flops = 2 * rows * (wqkv.size + wout.size + wup.size + wdown.size)
    moved = 2 * (wqkv.size + wout.size + wup.size + wdown.size) + 2 * layers * rows * sum(sizes)
    total = first_in.shape[0]
    shapes = [jax.ShapeDtypeStruct(*k) for k in forward_shapes(layers, total, width, hidden)]
    out = pl.pallas_call(
        functools.partial(forward_kernel, tick, len(kept), rows, block, per_micro, unroll),
        out_shape=[jax.ShapeDtypeStruct((rows, width), BF16)] + shapes,
        in_specs=[SMEM, ANY, ANY, VMEM, VMEM, VMEM] + [ANY] * 4 + [ANY] * len(kept),
        out_specs=[VMEM] + [ANY] * 11,
        scratch_shapes=scratch,
        input_output_aliases={10 + i: 1 + i for i in range(len(kept))},
        compiler_params=pltpu.CompilerParams(vmem_limit_bytes=LIMIT),
        cost_estimate=pl.CostEstimate(flops=flops, bytes_accessed=moved, transcendentals=0),
        name="section_forward",
    )(meta, first_in, recv, mask, gains, biases, *weights, *kept)
    return out[0], list(out[1:])


def run_backward(tick, meta, last_in, recv, mask, gains, weights, kept, made, rows, per_micro, block=48, unroll=1):
    wqkv, wout, wup, wdown = weights
    layers, width = wqkv.shape[0], wqkv.shape[1]
    hidden = wup.shape[2]
    n1, _, qkv, _, n2, _, u, _, r1, r2, _ = kept
    scratch = [pltpu.VMEM(w.shape, BF16) for w in weights]
    scratch += [pltpu.VMEM((rows, width), BF16), pltpu.VMEM((rows, width), F32), pltpu.VMEM((rows, width), F32),
                pltpu.VMEM((rows, width), BF16)]
    scratch += [pltpu.VMEM((layers, rows, size), BF16) for size in (width, 3 * width, width, hidden)]
    scratch += [pltpu.VMEM((layers, rows, 128), F32)] * 2
    scratch += [pltpu.VMEM((layers, rows, size), BF16) for size in (3 * width, width, hidden, width)]
    scratch += [pltpu.VMEM((layers, 8, 8 * width + hidden), F32)]
    scratch += [pltpu.SemaphoreType.DMA((layers, hidden // TILE + 3)), pltpu.SemaphoreType.DMA((layers, 6)),
                pltpu.SemaphoreType.DMA((layers, 5)), pltpu.SemaphoreType.DMA]
    total = wqkv.size + wout.size + wup.size + wdown.size
    flops = 2 * rows * total
    moved = 2 * total + 2 * layers * rows * (14 * width)
    shapes = [jax.ShapeDtypeStruct(*k) for k in backward_shapes(
        layers, last_in.shape[0], width, hidden, last_in.shape[0] // rows)]
    out = pl.pallas_call(
        functools.partial(backward_kernel, tick, len(made), rows, block, per_micro, unroll),
        out_shape=[jax.ShapeDtypeStruct((rows, width), BF16)] + shapes,
        in_specs=[SMEM, ANY, ANY, VMEM, VMEM] + [ANY] * 4 + [ANY] * 6 + [ANY] * len(made),
        out_specs=[VMEM] + [ANY] * 6,
        scratch_shapes=scratch,
        input_output_aliases={15 + i: 1 + i for i in range(len(made))},
        compiler_params=pltpu.CompilerParams(vmem_limit_bytes=LIMIT),
        cost_estimate=pl.CostEstimate(flops=flops, bytes_accessed=moved, transcendentals=0),
        name="section_backward",
    )(meta, last_in, recv, mask, gains, *weights, n1, qkv, n2, u, r1, r2, *made)
    return out[0], list(out[1:])


def hop(value, steps):
    count = lax.axis_size("section")
    pairs = [(s, s + steps) for s in range(count) if 0 <= s + steps < count]
    return lax.ppermute(value, "section", pairs) if pairs else jnp.zeros_like(value)


def halves(values, order):
    count = lax.axis_size("dp")
    here = lax.axis_index("dp")
    left = [bit for bit in reversed(range(count.bit_length() - 1))]
    values = values.reshape((2,) * len(left) + values.shape[1:])
    for bit in order:
        spot = left.index(bit)
        left.remove(bit)
        mine = (here >> bit) & 1
        send = lax.dynamic_index_in_dim(values, 1 - mine, spot, keepdims=False)
        keep = lax.dynamic_index_in_dim(values, mine, spot, keepdims=False)
        recv = lax.ppermute(send, "dp", [(device, device ^ (1 << bit)) for device in range(count)])
        values = keep.astype(F32) + recv.astype(F32)
        if left:
            values = values.astype(BF16)
    return values


def scatter_sum(full):
    count = lax.axis_size("dp")
    bits = count.bit_length() - 1
    return halves(full.reshape(count, full.shape[0] // count, full.shape[1]), range(bits))


def weight_grad(left, right):
    return jnp.einsum("rd,re->de", left, right, preferred_element_type=F32).astype(BF16)


MICROS = 2


def shards(
    section_input, out_cotangent, series_counts, norm_gains, biases,
    qkv_weight, out_weight, up_weight, down_weight,
):
    sections = lax.axis_size("section")
    section = lax.axis_index("section")
    micro_count, per_micro, width = section_input.shape
    layers = qkv_weight.shape[0]
    total = micro_count * per_micro
    rows = MICROS * per_micro
    chunks = micro_count // MICROS
    ticks = chunks + 2 * (sections - 1)
    weights = (qkv_weight, out_weight, up_weight, down_weight)
    mask = mask_table()
    counts = jnp.broadcast_to(series_counts.reshape(1, micro_count), (ticks, micro_count))
    tick_ids = jnp.arange(ticks, dtype=jnp.int32)

    def table(place):
        chunk = tick_ids - 2 * place
        active = (chunk >= 0) & (chunk < chunks)
        edge = jnp.broadcast_to(place == 0, (ticks,))
        columns = [active, jnp.clip(chunk, 0, chunks - 1), edge]
        columns = [column.astype(jnp.int32)[:, None] for column in columns]
        return jnp.concatenate(columns + [counts], axis=1)

    entering = section_input.reshape(total, width)
    leaving = out_cotangent.reshape(total, width)
    meta = table(section)
    arrived = [entering[:rows]] * 2
    kept = []
    for tick in range(ticks):
        sent, kept = run_forward(
            tick, meta, entering, arrived[tick], mask, norm_gains, biases, weights, kept, rows, per_micro)
        if tick + 2 < ticks:
            arrived.append(hop(sent, 1))
    meta = table(sections - 1 - section)
    arrived = [leaving[:rows]] * 2
    made = []
    for tick in range(ticks):
        sent, made = run_backward(
            tick, meta, leaving, arrived[tick], mask, norm_gains, weights, kept, made, rows, per_micro)
        if tick + 2 < ticks:
            arrived.append(hop(sent, -1))
    _, e1, _, attended, _, e2, _, hidden, _, _, outputs = kept
    dqkv, da, du, df, sums, input_grads = made
    pairs = ((e1, dqkv), (attended, da), (e2, du), (hidden, df))
    grads = [[None] * layers for _ in pairs]
    for layer in reversed(range(layers)):
        for which in (3, 2, 1, 0):
            left, right = pairs[which]
            grads[which][layer] = scatter_sum(weight_grad(left[layer], right[layer]))
    count = lax.axis_size("dp")
    small = jnp.sum(sums, axis=(0, 2)).astype(BF16)
    cut = biases.shape[1]
    small = jnp.concatenate([small[:, :cut].reshape(layers, count, -1), small[:, cut:].reshape(layers, count, -1)], axis=2)
    small = halves(jnp.swapaxes(small, 0, 1), range(count.bit_length() - 1))
    small_bias, small_gain = small[:, :cut // count], small[:, cut // count:]
    return (
        outputs.reshape(1, micro_count, per_micro, width),
        input_grads.reshape(1, micro_count, per_micro, width),
        small_gain,
        small_bias,
        *(jnp.stack(grad) for grad in grads),
    )


def solution(mesh):
    stacked = P("section", None, None)
    return jax.shard_map(
        shards,
        mesh=mesh,
        in_specs=(P(None, "dp", None), P(None, "dp", None), P(None, "dp"),
                  P("section", None), P("section", None), stacked, stacked, stacked, stacked),
        out_specs=(P("section", None, "dp", None), P("section", None, "dp", None),
                   P("section", "dp"), P("section", "dp"),
                   P("section", "dp", None), P("section", "dp", None),
                   P("section", "dp", None), P("section", "dp", None)),
        check_vma=False,
    )
```

```python
import functools

import jax
import jax.numpy as jnp
from jax import lax
from jax.experimental import pallas as pl
from jax.experimental.pallas import tpu as pltpu
from jax.sharding import PartitionSpec as P

HEADS = 8
HEAD_DIM = 128
SEG = 15
LAYERS_DEV = 2
EPSILON = 1e-05
MICROS = 2
NEGATIVE = -1e30
SCALE = HEAD_DIM ** (-0.5)
GELU_A = 0.7978845608028654
GELU_B = 0.044715
TILE = 1024
STEP = 512
F32 = jnp.float32
BF16 = jnp.bfloat16


def dot_nn(left, right):
    return jnp.dot(left, right, preferred_element_type=F32)


def dot_nt(left, right):
    return lax.dot_general(left, right, (((1,), (1,)), ((), ())), preferred_element_type=F32)


def dot_tn(left, right):
    return lax.dot_general(left, right, (((0,), (0,)), ((), ())), preferred_element_type=F32)


def query_blocks(rows):
    blocks = []
    for base in range(0, rows, 240):
        blocks += [(base, 128, base), (base + 128, 112, base + 112)]
    return blocks


def mask_table():
    tables = []
    for query_start, key_start in ((0, 0), (128, 112)):
        query = query_start + lax.broadcasted_iota(jnp.int32, (128, 128), 0)
        key = key_start + lax.broadcasted_iota(jnp.int32, (128, 128), 1)
        seen = (query // SEG == key // SEG) & (key <= query)
        tables.append(jnp.where(seen, 0.0, NEGATIVE).astype(F32))
    return jnp.stack(tables)


def fold_rows(values):
    rows, width = values.shape
    return jnp.sum(values.reshape(rows // 8, 8, width), axis=0)


def live_column(meta, tick, rows, per_micro):
    micros = rows // per_micro
    row = lax.broadcasted_iota(jnp.int32, (rows, 1), 0)
    live = None
    for micro in range(micros):
        count = meta[tick, 3 + meta[tick, 1] * micros + micro]
        inside = (row >= micro * per_micro) & (row < micro * per_micro + count * SEG)
        live = inside if live is None else live | inside
    return live.astype(F32)


def exponent(scores, mask):
    scores = scores + mask
    return jnp.exp((scores - jnp.max(scores, axis=-1, keepdims=True)) * SCALE)


def forward_kernel(
    tick, aliased, rows, block, per_micro, unroll,
    meta, first_in, recv, mask, gains, biases, wqkv, wout, wup, wdown,
    *refs,
):
    (y_ref, n1_o, e1_o, qkv_o, o_o, n2_o, e2_o, u_o, h_o, r1_o, r2_o, made_o) = refs[aliased:aliased + 12]
    fresh = tick == 0
    wq, wo, wu, wd = refs[aliased + 12:aliased + 16]
    (xb, xs, qb, n1_s, e1_s, qkv_s, o_s, n2_s, e2_s, u_s, h_s, r1_s, r2_s,
     wsem, ssem, xsem) = refs[aliased + 16:]
    width = xs.shape[1]
    hidden = wu.shape[2]
    layers = wq.shape[0]

    def weight_pieces(layer):
        pieces = []
        for tile in range(3 * width // TILE):
            cut = pl.ds(tile * TILE, TILE)
            pieces.append((wqkv.at[layer, :, cut], wq.at[layer, :, cut]))
        pieces.append((wout.at[layer], wo.at[layer]))
        for tile in range(hidden // TILE):
            cut = pl.ds(tile * TILE, TILE)
            pieces.append((wup.at[layer, :, cut], wu.at[layer, :, cut]))
        for tile in range(hidden // TILE):
            cut = pl.ds(tile * TILE, TILE)
            pieces.append((wdown.at[layer, cut, :], wd.at[layer, cut, :]))
        return pieces

    def each_weight(act):
        for layer in range(layers):
            for spot, (source, target) in enumerate(weight_pieces(layer)):
                act(pltpu.make_async_copy(source, target, wsem.at[layer, spot]))

    def wait_weight(layer, spot, source, target):
        if fresh:
            pltpu.make_async_copy(source, target, wsem.at[layer, spot]).wait()

    if fresh:
        @pl.when(meta[tick, 0] == 1)
        def _():
            copy = pltpu.make_async_copy(first_in.at[pl.ds(0, rows)], xb, xsem)
            copy.start()
            copy.wait()
            each_weight(lambda copy: copy.start())


        @pl.when(meta[tick, 0] != 1)
        def _():
            each_weight(lambda copy: copy.start())
            each_weight(lambda copy: copy.wait())

    n_qkv = 3 * width // TILE
    n_hid = hidden // TILE
    at_out = n_qkv
    at_up = n_qkv + 1
    at_down = at_up + n_hid

    @pl.when(meta[tick, 0] == 1)
    def _():
        row0 = pl.multiple_of(meta[tick, 1] * rows, 16)

        if not fresh:
            @pl.when(meta[tick, 2] == 1)
            def _():
                copy = pltpu.make_async_copy(first_in.at[pl.ds(row0, rows)], xb, xsem)
                copy.start()
                copy.wait()

            @pl.when(meta[tick, 2] != 1)
            def _():
                copy = pltpu.make_async_copy(recv.at[pl.ds(0, rows)], xb, xsem)
                copy.start()
                copy.wait()

        saves = ((n1_s, n1_o), (e1_s, e1_o), (qkv_s, qkv_o), (o_s, o_o), (n2_s, n2_o), (e2_s, e2_o),
                 (u_s, u_o), (h_s, h_o), (r1_s, r1_o), (r2_s, r2_o))

        def save(layer, spot):
            source, target = saves[spot]
            return pltpu.make_async_copy(
                source.at[layer], target.at[layer, pl.ds(row0, rows)], ssem.at[layer, spot])

        @pl.loop(0, rows // block)
        def _(step):
            cut = pl.ds(pl.multiple_of(step * block, 16), block)
            xs[cut, :] = xb[cut, :].astype(F32)

        def norm(layer, gain, shift, n_s, e_s, r_s):
            @pl.loop(0, rows // block)
            def _(step):
                cut = pl.ds(pl.multiple_of(step * block, 16), block)
                values = xs[cut, :]
                centred = values - jnp.mean(values, axis=-1, keepdims=True)
                inverse = lax.rsqrt(jnp.mean(centred * centred, axis=-1, keepdims=True) + EPSILON)
                normed = centred * inverse
                n_s[layer, cut, :] = normed.astype(BF16)
                e_s[layer, cut, :] = (normed * gain + shift).astype(BF16)
                r_s[layer, cut, :] = jnp.broadcast_to(inverse, (block, 128))

        @pl.loop(0, layers)
        def _(layer):
            norm(layer, gains[pl.ds(layer, 1), :width], biases[pl.ds(layer, 1), :width], n1_s, e1_s, r1_s)
            save(layer, 0).start()
            save(layer, 1).start()
            save(layer, 8).start()
            qb[:, :width] = biases[pl.ds(layer, 1), width:2 * width]
            qb[:, width:2 * width] = jnp.zeros((1, width), F32)
            qb[:, 2 * width:] = biases[pl.ds(layer, 1), 2 * width:3 * width]

            for tile in range(n_qkv):
                cut = pl.ds(tile * TILE, TILE)
                wait_weight(layer, tile, wqkv.at[layer, :, cut], wq.at[layer, :, cut])
                for start in range(tile * TILE, (tile + 1) * TILE, STEP):
                    part = pl.ds(start, STEP)
                    qkv_s[layer, :, part] = (dot_nn(e1_s[layer], wq[layer, :, part]) + qb[:, part]).astype(BF16)

            save(layer, 2).start()

            jobs = [(head * HEAD_DIM, spot % 2, q0, nq, k0) for head in range(HEADS)
                    for spot, (q0, nq, k0) in enumerate(query_blocks(rows))]
            scores = []
            for col, _, q0, nq, k0 in jobs:
                query = qkv_s[layer, q0:q0 + nq, col:col + HEAD_DIM]
                key = qkv_s[layer, k0:k0 + 128, width + col:width + col + HEAD_DIM]
                scores.append(dot_nt(query, key))
            soft = []
            for (_, kind, _, nq, _), score in zip(jobs, scores):
                raised = exponent(score, mask[kind, :nq, :])
                soft.append((raised * (1.0 / jnp.sum(raised, axis=-1, keepdims=True))).astype(BF16))
            for (col, _, q0, nq, k0), share in zip(jobs, soft):
                value = qkv_s[layer, k0:k0 + 128, 2 * width + col:2 * width + col + HEAD_DIM]
                o_s[layer, q0:q0 + nq, col:col + HEAD_DIM] = dot_nn(share, value).astype(BF16)

            save(layer, 3).start()
            wait_weight(layer, at_out, wout.at[layer], wo.at[layer])
            for start in range(0, width, STEP):
                part = pl.ds(start, STEP)
                xs[:, part] += dot_nn(o_s[layer], wo[layer, :, part]) + biases[pl.ds(layer, 1), pl.ds(3 * width + start, STEP)]
            norm(layer, gains[pl.ds(layer, 1), width:], biases[pl.ds(layer, 1), 4 * width:5 * width], n2_s, e2_s, r2_s)
            save(layer, 4).start()
            save(layer, 5).start()
            save(layer, 9).start()

            for tile in range(n_hid):
                cut = pl.ds(tile * TILE, TILE)
                wait_weight(layer, at_up + tile, wup.at[layer, :, cut], wu.at[layer, :, cut])
                for start in range(tile * TILE, (tile + 1) * TILE, STEP):
                    part = pl.ds(start, STEP)
                    pre = dot_nn(e2_s[layer], wu[layer, :, part]) + biases[pl.ds(layer, 1), pl.ds(6 * width + start, STEP)]
                    u_s[layer, :, part] = pre.astype(BF16)
                    half = 0.5 * pre
                    turned = jnp.tanh(pre * (GELU_A + (GELU_A * GELU_B) * (pre * pre)))
                    h_s[layer, :, part] = (half + half * turned).astype(BF16)

            save(layer, 6).start()
            save(layer, 7).start()
            for tile in range(n_hid):
                cut = pl.ds(tile * TILE, TILE)
                wait_weight(layer, at_down + tile, wdown.at[layer, cut, :], wd.at[layer, cut, :])
            for start in range(0, width, STEP):
                part = pl.ds(start, STEP)
                xs[:, part] += dot_nn(h_s[layer], wd[layer, :, part]) + biases[pl.ds(layer, 1), pl.ds(5 * width + start, STEP)]

        y_ref[...] = (xs[...] * live_column(meta, tick, rows, per_micro)).astype(BF16)
        made = pltpu.make_async_copy(y_ref, made_o.at[pl.ds(row0, rows)], xsem)
        made.start()
        for layer in range(layers):
            for spot in range(len(saves)):
                save(layer, spot).wait()
        made.wait()


def backward_kernel(
    tick, top, count, aliased, rows, block, per_micro, unroll,
    meta, last_in, recv, mask, gains, wqkv, wout, wup, wdown,
    n1_i, qkv_i, n2_i, u_i, r1_i, r2_i,
    *refs,
):
    (gx_ref, dqkv_o, da_o, du_o, df_o, sums_o, made_o) = refs[aliased:aliased + 7]
    loaded = count < wqkv.shape[0]
    wq, wo, wu, wd = refs[-4:] if loaded else refs[aliased + 7:aliased + 11]
    (gb, gs, de_s, do_s, n1_s, qkv_s, n2_s, u_s, r1_s, r2_s,
     dqkv_s, da_s, du_s, df_s, sums_s, lsem, ssem, xsem) = (
         refs[aliased + 7:-5] if loaded else refs[aliased + 11:])
    width = gs.shape[1]
    hidden = wu.shape[2]
    first, last = top + 1 == wqkv.shape[0], top + 1 == count

    def weight(spot):
        pair = ((wdown, wd), (wup, wu), (wout, wo), (wqkv, wq))[spot]
        return pltpu.make_async_copy(pair[0].at[top], pair[1].at[0], refs[-5].at[spot])

    def weight_here(spot):
        if loaded:
            weight(spot).wait()
    HALF = 1024

    @pl.when(meta[tick, 0] == 1)
    def _():
        row0 = pl.multiple_of(meta[tick, 1] * rows, 16)

        if first:
            @pl.when(meta[tick, 2] == 1)
            def _():
                copy = pltpu.make_async_copy(last_in.at[pl.ds(row0, rows)], gb, xsem)
                copy.start()
                copy.wait()

            @pl.when(meta[tick, 2] != 1)
            def _():
                copy = pltpu.make_async_copy(recv.at[pl.ds(0, rows)], gb, xsem)
                copy.start()
                copy.wait()

            gs[...] = gb[...].astype(F32) * live_column(meta, tick, rows, per_micro)
        else:
            copy = pltpu.make_async_copy(recv, gs, xsem)
            copy.start()
            copy.wait()

        loads = ((u_i, u_s), (n2_i, n2_s), (r2_i, r2_s), (qkv_i, qkv_s), (n1_i, n1_s), (r1_i, r1_s))

        def load(layer, spot):
            source, target = loads[spot]
            return pltpu.make_async_copy(
                source.at[layer, pl.ds(row0, rows)], target.at[layer], lsem.at[layer, spot])

        saves = ((df_s, df_o), (du_s, du_o), (da_s, da_o), (dqkv_s, dqkv_o))

        def save(layer, spot):
            source, target = saves[spot]
            return pltpu.make_async_copy(
                source.at[layer], target.at[layer, pl.ds(row0, rows)], ssem.at[layer, spot])

        def save_sums(layer):
            return pltpu.make_async_copy(sums_s.at[layer], sums_o.at[meta[tick, 1], layer], ssem.at[layer, 4])

        for layer in range(top, top - count, -1):
            for spot in range(len(loads)):
                load(layer, spot).start()
                if loaded and spot < 4:
                    weight(spot).start()

        sums_s[...] = jnp.zeros(sums_s.shape, F32)

        def add_sum(layer, start, size, values):
            sums_s[layer, :, pl.ds(start, size)] += fold_rows(values)

        def norm_back(layer, gain, n_s, r_s, shift_at, gain_at, narrow):
            @pl.loop(0, rows // block)
            def _(step):
                cut = pl.ds(pl.multiple_of(step * block, 16), block)
                grad = de_s[cut, :]
                normed = n_s[layer, cut, :].astype(F32)
                scaled = grad * gain
                along = grad * normed
                first = jnp.mean(scaled, axis=-1, keepdims=True)
                second = jnp.mean(along * gain, axis=-1, keepdims=True)
                inverse = r_s[layer, cut, :1]
                fresh = gs[cut, :] + inverse * (scaled - first - normed * second)
                gs[cut, :] = fresh
                add_sum(layer, shift_at, width, grad)
                add_sum(layer, gain_at, width, along)
                if narrow is not None:
                    rounded = fresh.astype(BF16)
                    narrow[layer, cut, :] = rounded
                    add_sum(layer, 3 * width, width, rounded.astype(F32))

        @pl.loop(0, count)
        def _(turn):
            layer = top - turn

            @pl.loop(0, rows // block)
            def _(step):
                cut = pl.ds(pl.multiple_of(step * block, 16), block)
                rounded = gs[cut, :].astype(BF16)
                df_s[layer, cut, :] = rounded
                add_sum(layer, 5 * width, width, rounded.astype(F32))

            save(layer, 0).start()
            load(layer, 0).wait()
            weight_here(0)
            shelf = 0 if loaded else layer

            @pl.loop(0, hidden // HALF)
            def _(tile):
                cut = pl.ds(pl.multiple_of(tile * HALF, HALF), HALF)
                back = dot_nt(df_s[layer], wd[shelf, cut, :]).astype(BF16).astype(F32)
                pre = u_s[layer, :, cut].astype(F32)
                square = pre * pre
                turned = jnp.tanh(GELU_A * pre * (1.0 + GELU_B * square))
                slope = 0.5 * (1.0 + turned) + (0.5 * GELU_A) * pre * (1.0 - turned * turned) * (
                    1.0 + (3.0 * GELU_B) * square)
                rounded = (back * slope).astype(BF16)
                du_s[layer, :, cut] = rounded
                add_sum(layer, pl.multiple_of(6 * width + tile * HALF, HALF), HALF, rounded.astype(F32))

            save(layer, 1).start()
            weight_here(1)

            @pl.loop(0, width // HALF)
            def _(tile):
                cut = pl.ds(pl.multiple_of(tile * HALF, HALF), HALF)
                de_s[:, cut] = dot_nt(du_s[layer], wu[shelf, cut, :])

            load(layer, 1).wait()
            load(layer, 2).wait()
            norm_back(layer, gains[pl.ds(layer, 1), width:], n2_s, r2_s, 4 * width, 9 * width, da_s)
            save(layer, 2).start()
            weight_here(2)
            do_s[...] = dot_nt(da_s[layer], wo[shelf]).astype(BF16)
            load(layer, 3).wait()

            @pl.loop(0, HEADS // unroll)
            def _(group):
                jobs = []
                for inner in range(unroll):
                    col = pl.multiple_of((group * unroll + inner) * HEAD_DIM, HEAD_DIM)
                    cuts = (pl.ds(col, HEAD_DIM), pl.ds(width + col, HEAD_DIM), pl.ds(2 * width + col, HEAD_DIM))
                    jobs += [(cuts, spot % 2, q0, nq, k0) for spot, (q0, nq, k0) in enumerate(query_blocks(rows))]
                first = []
                for cuts, _, q0, nq, k0 in jobs:
                    query = qkv_s[layer, q0:q0 + nq, cuts[0]]
                    key = qkv_s[layer, k0:k0 + 128, cuts[1]]
                    value = qkv_s[layer, k0:k0 + 128, cuts[2]]
                    grad = do_s[q0:q0 + nq, cuts[0]]
                    first.append((dot_nt(query, key), dot_nt(grad, value)))
                second = []
                for (_, kind, _, nq, _), (score, soft_grad) in zip(jobs, first):
                    raised = exponent(score, mask[kind, :nq, :])
                    soft = raised * (1.0 / jnp.sum(raised, axis=-1, keepdims=True))
                    inner_sum = jnp.sum(soft_grad * soft, axis=-1, keepdims=True)
                    second.append((soft.astype(BF16), (soft * (soft_grad - inner_sum)).astype(BF16)))
                tail_k = tail_v = None
                for (cuts, kind, q0, nq, k0), (soft, score_grad) in zip(jobs, second):
                    query = qkv_s[layer, q0:q0 + nq, cuts[0]]
                    key = qkv_s[layer, k0:k0 + 128, cuts[1]]
                    grad = do_s[q0:q0 + nq, cuts[0]]
                    dqkv_s[layer, q0:q0 + nq, cuts[0]] = (dot_nn(score_grad, key) * SCALE).astype(BF16)
                    dk = dot_tn(score_grad, query) * SCALE
                    dv = dot_tn(soft, grad)
                    if kind == 0:
                        tail_k, tail_v = dk[112:], dv[112:]
                        high = 112
                        dk, dv = dk[:112], dv[:112]
                    else:
                        high = 128
                        dk = jnp.concatenate([dk[:16] + tail_k, dk[16:]], axis=0)
                        dv = jnp.concatenate([dv[:16] + tail_v, dv[16:]], axis=0)
                    dqkv_s[layer, k0:k0 + high, cuts[1]] = dk.astype(BF16)
                    dqkv_s[layer, k0:k0 + high, cuts[2]] = dv.astype(BF16)

            sums_s[layer, :, width:2 * width] = fold_rows(dqkv_s[layer, :, :width].astype(F32))
            sums_s[layer, :, 2 * width:3 * width] = fold_rows(dqkv_s[layer, :, 2 * width:].astype(F32))
            save(layer, 3).start()
            weight_here(3)

            @pl.loop(0, width // HALF)
            def _(tile):
                cut = pl.ds(pl.multiple_of(tile * HALF, HALF), HALF)
                de_s[:, cut] = dot_nt(dqkv_s[layer], wq[shelf, cut, :])

            load(layer, 4).wait()
            load(layer, 5).wait()
            norm_back(layer, gains[pl.ds(layer, 1), :width], n1_s, r1_s, 0, 8 * width, None)
            save_sums(layer).start()

        if last:
            gx_ref[...] = gs[...].astype(BF16)
            made = pltpu.make_async_copy(gx_ref, made_o.at[pl.ds(row0, rows)], xsem)
            made.start()
        else:
            gx_ref[...] = gs[...]
        for layer in range(top, top - count, -1):
            for spot in range(len(saves)):
                save(layer, spot).wait()
            save_sums(layer).wait()
        if last:
            made.wait()


def gradient_kernel(
    jobs, grid, tick, extra,
    meta, *refs,
):
    inputs, (send_o, keep_o), scratch = refs[:extra], refs[extra:extra + 2], refs[extra + 2:]
    lefts, rights = scratch[:len(jobs)], scratch[len(jobs):2 * len(jobs)]
    res, patch_s, lsem, osem, psem = scratch[2 * len(jobs):2 * len(jobs) + 5]
    mine = meta[0, meta.shape[1] - 1]
    loads = []
    for spot, (left, right, layer, _) in enumerate(jobs):
        loads.append((pltpu.make_async_copy(inputs[left].at[layer], lefts[spot], lsem.at[spot, 0]),
                      pltpu.make_async_copy(inputs[right].at[layer], rights[spot], lsem.at[spot, 1])))
        for load in loads[-1]:
            load.start()
    sends = []
    at = tile = 0
    for spot, (_, _, _, patch) in enumerate(jobs):
        for load in loads[spot]:
            load.wait()
        if patch is not None:
            @pl.when(meta[tick, 0] == 1)
            def _():
                rows = patch_s.shape[0]
                copy = pltpu.make_async_copy(inputs[patch], patch_s, psem)
                copy.start()
                copy.wait()
                values = patch_s[...].astype(F32)
                if patch_s.dtype == BF16:
                    values = values * live_column(meta, tick, rows, rows // MICROS)
                cut = pl.ds(pl.multiple_of(meta[tick, 1] * rows, 16), rows)
                rights[spot][cut, :] = values.astype(BF16)

        deep, wide = lefts[spot].shape[1], rights[spot].shape[1]
        block = deep // grid
        pairs = TILE // (2 * block)
        for col in range(0, wide, TILE):
            for row in range(0, deep, TILE):
                start = row // (2 * block)
                view = res.at[tile].reshape(pairs, 2, block, TILE)

                @pl.loop(0, TILE // 512)
                def _(part):
                    lane = pl.multiple_of(row + part * 512, 512)
                    fresh = dot_tn(lefts[spot][:, pl.ds(lane, 512)], rights[spot][:, col:col + TILE])
                    res[tile, pl.ds(pl.multiple_of(part * 512, 512), 512), :] = fresh.astype(BF16)

                for which, (output, half) in enumerate(((send_o, 1 - mine), (keep_o, mine))):
                    copy = pltpu.make_async_copy(
                        view.at[:, half], output.at[start:start + pairs, at:at + block, :], osem.at[tile, which])
                    copy.start()
                    sends.append(copy)
                tile += 1
            at += block
    if send_o.shape[1] > at:
        small_s = scratch[-1]
        copy = pltpu.make_async_copy(inputs[extra - 1], small_s, psem)
        copy.start()
        copy.wait()
        for which, (output, half) in enumerate(((send_o, 1 - mine), (keep_o, mine))):
            copy = pltpu.make_async_copy(small_s.at[:, half], output.at[:, at:, :], osem.at[tile, which])
            copy.start()
            sends.append(copy)
    for copy in sends:
        copy.wait()


HBM = pl.BlockSpec(memory_space=pltpu.HBM)
FREE = pl.BlockSpec(memory_space=pl.ANY)
VMEM = pl.BlockSpec(memory_space=pltpu.VMEM)
SMEM = pl.BlockSpec(memory_space=pltpu.SMEM)
LIMIT = 26 << 20
LAST_LIMIT = 56 << 20
NO_COST = pl.CostEstimate(flops=int(2e10), bytes_accessed=int(5e7), transcendentals=0)


def forward_shapes(layers, total, width, hidden):
    sizes = (width, width, 3 * width, width, width, width, hidden, hidden)
    shapes = [((layers, total, size), BF16) for size in sizes]
    shapes += [((layers, total, 128), F32)] * 2
    shapes.append(((total, width), BF16))
    return shapes


def backward_shapes(layers, total, width, hidden, chunks):
    shapes = [((layers, total, size), BF16) for size in (3 * width, width, hidden, width)]
    shapes.append(((chunks, layers, 8, 8 * width + hidden), F32))
    shapes.append(((total, width), BF16))
    return shapes


def run_forward(tick, meta, first_in, recv, mask, gains, biases, weights, kept, rows, per_micro, block=240, unroll=2):
    wqkv, wout, wup, wdown = weights
    layers, width = wqkv.shape[0], wqkv.shape[1]
    hidden = wup.shape[2]
    sizes = (width, width, 3 * width, width, width, width, hidden, hidden)
    pieces = 3 * width // TILE + 1 + 2 * (hidden // TILE)
    fresh = tick == 0
    scratch = [pltpu.VMEM((rows, width), BF16), pltpu.VMEM((rows, width), F32), pltpu.VMEM((1, 3 * width), F32)]
    scratch += [pltpu.VMEM((layers, rows, size), BF16) for size in sizes]
    scratch += [pltpu.VMEM((layers, rows, 128), F32)] * 2
    scratch += [pltpu.SemaphoreType.DMA((layers, pieces)), pltpu.SemaphoreType.DMA((layers, 10)), pltpu.SemaphoreType.DMA]
    flops = 2 * rows * (wqkv.size + wout.size + wup.size + wdown.size)
    moved = 2 * (wqkv.size + wout.size + wup.size + wdown.size) + 2 * layers * rows * sum(sizes)
    total = first_in.shape[0]
    shapes = [jax.ShapeDtypeStruct(*k) for k in forward_shapes(layers, total, width, hidden)]
    out = pl.pallas_call(
        functools.partial(forward_kernel, tick, len(kept), rows, block, per_micro, unroll),
        out_shape=[jax.ShapeDtypeStruct((rows, width), BF16)] + shapes + [pltpu.VMEM(w.shape, BF16) for w in weights],
        in_specs=[SMEM, HBM, FREE, VMEM, VMEM, VMEM] + [HBM if fresh else VMEM] * 4 + [HBM] * len(kept),
        out_specs=[VMEM] + [HBM] * 11 + [VMEM] * 4,
        scratch_shapes=scratch,
        input_output_aliases={10 + i: 1 + i for i in range(len(kept))} | ({} if fresh else {6 + i: 12 + i for i in range(4)}),
        compiler_params=pltpu.CompilerParams(vmem_limit_bytes=LIMIT),
        cost_estimate=pl.CostEstimate(flops=flops, bytes_accessed=moved, transcendentals=0),
        name="section_forward",
    )(meta, first_in, recv, mask, gains, biases, *weights, *kept)
    return out[0], list(out[1:12]), list(out[12:])


def run_backward(tick, top, count, meta, last_in, recv, mask, gains, weights, kept, made, rows, per_micro,
                 block=240, unroll=8):
    wqkv, wout, wup, wdown = weights
    layers, width = wqkv.shape[0], wqkv.shape[1]
    hidden = wup.shape[2]
    n1, _, qkv, _, n2, _, u, _, r1, r2, _ = kept
    scratch = [pltpu.VMEM((rows, width), BF16), pltpu.VMEM((rows, width), F32), pltpu.VMEM((rows, width), F32),
               pltpu.VMEM((rows, width), BF16)]
    scratch += [pltpu.VMEM((layers, rows, size), BF16) for size in (width, 3 * width, width, hidden)]
    scratch += [pltpu.VMEM((layers, rows, 128), F32)] * 2
    scratch += [pltpu.VMEM((layers, rows, size), BF16) for size in (3 * width, width, hidden, width)]
    scratch += [pltpu.VMEM((layers, 8, 8 * width + hidden), F32)]
    scratch += [pltpu.SemaphoreType.DMA((layers, 6)), pltpu.SemaphoreType.DMA((layers, 5)), pltpu.SemaphoreType.DMA]
    loaded = count < layers
    if loaded:
        scratch.append(pltpu.SemaphoreType.DMA((4,)))
        scratch += [pltpu.VMEM((1,) + w.shape[1:], BF16) for w in weights]
    total = (wqkv.size + wout.size + wup.size + wdown.size) * count // layers
    shapes = [jax.ShapeDtypeStruct(*k) for k in backward_shapes(
        layers, last_in.shape[0], width, hidden, last_in.shape[0] // rows)]
    out = pl.pallas_call(
        functools.partial(backward_kernel, tick, top, count, len(made), rows, block, per_micro, unroll),
        out_shape=[jax.ShapeDtypeStruct((rows, width), BF16 if count == top + 1 else F32)] + shapes
        + ([] if loaded else [pltpu.VMEM(w.shape, BF16) for w in weights]),
        in_specs=[SMEM, HBM, FREE, VMEM, VMEM] + [HBM if loaded else VMEM] * 4 + [HBM] * 6 + [HBM] * len(made),
        out_specs=[VMEM] + [HBM] * 6 + ([] if loaded else [VMEM] * 4),
        scratch_shapes=scratch,
        input_output_aliases={15 + i: 1 + i for i in range(len(made))} | (
            {} if loaded else {5 + i: 7 + i for i in range(4)}),
        compiler_params=pltpu.CompilerParams(vmem_limit_bytes=LAST_LIMIT if loaded else LIMIT),
        cost_estimate=NO_COST,
        name="section_backward",
    )(meta, last_in, recv, mask, gains, *weights, n1, qkv, n2, u, r1, r2, *made)
    return out[0], list(out[1:7]), weights if loaded else list(out[7:])


def run_gradient(jobs, tick, meta, arrays, grid, small=None, patched=False):
    rows = arrays[jobs[0][0]].shape[1]
    inputs = list(arrays) + ([] if small is None else [small])
    height = sum(arrays[left].shape[2] // grid * (arrays[right].shape[2] // TILE) for left, right, _, _ in jobs)
    tiles = sum(arrays[left].shape[2] * arrays[right].shape[2] // TILE ** 2 for left, right, _, _ in jobs)
    flops = 2 * rows * tiles * TILE ** 2
    if small is not None:
        height += small.shape[2]
    width = arrays[jobs[0][1]].shape[2]
    patch = next((inputs[job[3]] for job in jobs if job[3] is not None), jax.ShapeDtypeStruct((16, 128), BF16))
    scratch = [pltpu.VMEM(arrays[left].shape[1:], BF16) for left, _, _, _ in jobs]
    scratch += [pltpu.VMEM(arrays[right].shape[1:], BF16) for _, right, _, _ in jobs]
    scratch += [pltpu.VMEM((tiles, TILE, TILE), BF16), pltpu.VMEM(patch.shape, patch.dtype),
                pltpu.SemaphoreType.DMA((len(jobs), 2)), pltpu.SemaphoreType.DMA((tiles + 1, 2)), pltpu.SemaphoreType.DMA]
    if small is not None:
        scratch.append(pltpu.VMEM(small.shape, small.dtype))
    shape = jax.ShapeDtypeStruct((grid // 2, height, TILE), BF16)
    return pl.pallas_call(
        functools.partial(gradient_kernel, jobs, grid, tick, len(inputs)),
        out_shape=[shape, shape],
        in_specs=[SMEM] + [HBM] * len(inputs),
        out_specs=[HBM, HBM],
        scratch_shapes=scratch,
        compiler_params=pltpu.CompilerParams(vmem_limit_bytes=LAST_LIMIT),
        cost_estimate=NO_COST,
        name="weight_gradient",
    )(meta, *inputs)


def split_kernel(_, keep_a, recv_a, keep_b, recv_b, send_o, keep_o):
    send_o[...] = (keep_a[...].astype(F32) + recv_a[...].astype(F32)).astype(BF16)
    keep_o[...] = (keep_b[...].astype(F32) + recv_b[...].astype(F32)).astype(BF16)


def run_split(mine, keep, recv, inner):
    blocks, height, width = keep.shape

    def half(pick):
        return pl.BlockSpec((1, height, width), lambda j, mine: (
            (j // inner * 2 + (mine[0] if pick else 1 - mine[0])) * inner + j % inner, 0, 0))

    out = pl.BlockSpec((1, height, width), lambda j, mine: (j, 0, 0))
    shape = jax.ShapeDtypeStruct((blocks // 2, height, width), BF16)
    return pl.pallas_call(
        split_kernel,
        out_shape=[shape, shape],
        grid_spec=pltpu.PrefetchScalarGridSpec(
            num_scalar_prefetch=1, grid=(blocks // 2,),
            in_specs=[half(False), half(False), half(True), half(True)], out_specs=[out, out]),
        compiler_params=pltpu.CompilerParams(vmem_limit_bytes=LAST_LIMIT),
        cost_estimate=NO_COST,
        name="split_sum",
    )(mine, keep, recv, keep, recv)


def last_kernel(keep, recv, out):
    out[...] = keep[...].astype(F32) + recv[...].astype(F32)


def run_last(keep, recv):
    _, height, width = keep.shape
    tall = height // 2 if height % 32 == 0 else height
    spec = pl.BlockSpec((None, tall, width), lambda j: (0, j, 0))
    return pl.pallas_call(
        last_kernel,
        out_shape=jax.ShapeDtypeStruct((height, width), F32),
        grid=(height // tall,),
        in_specs=[spec, spec],
        out_specs=pl.BlockSpec((tall, width), lambda j: (j, 0)),
        compiler_params=pltpu.CompilerParams(vmem_limit_bytes=LAST_LIMIT),
        cost_estimate=NO_COST,
        name="last_sum",
    )(keep, recv)


def hop(value, steps):
    count = lax.axis_size("section")
    pairs = [(s, s + steps) for s in range(count) if 0 <= s + steps < count]
    return lax.ppermute(value, "section", pairs) if pairs else jnp.zeros_like(value)


def after(value, token):
    return value if token is None else lax.optimization_barrier((value, token))[0]


class Piece:
    def __init__(self, send, keep, order):
        self.bits = lax.axis_size("dp").bit_length() - 1
        self.left = list(reversed(range(1, self.bits)))
        self.order = list(order)
        self.send, self.keep = send, keep
        self.recv = None

    def start(self):
        bit = self.order.pop(0)
        pairs = [(device, device ^ (1 << bit)) for device in range(lax.axis_size("dp"))]
        self.recv = lax.ppermute(self.send, "dp", pairs)
        return self.send

    def finish(self, token):
        recv = after(self.recv, token)
        self.recv = None
        if not self.order:
            self.keep = run_last(self.keep, recv)
            return self.keep
        bit = self.order[0]
        spot = self.left.index(bit)
        self.left.remove(bit)
        mine = ((lax.axis_index("dp") >> bit) & 1).astype(jnp.int32).reshape(1)
        self.send, self.keep = run_split(mine, self.keep, recv, 2 ** (len(self.left) - spot))
        return self.send


def shards(
    section_input, out_cotangent, series_counts, norm_gains, biases,
    qkv_weight, out_weight, up_weight, down_weight,
):
    sections = lax.axis_size("section")
    section = lax.axis_index("section")
    group = lax.axis_size("dp")
    micro_count, per_micro, width = section_input.shape
    layers = qkv_weight.shape[0]
    hidden = up_weight.shape[2]
    total = micro_count * per_micro
    rows = MICROS * per_micro
    chunks = micro_count // MICROS
    ticks = chunks + 2 * (sections - 1)
    weights = (qkv_weight, out_weight, up_weight, down_weight)
    last_weights = weights
    mask = mask_table()
    counts = jnp.broadcast_to(series_counts.reshape(1, micro_count), (ticks, micro_count))
    tick_ids = jnp.arange(ticks, dtype=jnp.int32)
    core = jnp.broadcast_to(lax.axis_index("dp") & 1, (ticks, 1))

    def table(place):
        chunk = tick_ids - 2 * place
        active = (chunk >= 0) & (chunk < chunks)
        edge = jnp.broadcast_to(place == 0, (ticks,))
        columns = [active, jnp.clip(chunk, 0, chunks - 1), edge]
        columns = [column.astype(jnp.int32)[:, None] for column in columns]
        return jnp.concatenate(columns + [counts, core], axis=1)

    tables = (table(section), table(sections - 1 - section), mask)
    forward_meta, backward_meta, mask = lax.optimization_barrier(tables)
    entering = section_input.reshape(total, width)
    leaving = out_cotangent.reshape(total, width)
    meta = forward_meta
    arrived = [entering] * 2
    kept = []
    for tick in range(ticks):
        sent, kept, weights = run_forward(
            tick, meta, entering, arrived[tick], mask, norm_gains, biases, weights, kept, rows, per_micro)
        if tick + 2 < ticks:
            arrived.append(hop(sent, 1))
    meta = backward_meta
    arrived = [leaving] * 2
    made = []

    def back(tick, top, count, recv, table_now, made, weights):
        return run_backward(tick, top, count, table_now, leaving, recv, mask, norm_gains, weights, kept, made,
                            rows, per_micro)

    final = ticks - 1
    for tick in range(final):
        sent, made, weights = back(tick, layers - 1, layers, arrived[tick], meta, made, weights)
        if tick + 2 < ticks:
            arrived.append(hop(sent, -1))
    e1, attended, e2, hidden_rows, outputs = kept[1], kept[3], kept[5], kept[7], kept[10]
    top = layers - 1
    bits = group.bit_length() - 1
    near = range(bits)

    def gradient(names, layer, token, order, small=None, patch=None):
        dqkv, da, du, df = made[:4]
        table_of = {"qkv": (e1, dqkv), "out": (attended, da), "up": (e2, du), "down": (hidden_rows, df)}
        arrays, jobs = [], []
        for name in names:
            arrays += table_of[name]
            jobs.append((len(arrays) - 2, len(arrays) - 1, layer, None))
        if patch is not None:
            jobs = [job[:3] + (len(arrays),) for job in jobs]
            arrays.append(patch)
        send, keep = run_gradient(tuple(jobs), final, after(meta, token), arrays, group, small)
        return Piece(send, keep, order)

    token = None
    pieces = {}

    def begin(name, names, layer, order, **more):
        nonlocal token
        pieces[name] = gradient(names, layer, token, order, **more)
        token = pieces[name].start()

    def step(*names):
        nonlocal token
        for name in names:
            token = pieces[name].finish(token)
            if pieces[name].order:
                pieces[name].start()

    begin(0, ("down",), top, near, patch=arrived[final])
    middle, made, _ = back(final, top, top, arrived[final], after(meta, token), made, last_weights)
    token = middle
    step(0)
    begin(1, ("up", "out"), top, near)
    begin(2, ("qkv",), top, near)
    step(1, 0)
    begin(3, ("down",), 0, near, patch=middle)
    step(2, 0)
    _, made, _ = back(final, 0, 1, middle, after(meta, token), made, last_weights)
    dqkv, da, du, df, sums, input_grads = made
    token = input_grads
    step(0, 3)
    begin(4, ("qkv",), 0, near)
    step(1)
    begin(5, ("up",), 0, near)
    step(4)
    small = jnp.sum(sums, axis=(0, 2)).astype(BF16)
    cut = biases.shape[1]
    small = jnp.concatenate([small[:, :cut].reshape(layers, group, -1), small[:, cut:].reshape(layers, group, -1)], axis=2)
    used = small.shape[2]
    small = jnp.swapaxes(small, 0, 1).reshape(group, layers * used)
    small = jnp.pad(small, ((0, 0), (0, 8 * TILE - layers * used))).reshape(group // 2, 2, 8, TILE)
    begin(6, ("out",), 0, near, small=small)
    step(1, 5, 6, 2, 1, 2, 3, 2, 3, 4, 3, 4, 5, 4, 5, 6, 5, 6, 6)
    for piece in pieces.values():
        while piece.order or piece.recv is not None:
            token = piece.finish(token)
            if piece.order:
                piece.start()

    def unpack(packed, at, deep, wide):
        block = deep // group
        tall = block * (wide // TILE)
        return jnp.swapaxes(packed[at:at + tall].reshape(wide // TILE, block, TILE), 0, 1).reshape(block, wide)

    up_rows, out_rows = width // group * (hidden // TILE), width // group
    got = {name: piece.keep for name, piece in pieces.items()}
    grad_down = [unpack(got[3], 0, hidden, width), unpack(got[0], 0, hidden, width)]
    grad_up = [unpack(got[5], 0, width, hidden), unpack(got[1], 0, width, hidden)]
    grad_out = [unpack(got[6], 0, width, width), unpack(got[1], up_rows, width, width)]
    grad_qkv = [unpack(got[4], 0, width, 3 * width), unpack(got[2], 0, width, 3 * width)]
    small = got[6][out_rows:].reshape(-1)[:layers * used].reshape(layers, used)
    return (
        outputs.reshape(1, micro_count, per_micro, width),
        input_grads.reshape(1, micro_count, per_micro, width),
        small[:, cut // group:],
        small[:, :cut // group],
        jnp.stack(grad_qkv), jnp.stack(grad_out), jnp.stack(grad_up), jnp.stack(grad_down),
    )


def solution(mesh):
    stacked = P("section", None, None)
    return jax.shard_map(
        shards,
        mesh=mesh,
        in_specs=(P(None, "dp", None), P(None, "dp", None), P(None, "dp"),
                  P("section", None), P("section", None), stacked, stacked, stacked, stacked),
        out_specs=(P("section", None, "dp", None), P("section", None, "dp", None),
                   P("section", "dp"), P("section", "dp"),
                   P("section", "dp", None), P("section", "dp", None),
                   P("section", "dp", None), P("section", "dp", None)),
        check_vma=False,
    )
```

```python
import functools

import jax
import jax.numpy as jnp
from jax import lax
from jax.experimental import pallas as pl
from jax.experimental.pallas import tpu as pltpu
from jax.sharding import PartitionSpec as P

HEADS = 8
HEAD_DIM = 128
SEG = 15
LAYERS_DEV = 2
EPSILON = 1e-05
MICROS = 2
NEGATIVE = -1e30
SCALE = HEAD_DIM ** (-0.5)
GELU_A = 0.7978845608028654
GELU_B = 0.044715
TILE = 1024
STEP = 512
F32 = jnp.float32
BF16 = jnp.bfloat16


def dot_nn(left, right):
    return jnp.dot(left, right, preferred_element_type=F32)


def dot_nt(left, right):
    return lax.dot_general(left, right, (((1,), (1,)), ((), ())), preferred_element_type=F32)


def dot_tn(left, right):
    return lax.dot_general(left, right, (((0,), (0,)), ((), ())), preferred_element_type=F32)


def query_blocks(rows):
    blocks = []
    for base in range(0, rows, 240):
        blocks += [(base, 128, base), (base + 128, 112, base + 112)]
    return blocks


def mask_table():
    tables = []
    for query_start, key_start in ((0, 0), (128, 112)):
        query = query_start + lax.broadcasted_iota(jnp.int32, (128, 128), 0)
        key = key_start + lax.broadcasted_iota(jnp.int32, (128, 128), 1)
        seen = (query // SEG == key // SEG) & (key <= query)
        tables.append(jnp.where(seen, 0.0, NEGATIVE).astype(F32))
    return jnp.stack(tables)


def fold_rows(values):
    rows, width = values.shape
    return jnp.sum(values.reshape(rows // 8, 8, width), axis=0)


def live_column(meta, tick, rows, per_micro):
    micros = rows // per_micro
    row = lax.broadcasted_iota(jnp.int32, (rows, 1), 0)
    live = None
    for micro in range(micros):
        count = meta[tick, 3 + meta[tick, 1] * micros + micro]
        inside = (row >= micro * per_micro) & (row < micro * per_micro + count * SEG)
        live = inside if live is None else live | inside
    return live.astype(F32)


def exponent(scores, mask):
    scores = scores + mask
    return jnp.exp((scores - jnp.max(scores, axis=-1, keepdims=True)) * SCALE)


def forward_kernel(
    tick, aliased, rows, block, per_micro, unroll,
    meta, first_in, recv, mask, gains, biases, wqkv, wout, wup, wdown,
    *refs,
):
    (y_ref, n1_o, e1_o, qkv_o, o_o, n2_o, e2_o, u_o, h_o, r1_o, r2_o, made_o) = refs[aliased:aliased + 12]
    fresh = tick == 0
    wq, wo, wu, wd = refs[aliased + 12:aliased + 16]
    (xb, xs, qb, n1_s, e1_s, qkv_s, o_s, n2_s, e2_s, u_s, h_s, r1_s, r2_s,
     wsem, ssem, xsem) = refs[aliased + 16:]
    width = xs.shape[1]
    hidden = wu.shape[2]
    layers = wq.shape[0]

    def weight_pieces(layer):
        pieces = []
        for tile in range(3 * width // TILE):
            cut = pl.ds(tile * TILE, TILE)
            pieces.append((wqkv.at[layer, :, cut], wq.at[layer, :, cut]))
        pieces.append((wout.at[layer], wo.at[layer]))
        for tile in range(hidden // TILE):
            cut = pl.ds(tile * TILE, TILE)
            pieces.append((wup.at[layer, :, cut], wu.at[layer, :, cut]))
        for tile in range(hidden // TILE):
            cut = pl.ds(tile * TILE, TILE)
            pieces.append((wdown.at[layer, cut, :], wd.at[layer, cut, :]))
        return pieces

    def each_weight(act):
        for layer in range(layers):
            for spot, (source, target) in enumerate(weight_pieces(layer)):
                act(pltpu.make_async_copy(source, target, wsem.at[layer, spot]))

    def wait_weight(layer, spot, source, target):
        if fresh:
            pltpu.make_async_copy(source, target, wsem.at[layer, spot]).wait()

    if fresh:
        @pl.when(meta[tick, 0] == 1)
        def _():
            copy = pltpu.make_async_copy(first_in.at[pl.ds(0, rows)], xb, xsem)
            copy.start()
            copy.wait()
            each_weight(lambda copy: copy.start())


        @pl.when(meta[tick, 0] != 1)
        def _():
            each_weight(lambda copy: copy.start())
            each_weight(lambda copy: copy.wait())

    n_qkv = 3 * width // TILE
    n_hid = hidden // TILE
    at_out = n_qkv
    at_up = n_qkv + 1
    at_down = at_up + n_hid

    @pl.when(meta[tick, 0] == 1)
    def _():
        row0 = pl.multiple_of(meta[tick, 1] * rows, 16)

        if not fresh:
            @pl.when(meta[tick, 2] == 1)
            def _():
                copy = pltpu.make_async_copy(first_in.at[pl.ds(row0, rows)], xb, xsem)
                copy.start()
                copy.wait()

            @pl.when(meta[tick, 2] != 1)
            def _():
                copy = pltpu.make_async_copy(recv.at[pl.ds(0, rows)], xb, xsem)
                copy.start()
                copy.wait()

        saves = ((n1_s, n1_o), (e1_s, e1_o), (qkv_s, qkv_o), (o_s, o_o), (n2_s, n2_o), (e2_s, e2_o),
                 (u_s, u_o), (h_s, h_o), (r1_s, r1_o), (r2_s, r2_o))

        def save(layer, spot):
            source, target = saves[spot]
            return pltpu.make_async_copy(
                source.at[layer], target.at[layer, pl.ds(row0, rows)], ssem.at[layer, spot])

        @pl.loop(0, rows // block)
        def _(step):
            cut = pl.ds(pl.multiple_of(step * block, 16), block)
            xs[cut, :] = xb[cut, :].astype(F32)

        def norm(layer, gain, shift, n_s, e_s, r_s):
            @pl.loop(0, rows // block)
            def _(step):
                cut = pl.ds(pl.multiple_of(step * block, 16), block)
                values = xs[cut, :]
                centred = values - jnp.mean(values, axis=-1, keepdims=True)
                inverse = lax.rsqrt(jnp.mean(centred * centred, axis=-1, keepdims=True) + EPSILON)
                normed = centred * inverse
                n_s[layer, cut, :] = normed.astype(BF16)
                e_s[layer, cut, :] = (normed * gain + shift).astype(BF16)
                r_s[layer, cut, :] = jnp.broadcast_to(inverse, (block, 128))

        @pl.loop(0, layers)
        def _(layer):
            norm(layer, gains[pl.ds(layer, 1), :width], biases[pl.ds(layer, 1), :width], n1_s, e1_s, r1_s)
            save(layer, 0).start()
            save(layer, 1).start()
            save(layer, 8).start()
            qb[:, :width] = biases[pl.ds(layer, 1), width:2 * width]
            qb[:, width:2 * width] = jnp.zeros((1, width), F32)
            qb[:, 2 * width:] = biases[pl.ds(layer, 1), 2 * width:3 * width]

            for tile in range(n_qkv):
                cut = pl.ds(tile * TILE, TILE)
                wait_weight(layer, tile, wqkv.at[layer, :, cut], wq.at[layer, :, cut])
                for start in range(tile * TILE, (tile + 1) * TILE, STEP):
                    part = pl.ds(start, STEP)
                    qkv_s[layer, :, part] = (dot_nn(e1_s[layer], wq[layer, :, part]) + qb[:, part]).astype(BF16)

            save(layer, 2).start()

            jobs = [(head * HEAD_DIM, spot % 2, q0, nq, k0) for head in range(HEADS)
                    for spot, (q0, nq, k0) in enumerate(query_blocks(rows))]
            scores = []
            for col, _, q0, nq, k0 in jobs:
                query = qkv_s[layer, q0:q0 + nq, col:col + HEAD_DIM]
                key = qkv_s[layer, k0:k0 + 128, width + col:width + col + HEAD_DIM]
                scores.append(dot_nt(query, key))
            soft = []
            for (_, kind, _, nq, _), score in zip(jobs, scores):
                raised = exponent(score, mask[kind, :nq, :])
                soft.append((raised * (1.0 / jnp.sum(raised, axis=-1, keepdims=True))).astype(BF16))
            for (col, _, q0, nq, k0), share in zip(jobs, soft):
                value = qkv_s[layer, k0:k0 + 128, 2 * width + col:2 * width + col + HEAD_DIM]
                o_s[layer, q0:q0 + nq, col:col + HEAD_DIM] = dot_nn(share, value).astype(BF16)

            save(layer, 3).start()
            wait_weight(layer, at_out, wout.at[layer], wo.at[layer])
            for start in range(0, width, STEP):
                part = pl.ds(start, STEP)
                xs[:, part] += dot_nn(o_s[layer], wo[layer, :, part]) + biases[pl.ds(layer, 1), pl.ds(3 * width + start, STEP)]
            norm(layer, gains[pl.ds(layer, 1), width:], biases[pl.ds(layer, 1), 4 * width:5 * width], n2_s, e2_s, r2_s)
            save(layer, 4).start()
            save(layer, 5).start()
            save(layer, 9).start()

            for tile in range(n_hid):
                cut = pl.ds(tile * TILE, TILE)
                wait_weight(layer, at_up + tile, wup.at[layer, :, cut], wu.at[layer, :, cut])
                for start in range(tile * TILE, (tile + 1) * TILE, STEP):
                    part = pl.ds(start, STEP)
                    pre = dot_nn(e2_s[layer], wu[layer, :, part]) + biases[pl.ds(layer, 1), pl.ds(6 * width + start, STEP)]
                    u_s[layer, :, part] = pre.astype(BF16)
                    half = 0.5 * pre
                    turned = jnp.tanh(pre * (GELU_A + (GELU_A * GELU_B) * (pre * pre)))
                    h_s[layer, :, part] = (half + half * turned).astype(BF16)

            save(layer, 6).start()
            save(layer, 7).start()
            for tile in range(n_hid):
                cut = pl.ds(tile * TILE, TILE)
                wait_weight(layer, at_down + tile, wdown.at[layer, cut, :], wd.at[layer, cut, :])
            for start in range(0, width, STEP):
                part = pl.ds(start, STEP)
                xs[:, part] += dot_nn(h_s[layer], wd[layer, :, part]) + biases[pl.ds(layer, 1), pl.ds(5 * width + start, STEP)]

        y_ref[...] = (xs[...] * live_column(meta, tick, rows, per_micro)).astype(BF16)
        made = pltpu.make_async_copy(y_ref, made_o.at[pl.ds(row0, rows)], xsem)
        made.start()
        for layer in range(layers):
            for spot in range(len(saves)):
                save(layer, spot).wait()
        made.wait()


def backward_kernel(
    tick, top, count, part, aliased, rows, block, per_micro, unroll,
    meta, token, last_in, recv, mask, gains, wqkv, wout, wup, wdown,
    n1_i, qkv_i, n2_i, u_i, r1_i, r2_i,
    *refs,
):
    (gx_ref, dqkv_o, da_o, du_o, df_o, sums_o, made_o) = refs[aliased:aliased + 7]
    loaded = part == 3
    wq, wo, wu, wd = refs[-4:] if loaded else refs[aliased + 7:aliased + 11]
    (gb, gs, de_s, do_s, n1_s, qkv_s, n2_s, u_s, r1_s, r2_s,
     dqkv_s, da_s, du_s, df_s, sums_s, lsem, ssem, xsem) = (
         refs[aliased + 7:-5] if loaded else refs[aliased + 11:])
    width = gs.shape[1]
    hidden = wu.shape[2]
    lower, upper = part != 1, part != 2
    first, last = top + 1 == wqkv.shape[0] and upper, top + 1 == count and lower

    def weight(spot):
        pair = ((wdown, wd), (wup, wu), (wout, wo), (wqkv, wq))[spot]
        return pltpu.make_async_copy(pair[0].at[top], pair[1].at[0], refs[-5].at[spot])

    def weight_here(spot):
        if loaded:
            weight(spot).wait()
    HALF = 1024

    @pl.when(meta[tick, 0] == 1)
    def _():
        row0 = pl.multiple_of(meta[tick, 1] * rows, 16)

        if first:
            @pl.when(meta[tick, 2] == 1)
            def _():
                copy = pltpu.make_async_copy(last_in.at[pl.ds(row0, rows)], gb, xsem)
                copy.start()
                copy.wait()

            @pl.when(meta[tick, 2] != 1)
            def _():
                copy = pltpu.make_async_copy(recv.at[pl.ds(0, rows)], gb, xsem)
                copy.start()
                copy.wait()

            gs[...] = gb[...].astype(F32) * live_column(meta, tick, rows, per_micro)
        else:
            copy = pltpu.make_async_copy(recv, gs, xsem)
            copy.start()
            copy.wait()

        loads = ((u_i, u_s), (n2_i, n2_s), (r2_i, r2_s), (qkv_i, qkv_s), (n1_i, n1_s), (r1_i, r1_s))

        def load(layer, spot):
            source, target = loads[spot]
            return pltpu.make_async_copy(
                source.at[layer, pl.ds(row0, rows)], target.at[layer], lsem.at[layer, spot])

        saves = ((df_s, df_o), (du_s, du_o), (da_s, da_o), (dqkv_s, dqkv_o))
        spots = (range(3) if upper else ()), (range(3, 4) if lower else ())
        spots = [spot for group in spots for spot in group]
        spans = ([(3 * width, 6 * width + hidden), (7 * width + hidden, 8 * width + hidden)] if upper else []) + (
            [(0, 3 * width), (6 * width + hidden, 7 * width + hidden)] if lower else [])

        def save(layer, spot):
            source, target = saves[spot]
            return pltpu.make_async_copy(
                source.at[layer], target.at[layer, pl.ds(row0, rows)], ssem.at[layer, spot])

        def save_sums(layer):
            return [pltpu.make_async_copy(
                sums_s.at[layer, :, low:high], sums_o.at[meta[tick, 1], layer, :, low:high], ssem.at[layer, 4 + spot])
                for spot, (low, high) in enumerate(spans)]

        def begin_loads(spots, weights):
            for layer in range(top, top - count, -1):
                for spot in spots:
                    load(layer, spot).start()
            if loaded:
                for spot in weights:
                    weight(spot).start()

        begin_loads((0,) if loaded else range(6), (0,))

        sums_s[...] = jnp.zeros(sums_s.shape, F32)

        def add_sum(layer, start, size, values):
            sums_s[layer, :, pl.ds(start, size)] += fold_rows(values)

        def norm_back(layer, gain, n_s, r_s, shift_at, gain_at, narrow):
            @pl.loop(0, rows // block)
            def _(step):
                cut = pl.ds(pl.multiple_of(step * block, 16), block)
                grad = de_s[cut, :]
                normed = n_s[layer, cut, :].astype(F32)
                scaled = grad * gain
                along = grad * normed
                first = jnp.mean(scaled, axis=-1, keepdims=True)
                second = jnp.mean(along * gain, axis=-1, keepdims=True)
                inverse = r_s[layer, cut, :1]
                fresh = gs[cut, :] + inverse * (scaled - first - normed * second)
                gs[cut, :] = fresh
                add_sum(layer, shift_at, width, grad)
                add_sum(layer, gain_at, width, along)
                if narrow is not None:
                    rounded = fresh.astype(BF16)
                    narrow[layer, cut, :] = rounded
                    add_sum(layer, 3 * width, width, rounded.astype(F32))

        @pl.loop(0, count)
        def _(turn):
            layer = top - turn

            shelf = 0 if loaded else layer
            if upper:
                @pl.loop(0, rows // block)
                def _(step):
                    cut = pl.ds(pl.multiple_of(step * block, 16), block)
                    rounded = gs[cut, :].astype(BF16)
                    df_s[layer, cut, :] = rounded
                    add_sum(layer, 5 * width, width, rounded.astype(F32))

                save(layer, 0).start()
                load(layer, 0).wait()
                weight_here(0)
                if loaded:
                    begin_loads((1, 2), (1,))

                @pl.loop(0, hidden // HALF)
                def _(tile):
                    cut = pl.ds(pl.multiple_of(tile * HALF, HALF), HALF)
                    back = dot_nt(df_s[layer], wd[shelf, cut, :]).astype(BF16).astype(F32)
                    pre = u_s[layer, :, cut].astype(F32)
                    square = pre * pre
                    turned = jnp.tanh(GELU_A * pre * (1.0 + GELU_B * square))
                    slope = 0.5 * (1.0 + turned) + (0.5 * GELU_A) * pre * (1.0 - turned * turned) * (
                        1.0 + (3.0 * GELU_B) * square)
                    rounded = (back * slope).astype(BF16)
                    du_s[layer, :, cut] = rounded
                    add_sum(layer, pl.multiple_of(6 * width + tile * HALF, HALF), HALF, rounded.astype(F32))

                save(layer, 1).start()
                weight_here(1)
                if loaded:
                    begin_loads((3, 4, 5), (2, 3))

                @pl.loop(0, width // HALF)
                def _(tile):
                    cut = pl.ds(pl.multiple_of(tile * HALF, HALF), HALF)
                    de_s[:, cut] = dot_nt(du_s[layer], wu[shelf, cut, :])

                load(layer, 1).wait()
                load(layer, 2).wait()
                norm_back(layer, gains[pl.ds(layer, 1), width:], n2_s, r2_s, 4 * width, 9 * width, da_s)
                save(layer, 2).start()
            if lower:
                if not upper:
                    da_s[layer] = gs[...].astype(BF16)
                weight_here(2)
                do_s[...] = dot_nt(da_s[layer], wo[shelf]).astype(BF16)
                load(layer, 3).wait()

                @pl.loop(0, HEADS // unroll)
                def _(group):
                    jobs = []
                    for inner in range(unroll):
                        col = pl.multiple_of((group * unroll + inner) * HEAD_DIM, HEAD_DIM)
                        cuts = (pl.ds(col, HEAD_DIM), pl.ds(width + col, HEAD_DIM), pl.ds(2 * width + col, HEAD_DIM))
                        jobs += [(cuts, spot % 2, q0, nq, k0) for spot, (q0, nq, k0) in enumerate(query_blocks(rows))]
                    first = []
                    for cuts, _, q0, nq, k0 in jobs:
                        query = qkv_s[layer, q0:q0 + nq, cuts[0]]
                        key = qkv_s[layer, k0:k0 + 128, cuts[1]]
                        value = qkv_s[layer, k0:k0 + 128, cuts[2]]
                        grad = do_s[q0:q0 + nq, cuts[0]]
                        first.append((dot_nt(query, key), dot_nt(grad, value)))
                    second = []
                    for (_, kind, _, nq, _), (score, soft_grad) in zip(jobs, first):
                        raised = exponent(score, mask[kind, :nq, :])
                        soft = raised * (1.0 / jnp.sum(raised, axis=-1, keepdims=True))
                        inner_sum = jnp.sum(soft_grad * soft, axis=-1, keepdims=True)
                        second.append((soft.astype(BF16), (soft * (soft_grad - inner_sum)).astype(BF16)))
                    tail_k = tail_v = None
                    for (cuts, kind, q0, nq, k0), (soft, score_grad) in zip(jobs, second):
                        query = qkv_s[layer, q0:q0 + nq, cuts[0]]
                        key = qkv_s[layer, k0:k0 + 128, cuts[1]]
                        grad = do_s[q0:q0 + nq, cuts[0]]
                        dqkv_s[layer, q0:q0 + nq, cuts[0]] = (dot_nn(score_grad, key) * SCALE).astype(BF16)
                        dk = dot_tn(score_grad, query) * SCALE
                        dv = dot_tn(soft, grad)
                        if kind == 0:
                            tail_k, tail_v = dk[112:], dv[112:]
                            high = 112
                            dk, dv = dk[:112], dv[:112]
                        else:
                            high = 128
                            dk = jnp.concatenate([dk[:16] + tail_k, dk[16:]], axis=0)
                            dv = jnp.concatenate([dv[:16] + tail_v, dv[16:]], axis=0)
                        dqkv_s[layer, k0:k0 + high, cuts[1]] = dk.astype(BF16)
                        dqkv_s[layer, k0:k0 + high, cuts[2]] = dv.astype(BF16)

                sums_s[layer, :, width:2 * width] = fold_rows(dqkv_s[layer, :, :width].astype(F32))
                sums_s[layer, :, 2 * width:3 * width] = fold_rows(dqkv_s[layer, :, 2 * width:].astype(F32))
                save(layer, 3).start()
                weight_here(3)

                @pl.loop(0, width // HALF)
                def _(tile):
                    cut = pl.ds(pl.multiple_of(tile * HALF, HALF), HALF)
                    de_s[:, cut] = dot_nt(dqkv_s[layer], wq[shelf, cut, :])

                load(layer, 4).wait()
                load(layer, 5).wait()
                norm_back(layer, gains[pl.ds(layer, 1), :width], n1_s, r1_s, 0, 8 * width, None)
            for copy in save_sums(layer):
                copy.start()

        if last:
            gx_ref[...] = gs[...].astype(BF16)
            made = pltpu.make_async_copy(gx_ref, made_o.at[pl.ds(row0, rows)], xsem)
            made.start()
        else:
            gx_ref[...] = gs[...]
        for layer in range(top, top - count, -1):
            for spot in spots:
                save(layer, spot).wait()
            for copy in save_sums(layer):
                copy.wait()
        if last:
            made.wait()


def gradient_kernel(
    jobs, cuts, grid, tick, extra,
    meta, token, *refs,
):
    count = 2 * len(cuts)
    inputs, outputs, scratch = refs[:extra], refs[extra:extra + count], refs[extra + count:]
    lefts, rights = scratch[:len(jobs)], scratch[len(jobs):2 * len(jobs)]
    res, patch_s, lsem, osem, psem = scratch[2 * len(jobs):2 * len(jobs) + 5]
    mine = meta[0, meta.shape[1] - 1]
    def tiles_of(spot):
        return lefts[spot].shape[1] // TILE, rights[spot].shape[1] // TILE

    def load(spot, which, tile):
        source, target = ((jobs[spot][0], lefts), (jobs[spot][1], rights))[which]
        cut = pl.ds(pl.multiple_of(tile * TILE, TILE), TILE)
        return pltpu.make_async_copy(
            inputs[source].at[jobs[spot][2], :, cut], target[spot].at[:, cut], lsem.at[spot, which, tile])

    for spot in range(len(jobs)):
        for which in range(2):
            for tile in range(tiles_of(spot)[which]):
                load(spot, which, tile).start()
    sends = []
    at = tile = 0
    for spot, (_, _, _, patch) in enumerate(jobs):
        if spot in cuts:
            at = 0
            send_o, keep_o = outputs[2 * cuts.index(spot):2 * cuts.index(spot) + 2]
        tall, broad = tiles_of(spot)
        if patch is not None:
            load(spot, 1, 0).wait()

            @pl.when(meta[tick, 0] == 1)
            def _():
                rows = patch_s.shape[0]
                copy = pltpu.make_async_copy(inputs[patch], patch_s, psem)
                copy.start()
                copy.wait()
                values = patch_s[...].astype(F32)
                if patch_s.dtype == BF16:
                    values = values * live_column(meta, tick, rows, rows // MICROS)
                cut = pl.ds(pl.multiple_of(meta[tick, 1] * rows, 16), rows)
                rights[spot][cut, :] = values.astype(BF16)

        deep = lefts[spot].shape[1]
        block = deep // grid
        pairs = TILE // (2 * block)

        def send(step, which, send_o=send_o, keep_o=keep_o, at=at, tile=tile):
            output, half = ((send_o, 1 - mine), (keep_o, mine))[which]
            row, col = (step, 0) if tall > 1 else (0, step)
            view = res.at[tile + step].reshape(pairs, 2, block, TILE)
            return pltpu.make_async_copy(
                view.at[:, half], output.at[pl.ds(row * pairs, pairs), pl.ds(at + col * block, block), :],
                osem.at[tile + step, which])

        @pl.loop(0, max(tall, broad))
        def _(step):
            row, col = (step, 0) if tall > 1 else (0, step)
            if tall > 1:
                load(spot, 0, step).wait()
            else:
                @pl.when(step == 0)
                def _():
                    load(spot, 0, 0).wait()

                if patch is None:
                    load(spot, 1, step).wait()
            if tall > 1 and patch is None:
                @pl.when(step == 0)
                def _():
                    load(spot, 1, 0).wait()

            rows_cut = pl.ds(pl.multiple_of(row * TILE, TILE), TILE)
            cols_cut = pl.ds(pl.multiple_of(col * TILE, TILE), TILE)
            res[tile + step] = dot_tn(lefts[spot][:, rows_cut], rights[spot][:, cols_cut]).astype(BF16)
            for which in range(2):
                send(step, which).start()

        for step in range(max(tall, broad)):
            for which in range(2):
                sends.append(send(step, which))
        tile += max(tall, broad)
        at += block * broad
    if send_o.shape[1] > at:
        small_s = scratch[-1]
        copy = pltpu.make_async_copy(inputs[extra - 1], small_s, psem)
        copy.start()
        copy.wait()
        for which, (output, half) in enumerate(((send_o, 1 - mine), (keep_o, mine))):
            copy = pltpu.make_async_copy(small_s.at[:, half], output.at[:, at:, :], osem.at[tile, which])
            copy.start()
            sends.append(copy)
    for copy in sends:
        copy.wait()


HBM = pl.BlockSpec(memory_space=pltpu.HBM)
FREE = pl.BlockSpec(memory_space=pl.ANY)
VMEM = pl.BlockSpec(memory_space=pltpu.VMEM)
SMEM = pl.BlockSpec(memory_space=pltpu.SMEM)
LIMIT = 26 << 20
LAST_LIMIT = 56 << 20
NO_COST = pl.CostEstimate(flops=int(2e11), bytes_accessed=int(5e8), transcendentals=0)


def forward_shapes(layers, total, width, hidden):
    sizes = (width, width, 3 * width, width, width, width, hidden, hidden)
    shapes = [((layers, total, size), BF16) for size in sizes]
    shapes += [((layers, total, 128), F32)] * 2
    shapes.append(((total, width), BF16))
    return shapes


def backward_shapes(layers, total, width, hidden, chunks):
    shapes = [((layers, total, size), BF16) for size in (3 * width, width, hidden, width)]
    shapes.append(((chunks, layers, 8, 8 * width + hidden), F32))
    shapes.append(((total, width), BF16))
    return shapes


def run_forward(tick, meta, first_in, recv, mask, gains, biases, weights, kept, rows, per_micro, block=240, unroll=2):
    wqkv, wout, wup, wdown = weights
    layers, width = wqkv.shape[0], wqkv.shape[1]
    hidden = wup.shape[2]
    sizes = (width, width, 3 * width, width, width, width, hidden, hidden)
    pieces = 3 * width // TILE + 1 + 2 * (hidden // TILE)
    fresh = tick == 0
    scratch = [pltpu.VMEM((rows, width), BF16), pltpu.VMEM((rows, width), F32), pltpu.VMEM((1, 3 * width), F32)]
    scratch += [pltpu.VMEM((layers, rows, size), BF16) for size in sizes]
    scratch += [pltpu.VMEM((layers, rows, 128), F32)] * 2
    scratch += [pltpu.SemaphoreType.DMA((layers, pieces)), pltpu.SemaphoreType.DMA((layers, 10)), pltpu.SemaphoreType.DMA]
    flops = 2 * rows * (wqkv.size + wout.size + wup.size + wdown.size)
    moved = 2 * (wqkv.size + wout.size + wup.size + wdown.size) + 2 * layers * rows * sum(sizes)
    total = first_in.shape[0]
    shapes = [jax.ShapeDtypeStruct(*k) for k in forward_shapes(layers, total, width, hidden)]
    out = pl.pallas_call(
        functools.partial(forward_kernel, tick, len(kept), rows, block, per_micro, unroll),
        out_shape=[jax.ShapeDtypeStruct((rows, width), BF16)] + shapes + [pltpu.VMEM(w.shape, BF16) for w in weights],
        in_specs=[SMEM, HBM, FREE, VMEM, VMEM, VMEM] + [HBM if fresh else VMEM] * 4 + [HBM] * len(kept),
        out_specs=[VMEM] + [HBM] * 11 + [VMEM] * 4,
        scratch_shapes=scratch,
        input_output_aliases={10 + i: 1 + i for i in range(len(kept))} | ({} if fresh else {6 + i: 12 + i for i in range(4)}),
        compiler_params=pltpu.CompilerParams(vmem_limit_bytes=LIMIT),
        cost_estimate=pl.CostEstimate(flops=flops, bytes_accessed=moved, transcendentals=0),
        name="section_forward",
    )(meta, first_in, recv, mask, gains, biases, *weights, *kept)
    return out[0], list(out[1:12]), list(out[12:])


def run_backward(tick, top, count, part, meta, token, last_in, recv, mask, gains, weights, kept, made, rows, per_micro,
                 block=240, unroll=8):
    wqkv, wout, wup, wdown = weights
    layers, width = wqkv.shape[0], wqkv.shape[1]
    hidden = wup.shape[2]
    n1, _, qkv, _, n2, _, u, _, r1, r2, _ = kept
    scratch = [pltpu.VMEM((rows, width), BF16), pltpu.VMEM((rows, width), F32), pltpu.VMEM((rows, width), F32),
               pltpu.VMEM((rows, width), BF16)]
    scratch += [pltpu.VMEM((layers, rows, size), BF16) for size in (width, 3 * width, width, hidden)]
    scratch += [pltpu.VMEM((layers, rows, 128), F32)] * 2
    scratch += [pltpu.VMEM((layers, rows, size), BF16) for size in (3 * width, width, hidden, width)]
    scratch += [pltpu.VMEM((layers, 8, 8 * width + hidden), F32)]
    scratch += [pltpu.SemaphoreType.DMA((layers, 6)), pltpu.SemaphoreType.DMA((layers, 8)), pltpu.SemaphoreType.DMA]
    loaded = part == 3
    if loaded:
        scratch.append(pltpu.SemaphoreType.DMA((4,)))
        scratch += [pltpu.VMEM((1,) + w.shape[1:], BF16) for w in weights]
    total = (wqkv.size + wout.size + wup.size + wdown.size) * count // layers
    shapes = [jax.ShapeDtypeStruct(*k) for k in backward_shapes(
        layers, last_in.shape[0], width, hidden, last_in.shape[0] // rows)]
    out = pl.pallas_call(
        functools.partial(backward_kernel, tick, top, count, part, len(made), rows, block, per_micro, unroll),
        out_shape=[jax.ShapeDtypeStruct((rows, width), BF16 if count == top + 1 and part != 1 else F32)] + shapes
        + ([] if loaded else [pltpu.VMEM(w.shape, BF16) for w in weights]),
        in_specs=[SMEM, FREE, HBM, FREE, VMEM, VMEM] + [HBM if loaded else VMEM] * 4 + [HBM] * 6 + [HBM] * len(made),
        out_specs=[VMEM] + [HBM] * 6 + ([] if loaded else [VMEM] * 4),
        scratch_shapes=scratch,
        input_output_aliases={16 + i: 1 + i for i in range(len(made))} | (
            {} if loaded else {6 + i: 7 + i for i in range(4)}),
        compiler_params=pltpu.CompilerParams(vmem_limit_bytes=LAST_LIMIT if loaded else LIMIT),
        cost_estimate=NO_COST,
        name="section_backward",
    )(meta, token, last_in, recv, mask, gains, *weights, n1, qkv, n2, u, r1, r2, *made)
    return out[0], list(out[1:7]), weights if loaded else list(out[7:])


def run_gradient(jobs, cuts, tick, meta, token, arrays, grid, small=None):
    rows = arrays[jobs[0][0]].shape[1]
    inputs = list(arrays) + ([] if small is None else [small])
    heights = []
    for spot, (left, right, _, _) in enumerate(jobs):
        if spot in cuts:
            heights.append(0)
        heights[-1] += arrays[left].shape[2] // grid * (arrays[right].shape[2] // TILE)
    tiles = sum(arrays[left].shape[2] * arrays[right].shape[2] // TILE ** 2 for left, right, _, _ in jobs)
    flops = 2 * rows * tiles * TILE ** 2
    if small is not None:
        heights[-1] += small.shape[2]
    width = arrays[jobs[0][1]].shape[2]
    patch = next((inputs[job[3]] for job in jobs if job[3] is not None), jax.ShapeDtypeStruct((16, 128), BF16))
    scratch = [pltpu.VMEM(arrays[left].shape[1:], BF16) for left, _, _, _ in jobs]
    scratch += [pltpu.VMEM(arrays[right].shape[1:], BF16) for _, right, _, _ in jobs]
    scratch += [pltpu.VMEM((tiles, TILE, TILE), BF16), pltpu.VMEM(patch.shape, patch.dtype),
                pltpu.SemaphoreType.DMA((len(jobs), 2, 4)), pltpu.SemaphoreType.DMA((tiles + 1, 2)), pltpu.SemaphoreType.DMA]
    if small is not None:
        scratch.append(pltpu.VMEM(small.shape, small.dtype))
    shapes = [jax.ShapeDtypeStruct((grid // 2, height, TILE), BF16) for height in heights for _ in range(2)]
    return pl.pallas_call(
        functools.partial(gradient_kernel, jobs, cuts, grid, tick, len(inputs)),
        out_shape=shapes,
        in_specs=[SMEM, FREE] + [HBM] * len(inputs),
        out_specs=[HBM] * len(shapes),
        scratch_shapes=scratch,
        compiler_params=pltpu.CompilerParams(vmem_limit_bytes=LAST_LIMIT),
        cost_estimate=NO_COST,
        name="weight_gradient",
    )(meta, token, *inputs)


def split_kernel(_, keep_a, recv_a, keep_b, recv_b, token, send_o, keep_o):
    send_o[...] = (keep_a[...].astype(F32) + recv_a[...].astype(F32)).astype(BF16)
    keep_o[...] = (keep_b[...].astype(F32) + recv_b[...].astype(F32)).astype(BF16)


def run_split(table, bit, keep, recv, inner, token):
    blocks, height, width = keep.shape

    def half(pick):
        return pl.BlockSpec((1, height, width), lambda j, mine: (
            (j // inner * 2 + (mine[bit] if pick else 1 - mine[bit])) * inner + j % inner, 0, 0))

    out = pl.BlockSpec((1, height, width), lambda j, mine: (j, 0, 0))
    shape = jax.ShapeDtypeStruct((blocks // 2, height, width), BF16)
    return pl.pallas_call(
        split_kernel,
        out_shape=[shape, shape],
        grid_spec=pltpu.PrefetchScalarGridSpec(
            num_scalar_prefetch=1, grid=(blocks // 2,),
            in_specs=[half(False), half(False), half(True), half(True), FREE], out_specs=[out, out]),
        compiler_params=pltpu.CompilerParams(vmem_limit_bytes=LAST_LIMIT),
        cost_estimate=NO_COST,
        name="split_sum",
    )(table, keep, recv, keep, recv, token)


def last_kernel(keep, recv, token, out):
    out[...] = keep[...].astype(F32) + recv[...].astype(F32)


def run_last(keep, recv, token):
    _, height, width = keep.shape
    tall = height // 2 if height % 32 == 0 else height
    spec = pl.BlockSpec((None, tall, width), lambda j: (0, j, 0))
    return pl.pallas_call(
        last_kernel,
        out_shape=jax.ShapeDtypeStruct((height, width), F32),
        grid=(height // tall,),
        in_specs=[spec, spec, FREE],
        out_specs=pl.BlockSpec((tall, width), lambda j: (j, 0)),
        compiler_params=pltpu.CompilerParams(vmem_limit_bytes=LAST_LIMIT),
        cost_estimate=NO_COST,
        name="last_sum",
    )(keep, recv, token)


PLAN = (
    "b0 g0 g2 s0 g1 s3 s2 s1 b1 s0 g3 s3 s0 s2 s5 s1 s4 s3 s0 s2 g4 s1 s5 s3 s4 s2 s6 s5 s1 s4 s6 s5 s6 s4 s6"
)
TURNS = "AABAABA"


def hop(value, steps):
    count = lax.axis_size("section")
    pairs = [(s, s + steps) for s in range(count) if 0 <= s + steps < count]
    return lax.ppermute(value, "section", pairs) if pairs else jnp.zeros_like(value)


class Piece:
    def __init__(self, send, keep, order, table):
        self.table = table
        self.bits = lax.axis_size("dp").bit_length() - 1
        self.left = list(reversed(range(1, self.bits)))
        self.order = list(order)
        self.send, self.keep = send, keep
        self.recv = None

    def start(self):
        bit = self.order.pop(0)
        pairs = [(device, device ^ (1 << bit)) for device in range(lax.axis_size("dp"))]
        self.recv = lax.ppermute(self.send, "dp", pairs)
        return self.send

    def finish(self, token):
        recv, self.recv = self.recv, None
        if not self.order:
            self.keep = run_last(self.keep, recv, token)
            return self.keep
        bit = self.order[0]
        spot = self.left.index(bit)
        self.left.remove(bit)
        self.send, self.keep = run_split(self.table, bit, self.keep, recv, 2 ** (len(self.left) - spot), token)
        return self.send


def shards(
    section_input, out_cotangent, series_counts, norm_gains, biases,
    qkv_weight, out_weight, up_weight, down_weight,
):
    sections = lax.axis_size("section")
    section = lax.axis_index("section")
    group = lax.axis_size("dp")
    micro_count, per_micro, width = section_input.shape
    layers = qkv_weight.shape[0]
    hidden = up_weight.shape[2]
    total = micro_count * per_micro
    rows = MICROS * per_micro
    chunks = micro_count // MICROS
    ticks = chunks + 2 * (sections - 1)
    weights = (qkv_weight, out_weight, up_weight, down_weight)
    last_weights = weights
    mask = mask_table()
    counts = jnp.broadcast_to(series_counts.reshape(1, micro_count), (ticks, micro_count))
    tick_ids = jnp.arange(ticks, dtype=jnp.int32)
    core = jnp.broadcast_to(lax.axis_index("dp") & 1, (ticks, 1))

    def table(place):
        chunk = tick_ids - 2 * place
        active = (chunk >= 0) & (chunk < chunks)
        edge = jnp.broadcast_to(place == 0, (ticks,))
        columns = [active, jnp.clip(chunk, 0, chunks - 1), edge]
        columns = [column.astype(jnp.int32)[:, None] for column in columns]
        return jnp.concatenate(columns + [counts, core], axis=1)

    own_bits = (lax.axis_index("dp") >> jnp.arange(group.bit_length() - 1, dtype=jnp.int32)) & 1
    tables = (table(section), table(sections - 1 - section), mask, own_bits)
    forward_meta, backward_meta, mask, bit_table = lax.optimization_barrier(tables)
    entering = section_input.reshape(total, width)
    leaving = out_cotangent.reshape(total, width)
    meta = forward_meta
    arrived = [entering] * 2
    kept = []
    for tick in range(ticks):
        sent, kept, weights = run_forward(
            tick, meta, entering, arrived[tick], mask, norm_gains, biases, weights, kept, rows, per_micro)
        if tick + 2 < ticks:
            arrived.append(hop(sent, 1))
    meta = backward_meta
    arrived = [leaving] * 2
    made = []

    def back(tick, top, count, part, recv, token, made, weights):
        return run_backward(tick, top, count, part, meta, token, leaving, recv, mask, norm_gains, weights, kept, made,
                            rows, per_micro)

    final = ticks - 1
    top = layers - 1
    for tick in range(final):
        sent, made, weights = back(tick, top, layers, 0, arrived[tick], arrived[tick], made, weights)
        if tick + 2 < ticks:
            arrived.append(hop(sent, -1))
    e1, attended, e2, hidden_rows, outputs = kept[1], kept[3], kept[5], kept[7], kept[10]
    top = layers - 1
    bits = group.bit_length() - 1
    near = range(bits)

    def gradient(groups, orders, token, small=None, patch=None):
        dqkv, da, du, df = made[:4]
        table_of = {"qkv": (e1, dqkv), "out": (attended, da), "up": (e2, du), "down": (hidden_rows, df)}
        arrays, jobs, cuts = [], [], []
        for members in groups:
            cuts.append(len(jobs))
            for name, level in members:
                arrays += table_of[name]
                jobs.append((len(arrays) - 2, len(arrays) - 1, level, None))
        if patch is not None:
            jobs[-1] = jobs[-1][:3] + (len(arrays),)
            arrays.append(patch)
        out = run_gradient(tuple(jobs), tuple(cuts), final, meta, token, arrays, group, small)
        return [Piece(*out[2 * spot:2 * spot + 2], order, bit_table) for spot, order in enumerate(orders)]

    token = arrived[final]
    pieces = {}

    def begin(names, groups, **more):
        nonlocal token
        fresh = gradient(groups, [orders[name] for name in names], token, **more)
        for name, piece in zip(names, fresh):
            pieces[name] = piece
            token = piece.start()

    def step(*names):
        nonlocal token
        for name in names:
            token = pieces[name].finish(token)
            if pieces[name].order:
                pieces[name].start()

    far = [0, 2, 1] + list(range(3, bits)) if bits > 3 else list(near)
    orders = [near if turn == "A" else far for turn in TURNS]
    calls = {
        0: ([0], [[("down", top)]]),
        1: ([1], [[("up", top), ("out", top)]]),
        2: ([2, 3], [[("qkv", top)], [("down", 0)]]),
        3: ([4, 5], [[("qkv", 0)], [("up", 0)]]),
        4: ([6], [[("out", 0)]]),
    }
    flow = arrived[final]
    for entry in PLAN.split():
        kind, which = entry[0], int(entry[1:])
        if kind == "b":
            layer, part, now = ((top, 0, weights), (0, 3, last_weights))[which]
            flow, made, _ = back(final, layer, 1, part, flow, token, made, now)
            token = flow
            if which == 1:
                sums, input_grads = made[4:]
                cut = biases.shape[1]
                small = jnp.sum(sums, axis=(0, 2)).astype(BF16)
                small = jnp.concatenate(
                    [small[:, :cut].reshape(layers, group, -1), small[:, cut:].reshape(layers, group, -1)], axis=2)
                used = small.shape[2]
                small = jnp.swapaxes(small, 0, 1).reshape(group, layers * used)
                small = jnp.pad(small, ((0, 0), (0, 8 * TILE - layers * used))).reshape(group // 2, 2, 8, TILE)
        elif kind == "g":
            more = {2: {"patch": flow}, 4: {"small": small} if which == 4 else {}}.get(which, {})
            begin(*calls[which], **more)
        else:
            step(which)
    for piece in pieces.values():
        while piece.order or piece.recv is not None:
            token = piece.finish(token)
            if piece.order:
                piece.start()

    def unpack(packed, at, deep, wide):
        block = deep // group
        tall = block * (wide // TILE)
        return jnp.swapaxes(packed[at:at + tall].reshape(wide // TILE, block, TILE), 0, 1).reshape(block, wide)

    up_rows, out_rows = width // group * (hidden // TILE), width // group
    got = {name: piece.keep for name, piece in pieces.items()}
    grad_down = [unpack(got[3], 0, hidden, width), unpack(got[0], 0, hidden, width)]
    grad_up = [unpack(got[5], 0, width, hidden), unpack(got[1], 0, width, hidden)]
    grad_out = [unpack(got[6], 0, width, width), unpack(got[1], up_rows, width, width)]
    grad_qkv = [unpack(got[4], 0, width, 3 * width), unpack(got[2], 0, width, 3 * width)]
    small = got[6][out_rows:].reshape(-1)[:layers * used].reshape(layers, used)
    return (
        outputs.reshape(1, micro_count, per_micro, width),
        input_grads.reshape(1, micro_count, per_micro, width),
        small[:, cut // group:],
        small[:, :cut // group],
        jnp.stack(grad_qkv), jnp.stack(grad_out), jnp.stack(grad_up), jnp.stack(grad_down),
    )


def solution(mesh):
    stacked = P("section", None, None)
    return jax.shard_map(
        shards,
        mesh=mesh,
        in_specs=(P(None, "dp", None), P(None, "dp", None), P(None, "dp"),
                  P("section", None), P("section", None), stacked, stacked, stacked, stacked),
        out_specs=(P("section", None, "dp", None), P("section", None, "dp", None),
                   P("section", "dp"), P("section", "dp"),
                   P("section", "dp", None), P("section", "dp", None),
                   P("section", "dp", None), P("section", "dp", None)),
        check_vma=False,
    )
```

```python
import functools

import jax
import jax.numpy as jnp
import numpy as np
from jax import lax
from jax.experimental import pallas as pl
from jax.experimental.pallas import tpu as pltpu
from jax.sharding import PartitionSpec as P

HEADS = 8
HEAD_DIM = 128
SEG = 15
LAYERS_DEV = 2
EPSILON = 1e-05
MICROS = 2
NEGATIVE = -1e30
SCALE = HEAD_DIM ** (-0.5)
GELU_A = 0.7978845608028654
GELU_B = 0.044715
TILE = 1024
STEP = 512
F32 = jnp.float32
BF16 = jnp.bfloat16


def dot_nn(left, right):
    return jnp.dot(left, right, preferred_element_type=F32)


def dot_nt(left, right):
    return lax.dot_general(left, right, (((1,), (1,)), ((), ())), preferred_element_type=F32)


def dot_tn(left, right):
    return lax.dot_general(left, right, (((0,), (0,)), ((), ())), preferred_element_type=F32)


def query_blocks(rows):
    blocks = []
    for base in range(0, rows, 240):
        blocks += [(base, 128, base), (base + 128, 112, base + 112)]
    return blocks


def mask_table():
    tables = []
    for query_start, key_start in ((0, 0), (128, 112)):
        query = query_start + np.arange(128)[:, None]
        key = key_start + np.arange(128)[None, :]
        seen = (query // SEG == key // SEG) & (key <= query)
        tables.append(np.where(seen, 0.0, NEGATIVE))
    return jnp.asarray(np.stack(tables), F32)


def fold_rows(values):
    rows, width = values.shape
    return jnp.sum(values.reshape(rows // 8, 8, width), axis=0)


def live_column(meta, tick, rows, per_micro):
    micros = rows // per_micro
    row = lax.broadcasted_iota(jnp.int32, (rows, 1), 0)
    live = None
    for micro in range(micros):
        count = meta[tick, 3 + meta[tick, 1] * micros + micro]
        inside = (row >= micro * per_micro) & (row < micro * per_micro + count * SEG)
        live = inside if live is None else live | inside
    return live.astype(F32)


def exponent(scores, mask):
    scores = scores + mask
    return jnp.exp((scores - jnp.max(scores, axis=-1, keepdims=True)) * SCALE)


def forward_kernel(
    tick, aliased, rows, block, per_micro, unroll,
    meta, first_in, recv, mask, gains, biases, wqkv, wout, wup, wdown,
    *refs,
):
    (y_ref, n1_o, e1_o, qkv_o, o_o, n2_o, e2_o, u_o, h_o, r1_o, r2_o, made_o) = refs[aliased:aliased + 12]
    fresh = tick == 0
    wq, wo, wu, wd = refs[aliased + 12:aliased + 16]
    (xb, xs, qb, n1_s, e1_s, qkv_s, o_s, n2_s, e2_s, u_s, h_s, r1_s, r2_s,
     wsem, ssem, xsem) = refs[aliased + 16:]
    width = xs.shape[1]
    hidden = wu.shape[2]
    layers = wq.shape[0]

    def weight_pieces(layer):
        pieces = []
        for tile in range(3 * width // TILE):
            cut = pl.ds(tile * TILE, TILE)
            pieces.append((wqkv.at[layer, :, cut], wq.at[layer, :, cut]))
        pieces.append((wout.at[layer], wo.at[layer]))
        for tile in range(hidden // TILE):
            cut = pl.ds(tile * TILE, TILE)
            pieces.append((wup.at[layer, :, cut], wu.at[layer, :, cut]))
        for tile in range(hidden // TILE):
            cut = pl.ds(tile * TILE, TILE)
            pieces.append((wdown.at[layer, cut, :], wd.at[layer, cut, :]))
        return pieces

    def each_weight(act):
        for layer in range(layers):
            for spot, (source, target) in enumerate(weight_pieces(layer)):
                act(pltpu.make_async_copy(source, target, wsem.at[layer, spot]))

    def wait_weight(layer, spot, source, target):
        if fresh:
            pltpu.make_async_copy(source, target, wsem.at[layer, spot]).wait()

    if fresh:
        @pl.when(meta[tick, 0] == 1)
        def _():
            copy = pltpu.make_async_copy(first_in.at[pl.ds(0, rows)], xb, xsem)
            copy.start()
            copy.wait()
            each_weight(lambda copy: copy.start())


        @pl.when(meta[tick, 0] != 1)
        def _():
            each_weight(lambda copy: copy.start())
            each_weight(lambda copy: copy.wait())

    n_qkv = 3 * width // TILE
    n_hid = hidden // TILE
    at_out = n_qkv
    at_up = n_qkv + 1
    at_down = at_up + n_hid

    @pl.when(meta[tick, 0] == 1)
    def _():
        row0 = pl.multiple_of(meta[tick, 1] * rows, 16)

        if not fresh:
            @pl.when(meta[tick, 2] == 1)
            def _():
                copy = pltpu.make_async_copy(first_in.at[pl.ds(row0, rows)], xb, xsem)
                copy.start()
                copy.wait()

            @pl.when(meta[tick, 2] != 1)
            def _():
                copy = pltpu.make_async_copy(recv.at[pl.ds(0, rows)], xb, xsem)
                copy.start()
                copy.wait()

        saves = ((n1_s, n1_o), (e1_s, e1_o), (qkv_s, qkv_o), (o_s, o_o), (n2_s, n2_o), (e2_s, e2_o),
                 (u_s, u_o), (h_s, h_o), (r1_s, r1_o), (r2_s, r2_o))

        def save(layer, spot):
            source, target = saves[spot]
            return pltpu.make_async_copy(
                source.at[layer], target.at[layer, pl.ds(row0, rows)], ssem.at[layer, spot])

        @pl.loop(0, rows // block)
        def _(step):
            cut = pl.ds(pl.multiple_of(step * block, 16), block)
            xs[cut, :] = xb[cut, :].astype(F32)

        def norm(layer, gain, shift, n_s, e_s, r_s):
            @pl.loop(0, rows // block)
            def _(step):
                cut = pl.ds(pl.multiple_of(step * block, 16), block)
                values = xs[cut, :]
                centred = values - jnp.mean(values, axis=-1, keepdims=True)
                inverse = lax.rsqrt(jnp.mean(centred * centred, axis=-1, keepdims=True) + EPSILON)
                normed = centred * inverse
                n_s[layer, cut, :] = normed.astype(BF16)
                e_s[layer, cut, :] = (normed * gain + shift).astype(BF16)
                r_s[layer, cut, :] = jnp.broadcast_to(inverse, (block, 128))

        @pl.loop(0, layers)
        def _(layer):
            norm(layer, gains[pl.ds(layer, 1), :width], biases[pl.ds(layer, 1), :width], n1_s, e1_s, r1_s)
            save(layer, 0).start()
            save(layer, 1).start()
            save(layer, 8).start()
            qb[:, :width] = biases[pl.ds(layer, 1), width:2 * width]
            qb[:, width:2 * width] = jnp.zeros((1, width), F32)
            qb[:, 2 * width:] = biases[pl.ds(layer, 1), 2 * width:3 * width]

            for tile in range(n_qkv):
                cut = pl.ds(tile * TILE, TILE)
                wait_weight(layer, tile, wqkv.at[layer, :, cut], wq.at[layer, :, cut])
                for start in range(tile * TILE, (tile + 1) * TILE, STEP):
                    part = pl.ds(start, STEP)
                    qkv_s[layer, :, part] = (dot_nn(e1_s[layer], wq[layer, :, part]) + qb[:, part]).astype(BF16)

            save(layer, 2).start()

            jobs = [(head * HEAD_DIM, spot % 2, q0, nq, k0) for head in range(HEADS)
                    for spot, (q0, nq, k0) in enumerate(query_blocks(rows))]
            scores = []
            for col, _, q0, nq, k0 in jobs:
                query = qkv_s[layer, q0:q0 + nq, col:col + HEAD_DIM]
                key = qkv_s[layer, k0:k0 + 128, width + col:width + col + HEAD_DIM]
                scores.append(dot_nt(query, key))
            soft = []
            for (_, kind, _, nq, _), score in zip(jobs, scores):
                raised = exponent(score, mask[kind, :nq, :])
                soft.append((raised * (1.0 / jnp.sum(raised, axis=-1, keepdims=True))).astype(BF16))
            for (col, _, q0, nq, k0), share in zip(jobs, soft):
                value = qkv_s[layer, k0:k0 + 128, 2 * width + col:2 * width + col + HEAD_DIM]
                o_s[layer, q0:q0 + nq, col:col + HEAD_DIM] = dot_nn(share, value).astype(BF16)

            save(layer, 3).start()
            wait_weight(layer, at_out, wout.at[layer], wo.at[layer])
            for start in range(0, width, STEP):
                part = pl.ds(start, STEP)
                xs[:, part] += dot_nn(o_s[layer], wo[layer, :, part]) + biases[pl.ds(layer, 1), pl.ds(3 * width + start, STEP)]
            norm(layer, gains[pl.ds(layer, 1), width:], biases[pl.ds(layer, 1), 4 * width:5 * width], n2_s, e2_s, r2_s)
            save(layer, 4).start()
            save(layer, 5).start()
            save(layer, 9).start()

            for tile in range(n_hid):
                cut = pl.ds(tile * TILE, TILE)
                wait_weight(layer, at_up + tile, wup.at[layer, :, cut], wu.at[layer, :, cut])
                for start in range(tile * TILE, (tile + 1) * TILE, STEP):
                    part = pl.ds(start, STEP)
                    pre = dot_nn(e2_s[layer], wu[layer, :, part]) + biases[pl.ds(layer, 1), pl.ds(6 * width + start, STEP)]
                    u_s[layer, :, part] = pre.astype(BF16)
                    half = 0.5 * pre
                    turned = jnp.tanh(pre * (GELU_A + (GELU_A * GELU_B) * (pre * pre)))
                    h_s[layer, :, part] = (half + half * turned).astype(BF16)

            save(layer, 6).start()
            save(layer, 7).start()
            for tile in range(n_hid):
                cut = pl.ds(tile * TILE, TILE)
                wait_weight(layer, at_down + tile, wdown.at[layer, cut, :], wd.at[layer, cut, :])
            for start in range(0, width, STEP):
                part = pl.ds(start, STEP)
                xs[:, part] += dot_nn(h_s[layer], wd[layer, :, part]) + biases[pl.ds(layer, 1), pl.ds(5 * width + start, STEP)]

        y_ref[...] = (xs[...] * live_column(meta, tick, rows, per_micro)).astype(BF16)
        made = pltpu.make_async_copy(y_ref, made_o.at[pl.ds(row0, rows)], xsem)
        made.start()
        for layer in range(layers):
            for spot in range(len(saves)):
                save(layer, spot).wait()
        made.wait()


def backward_kernel(
    tick, top, count, part, aliased, rows, block, per_micro, unroll,
    meta, token, last_in, recv, mask, gains, wqkv, wout, wup, wdown,
    n1_i, qkv_i, n2_i, u_i, r1_i, r2_i,
    *refs,
):
    (gx_ref, dqkv_o, da_o, du_o, df_o, sums_o, made_o) = refs[aliased:aliased + 7]
    loaded = part == 3
    wq, wo, wu, wd = refs[-4:] if loaded else refs[aliased + 7:aliased + 11]
    (gb, gs, de_s, do_s, n1_s, qkv_s, n2_s, u_s, r1_s, r2_s,
     dqkv_s, da_s, du_s, df_s, sums_s, lsem, ssem, xsem) = (
         refs[aliased + 7:-5] if loaded else refs[aliased + 11:])
    width = gs.shape[1]
    hidden = wu.shape[2]
    lower, upper = part != 1, part != 2
    first, last = top + 1 == wqkv.shape[0] and upper, top + 1 == count and lower

    def weight(spot):
        pair = ((wdown, wd), (wup, wu), (wout, wo), (wqkv, wq))[spot]
        return pltpu.make_async_copy(pair[0].at[top], pair[1].at[0], refs[-5].at[spot])

    def weight_here(spot):
        if loaded:
            weight(spot).wait()
    HALF = 1024

    @pl.when(meta[tick, 0] == 1)
    def _():
        row0 = pl.multiple_of(meta[tick, 1] * rows, 16)

        if first:
            @pl.when(meta[tick, 2] == 1)
            def _():
                copy = pltpu.make_async_copy(last_in.at[pl.ds(row0, rows)], gb, xsem)
                copy.start()
                copy.wait()

            @pl.when(meta[tick, 2] != 1)
            def _():
                copy = pltpu.make_async_copy(recv.at[pl.ds(0, rows)], gb, xsem)
                copy.start()
                copy.wait()

            gs[...] = gb[...].astype(F32) * live_column(meta, tick, rows, per_micro)
        else:
            copy = pltpu.make_async_copy(recv, gs, xsem)
            copy.start()
            copy.wait()

        loads = ((u_i, u_s), (n2_i, n2_s), (r2_i, r2_s), (qkv_i, qkv_s), (n1_i, n1_s), (r1_i, r1_s))

        def load(layer, spot):
            source, target = loads[spot]
            return pltpu.make_async_copy(
                source.at[layer, pl.ds(row0, rows)], target.at[layer], lsem.at[layer, spot])

        saves = ((df_s, df_o), (du_s, du_o), (da_s, da_o), (dqkv_s, dqkv_o))
        spots = (range(3) if upper else ()), (range(3, 4) if lower else ())
        spots = [spot for group in spots for spot in group]
        spans = ([(3 * width, 6 * width + hidden), (7 * width + hidden, 8 * width + hidden)] if upper else []) + (
            [(0, 3 * width), (6 * width + hidden, 7 * width + hidden)] if lower else [])

        def save(layer, spot):
            source, target = saves[spot]
            return pltpu.make_async_copy(
                source.at[layer], target.at[layer, pl.ds(row0, rows)], ssem.at[layer, spot])

        def save_sums(layer):
            return [pltpu.make_async_copy(
                sums_s.at[layer, :, low:high], sums_o.at[meta[tick, 1], layer, :, low:high], ssem.at[layer, 4 + spot])
                for spot, (low, high) in enumerate(spans)]

        def begin_loads(spots, weights):
            for layer in range(top, top - count, -1):
                for spot in spots:
                    load(layer, spot).start()
            if loaded:
                for spot in weights:
                    weight(spot).start()

        begin_loads((0,) if loaded else range(6), (0,))

        sums_s[...] = jnp.zeros(sums_s.shape, F32)

        def add_sum(layer, start, size, values):
            sums_s[layer, :, pl.ds(start, size)] += fold_rows(values)

        def norm_back(layer, gain, n_s, r_s, shift_at, gain_at, narrow):
            @pl.loop(0, rows // block)
            def _(step):
                cut = pl.ds(pl.multiple_of(step * block, 16), block)
                grad = de_s[cut, :]
                normed = n_s[layer, cut, :].astype(F32)
                scaled = grad * gain
                along = grad * normed
                first = jnp.mean(scaled, axis=-1, keepdims=True)
                second = jnp.mean(along * gain, axis=-1, keepdims=True)
                inverse = r_s[layer, cut, :1]
                fresh = gs[cut, :] + inverse * (scaled - first - normed * second)
                gs[cut, :] = fresh
                add_sum(layer, shift_at, width, grad)
                add_sum(layer, gain_at, width, along)
                if narrow is not None:
                    rounded = fresh.astype(BF16)
                    narrow[layer, cut, :] = rounded
                    add_sum(layer, 3 * width, width, rounded.astype(F32))

        @pl.loop(0, count)
        def _(turn):
            layer = top - turn

            shelf = 0 if loaded else layer
            if upper:
                @pl.loop(0, rows // block)
                def _(step):
                    cut = pl.ds(pl.multiple_of(step * block, 16), block)
                    rounded = gs[cut, :].astype(BF16)
                    df_s[layer, cut, :] = rounded
                    add_sum(layer, 5 * width, width, rounded.astype(F32))

                save(layer, 0).start()
                load(layer, 0).wait()
                weight_here(0)
                if loaded:
                    begin_loads((1, 2), (1,))

                @pl.loop(0, hidden // HALF)
                def _(tile):
                    cut = pl.ds(pl.multiple_of(tile * HALF, HALF), HALF)
                    back = dot_nt(df_s[layer], wd[shelf, cut, :]).astype(BF16).astype(F32)
                    pre = u_s[layer, :, cut].astype(F32)
                    square = pre * pre
                    turned = jnp.tanh(GELU_A * pre * (1.0 + GELU_B * square))
                    slope = 0.5 * (1.0 + turned) + (0.5 * GELU_A) * pre * (1.0 - turned * turned) * (
                        1.0 + (3.0 * GELU_B) * square)
                    rounded = (back * slope).astype(BF16)
                    du_s[layer, :, cut] = rounded
                    add_sum(layer, pl.multiple_of(6 * width + tile * HALF, HALF), HALF, rounded.astype(F32))

                save(layer, 1).start()
                weight_here(1)
                if loaded:
                    begin_loads((3, 4, 5), (2, 3))

                @pl.loop(0, width // HALF)
                def _(tile):
                    cut = pl.ds(pl.multiple_of(tile * HALF, HALF), HALF)
                    de_s[:, cut] = dot_nt(du_s[layer], wu[shelf, cut, :])

                load(layer, 1).wait()
                load(layer, 2).wait()
                norm_back(layer, gains[pl.ds(layer, 1), width:], n2_s, r2_s, 4 * width, 9 * width, da_s)
                save(layer, 2).start()
            if lower:
                if not upper:
                    da_s[layer] = gs[...].astype(BF16)
                weight_here(2)
                do_s[...] = dot_nt(da_s[layer], wo[shelf]).astype(BF16)
                load(layer, 3).wait()

                @pl.loop(0, HEADS // unroll)
                def _(group):
                    jobs = []
                    for inner in range(unroll):
                        col = pl.multiple_of((group * unroll + inner) * HEAD_DIM, HEAD_DIM)
                        cuts = (pl.ds(col, HEAD_DIM), pl.ds(width + col, HEAD_DIM), pl.ds(2 * width + col, HEAD_DIM))
                        jobs += [(cuts, spot % 2, q0, nq, k0) for spot, (q0, nq, k0) in enumerate(query_blocks(rows))]
                    first = []
                    for cuts, _, q0, nq, k0 in jobs:
                        query = qkv_s[layer, q0:q0 + nq, cuts[0]]
                        key = qkv_s[layer, k0:k0 + 128, cuts[1]]
                        value = qkv_s[layer, k0:k0 + 128, cuts[2]]
                        grad = do_s[q0:q0 + nq, cuts[0]]
                        first.append((dot_nt(query, key), dot_nt(grad, value)))
                    second = []
                    for (_, kind, _, nq, _), (score, soft_grad) in zip(jobs, first):
                        raised = exponent(score, mask[kind, :nq, :])
                        soft = raised * (1.0 / jnp.sum(raised, axis=-1, keepdims=True))
                        inner_sum = jnp.sum(soft_grad * soft, axis=-1, keepdims=True)
                        second.append((soft.astype(BF16), (soft * (soft_grad - inner_sum)).astype(BF16)))
                    tail_k = tail_v = None
                    for (cuts, kind, q0, nq, k0), (soft, score_grad) in zip(jobs, second):
                        query = qkv_s[layer, q0:q0 + nq, cuts[0]]
                        key = qkv_s[layer, k0:k0 + 128, cuts[1]]
                        grad = do_s[q0:q0 + nq, cuts[0]]
                        dqkv_s[layer, q0:q0 + nq, cuts[0]] = (dot_nn(score_grad, key) * SCALE).astype(BF16)
                        dk = dot_tn(score_grad, query) * SCALE
                        dv = dot_tn(soft, grad)
                        if kind == 0:
                            tail_k, tail_v = dk[112:], dv[112:]
                            high = 112
                            dk, dv = dk[:112], dv[:112]
                        else:
                            high = 128
                            dk = jnp.concatenate([dk[:16] + tail_k, dk[16:]], axis=0)
                            dv = jnp.concatenate([dv[:16] + tail_v, dv[16:]], axis=0)
                        dqkv_s[layer, k0:k0 + high, cuts[1]] = dk.astype(BF16)
                        dqkv_s[layer, k0:k0 + high, cuts[2]] = dv.astype(BF16)

                sums_s[layer, :, width:2 * width] = fold_rows(dqkv_s[layer, :, :width].astype(F32))
                sums_s[layer, :, 2 * width:3 * width] = fold_rows(dqkv_s[layer, :, 2 * width:].astype(F32))
                save(layer, 3).start()
                weight_here(3)

                @pl.loop(0, width // HALF)
                def _(tile):
                    cut = pl.ds(pl.multiple_of(tile * HALF, HALF), HALF)
                    de_s[:, cut] = dot_nt(dqkv_s[layer], wq[shelf, cut, :])

                load(layer, 4).wait()
                load(layer, 5).wait()
                norm_back(layer, gains[pl.ds(layer, 1), :width], n1_s, r1_s, 0, 8 * width, None)
            for copy in save_sums(layer):
                copy.start()

        if last:
            gx_ref[...] = gs[...].astype(BF16)
            made = pltpu.make_async_copy(gx_ref, made_o.at[pl.ds(row0, rows)], xsem)
            made.start()
        else:
            gx_ref[...] = gs[...]
        for layer in range(top, top - count, -1):
            for spot in spots:
                save(layer, spot).wait()
            for copy in save_sums(layer):
                copy.wait()
        if last:
            made.wait()


def gradient_kernel(
    jobs, cuts, grid, tick, extra,
    meta, token, *refs,
):
    count = 2 * len(cuts)
    inputs, outputs, scratch = refs[:extra], refs[extra:extra + count], refs[extra + count:]
    lefts, rights = scratch[:len(jobs)], scratch[len(jobs):2 * len(jobs)]
    res, patch_s, lsem, osem, psem = scratch[2 * len(jobs):2 * len(jobs) + 5]
    mine = meta[0, meta.shape[1] - 1]
    def tiles_of(spot):
        return lefts[spot].shape[1] // TILE, rights[spot].shape[1] // TILE

    def load(spot, which, tile):
        source, target = ((jobs[spot][0], lefts), (jobs[spot][1], rights))[which]
        cut = pl.ds(pl.multiple_of(tile * TILE, TILE), TILE)
        return pltpu.make_async_copy(
            inputs[source].at[jobs[spot][2], :, cut], target[spot].at[:, cut], lsem.at[spot, which, tile])

    for spot in range(len(jobs)):
        for which in range(2):
            for tile in range(tiles_of(spot)[which]):
                load(spot, which, tile).start()
    sends = []
    at = tile = 0
    for spot, (_, _, _, patch) in enumerate(jobs):
        if spot in cuts:
            at = 0
            send_o, keep_o = outputs[2 * cuts.index(spot):2 * cuts.index(spot) + 2]
        tall, broad = tiles_of(spot)
        if patch is not None:
            load(spot, 1, 0).wait()

            @pl.when(meta[tick, 0] == 1)
            def _():
                rows = patch_s.shape[0]
                copy = pltpu.make_async_copy(inputs[patch], patch_s, psem)
                copy.start()
                copy.wait()
                values = patch_s[...].astype(F32)
                if patch_s.dtype == BF16:
                    values = values * live_column(meta, tick, rows, rows // MICROS)
                cut = pl.ds(pl.multiple_of(meta[tick, 1] * rows, 16), rows)
                rights[spot][cut, :] = values.astype(BF16)

        deep = lefts[spot].shape[1]
        block = deep // grid
        pairs = TILE // (2 * block)

        def send(step, which, send_o=send_o, keep_o=keep_o, at=at, tile=tile):
            output, half = ((send_o, 1 - mine), (keep_o, mine))[which]
            row, col = (step, 0) if tall > 1 else (0, step)
            view = res.at[tile + step].reshape(pairs, 2, block, TILE)
            return pltpu.make_async_copy(
                view.at[:, half], output.at[pl.ds(row * pairs, pairs), pl.ds(at + col * block, block), :],
                osem.at[tile + step, which])

        @pl.loop(0, max(tall, broad))
        def _(step):
            row, col = (step, 0) if tall > 1 else (0, step)
            if tall > 1:
                load(spot, 0, step).wait()
            else:
                @pl.when(step == 0)
                def _():
                    load(spot, 0, 0).wait()

                if patch is None:
                    load(spot, 1, step).wait()
            if tall > 1 and patch is None:
                @pl.when(step == 0)
                def _():
                    load(spot, 1, 0).wait()

            rows_cut = pl.ds(pl.multiple_of(row * TILE, TILE), TILE)
            cols_cut = pl.ds(pl.multiple_of(col * TILE, TILE), TILE)
            res[tile + step] = dot_tn(lefts[spot][:, rows_cut], rights[spot][:, cols_cut]).astype(BF16)
            for which in range(2):
                send(step, which).start()

        for step in range(max(tall, broad)):
            for which in range(2):
                sends.append(send(step, which))
        tile += max(tall, broad)
        at += block * broad
    if send_o.shape[1] > at:
        small_s = scratch[-1]
        copy = pltpu.make_async_copy(inputs[extra - 1], small_s, psem)
        copy.start()
        copy.wait()
        for which, (output, half) in enumerate(((send_o, 1 - mine), (keep_o, mine))):
            copy = pltpu.make_async_copy(small_s.at[:, half], output.at[:, at:, :], osem.at[tile, which])
            copy.start()
            sends.append(copy)
    for copy in sends:
        copy.wait()


HBM = pl.BlockSpec(memory_space=pltpu.HBM)
FREE = pl.BlockSpec(memory_space=pl.ANY)
VMEM = pl.BlockSpec(memory_space=pltpu.VMEM)
SMEM = pl.BlockSpec(memory_space=pltpu.SMEM)
LIMIT = 26 << 20
LAST_LIMIT = 56 << 20
NO_COST = pl.CostEstimate(flops=int(2e11), bytes_accessed=int(5e8), transcendentals=0)


def forward_shapes(layers, total, width, hidden):
    sizes = (width, width, 3 * width, width, width, width, hidden, hidden)
    shapes = [((layers, total, size), BF16) for size in sizes]
    shapes += [((layers, total, 128), F32)] * 2
    shapes.append(((total, width), BF16))
    return shapes


def backward_shapes(layers, total, width, hidden, chunks):
    shapes = [((layers, total, size), BF16) for size in (3 * width, width, hidden, width)]
    shapes.append(((chunks, layers, 8, 8 * width + hidden), F32))
    shapes.append(((total, width), BF16))
    return shapes


def run_forward(tick, meta, first_in, recv, mask, gains, biases, weights, kept, rows, per_micro, block=240, unroll=2):
    wqkv, wout, wup, wdown = weights
    layers, width = wqkv.shape[0], wqkv.shape[1]
    hidden = wup.shape[2]
    sizes = (width, width, 3 * width, width, width, width, hidden, hidden)
    pieces = 3 * width // TILE + 1 + 2 * (hidden // TILE)
    fresh = tick == 0
    scratch = [pltpu.VMEM((rows, width), BF16), pltpu.VMEM((rows, width), F32), pltpu.VMEM((1, 3 * width), F32)]
    scratch += [pltpu.VMEM((layers, rows, size), BF16) for size in sizes]
    scratch += [pltpu.VMEM((layers, rows, 128), F32)] * 2
    scratch += [pltpu.SemaphoreType.DMA((layers, pieces)), pltpu.SemaphoreType.DMA((layers, 10)), pltpu.SemaphoreType.DMA]
    flops = 2 * rows * (wqkv.size + wout.size + wup.size + wdown.size)
    moved = 2 * (wqkv.size + wout.size + wup.size + wdown.size) + 2 * layers * rows * sum(sizes)
    total = first_in.shape[0]
    shapes = [jax.ShapeDtypeStruct(*k) for k in forward_shapes(layers, total, width, hidden)]
    out = pl.pallas_call(
        functools.partial(forward_kernel, tick, len(kept), rows, block, per_micro, unroll),
        out_shape=[jax.ShapeDtypeStruct((rows, width), BF16)] + shapes + [pltpu.VMEM(w.shape, BF16) for w in weights],
        in_specs=[SMEM, HBM, FREE, VMEM, VMEM, VMEM] + [HBM if fresh else VMEM] * 4 + [HBM] * len(kept),
        out_specs=[VMEM] + [HBM] * 11 + [VMEM] * 4,
        scratch_shapes=scratch,
        input_output_aliases={10 + i: 1 + i for i in range(len(kept))} | ({} if fresh else {6 + i: 12 + i for i in range(4)}),
        compiler_params=pltpu.CompilerParams(vmem_limit_bytes=LIMIT),
        cost_estimate=pl.CostEstimate(flops=flops, bytes_accessed=moved, transcendentals=0),
        name="section_forward",
    )(meta, first_in, recv, mask, gains, biases, *weights, *kept)
    return out[0], list(out[1:12]), list(out[12:])


def run_backward(tick, top, count, part, meta, token, last_in, recv, mask, gains, weights, kept, made, rows, per_micro,
                 block=240, unroll=8):
    wqkv, wout, wup, wdown = weights
    layers, width = wqkv.shape[0], wqkv.shape[1]
    hidden = wup.shape[2]
    n1, _, qkv, _, n2, _, u, _, r1, r2, _ = kept
    scratch = [pltpu.VMEM((rows, width), BF16), pltpu.VMEM((rows, width), F32), pltpu.VMEM((rows, width), F32),
               pltpu.VMEM((rows, width), BF16)]
    scratch += [pltpu.VMEM((layers, rows, size), BF16) for size in (width, 3 * width, width, hidden)]
    scratch += [pltpu.VMEM((layers, rows, 128), F32)] * 2
    scratch += [pltpu.VMEM((layers, rows, size), BF16) for size in (3 * width, width, hidden, width)]
    scratch += [pltpu.VMEM((layers, 8, 8 * width + hidden), F32)]
    scratch += [pltpu.SemaphoreType.DMA((layers, 6)), pltpu.SemaphoreType.DMA((layers, 8)), pltpu.SemaphoreType.DMA]
    loaded = part == 3
    if loaded:
        scratch.append(pltpu.SemaphoreType.DMA((4,)))
        scratch += [pltpu.VMEM((1,) + w.shape[1:], BF16) for w in weights]
    total = (wqkv.size + wout.size + wup.size + wdown.size) * count // layers
    shapes = [jax.ShapeDtypeStruct(*k) for k in backward_shapes(
        layers, last_in.shape[0], width, hidden, last_in.shape[0] // rows)]
    out = pl.pallas_call(
        functools.partial(backward_kernel, tick, top, count, part, len(made), rows, block, per_micro, unroll),
        out_shape=[jax.ShapeDtypeStruct((rows, width), BF16 if count == top + 1 and part != 1 else F32)] + shapes
        + ([] if loaded else [pltpu.VMEM(w.shape, BF16) for w in weights]),
        in_specs=[SMEM, FREE, HBM, FREE, VMEM, VMEM] + [HBM if loaded else VMEM] * 4 + [HBM] * 6 + [HBM] * len(made),
        out_specs=[VMEM] + [HBM] * 6 + ([] if loaded else [VMEM] * 4),
        scratch_shapes=scratch,
        input_output_aliases={16 + i: 1 + i for i in range(len(made))} | (
            {} if loaded else {6 + i: 7 + i for i in range(4)}),
        compiler_params=pltpu.CompilerParams(vmem_limit_bytes=LAST_LIMIT if loaded else LIMIT),
        cost_estimate=NO_COST,
        name="section_backward",
    )(meta, token, last_in, recv, mask, gains, *weights, n1, qkv, n2, u, r1, r2, *made)
    return out[0], list(out[1:7]), weights if loaded else list(out[7:])


def run_gradient(jobs, cuts, tick, meta, token, arrays, grid, small=None):
    rows = arrays[jobs[0][0]].shape[1]
    inputs = list(arrays) + ([] if small is None else [small])
    heights = []
    for spot, (left, right, _, _) in enumerate(jobs):
        if spot in cuts:
            heights.append(0)
        heights[-1] += arrays[left].shape[2] // grid * (arrays[right].shape[2] // TILE)
    tiles = sum(arrays[left].shape[2] * arrays[right].shape[2] // TILE ** 2 for left, right, _, _ in jobs)
    flops = 2 * rows * tiles * TILE ** 2
    if small is not None:
        heights[-1] += small.shape[2]
    width = arrays[jobs[0][1]].shape[2]
    patch = next((inputs[job[3]] for job in jobs if job[3] is not None), jax.ShapeDtypeStruct((16, 128), BF16))
    scratch = [pltpu.VMEM(arrays[left].shape[1:], BF16) for left, _, _, _ in jobs]
    scratch += [pltpu.VMEM(arrays[right].shape[1:], BF16) for _, right, _, _ in jobs]
    scratch += [pltpu.VMEM((tiles, TILE, TILE), BF16), pltpu.VMEM(patch.shape, patch.dtype),
                pltpu.SemaphoreType.DMA((len(jobs), 2, 4)), pltpu.SemaphoreType.DMA((tiles + 1, 2)), pltpu.SemaphoreType.DMA]
    if small is not None:
        scratch.append(pltpu.VMEM(small.shape, small.dtype))
    shapes = [jax.ShapeDtypeStruct((grid // 2, height, TILE), BF16) for height in heights for _ in range(2)]
    return pl.pallas_call(
        functools.partial(gradient_kernel, jobs, cuts, grid, tick, len(inputs)),
        out_shape=shapes,
        in_specs=[SMEM, FREE] + [HBM] * len(inputs),
        out_specs=[HBM] * len(shapes),
        scratch_shapes=scratch,
        compiler_params=pltpu.CompilerParams(vmem_limit_bytes=LAST_LIMIT),
        cost_estimate=NO_COST,
        name="weight_gradient",
    )(meta, token, *inputs)


def split_kernel(bit, inner, table, keep, recv, token, send_o, keep_o, keep_s, recv_s, sems):
    blocks = keep.shape[0]
    mine = table[bit]

    def loads(spot):
        half, place = spot // (blocks // 2), spot % (blocks // 2)
        pick = 1 - mine if half == 0 else mine
        source = (place // inner * 2 + pick) * inner + place % inner
        return [pltpu.make_async_copy(origin.at[source], target.at[spot], sems.at[which, spot])
                for which, (origin, target) in enumerate(((keep, keep_s), (recv, recv_s)))]

    def store(spot):
        output = send_o if spot < blocks // 2 else keep_o
        return pltpu.make_async_copy(keep_s.at[spot], output.at[spot % (blocks // 2)], sems.at[2, spot])

    for spot in range(blocks):
        for copy in loads(spot):
            copy.start()
    for spot in range(blocks):
        for copy in loads(spot):
            copy.wait()
        keep_s[spot] = (keep_s[spot].astype(F32) + recv_s[spot].astype(F32)).astype(BF16)
        store(spot).start()
    for spot in range(blocks):
        store(spot).wait()


def run_split(table, bit, keep, recv, inner, token):
    blocks, height, width = keep.shape
    shape = jax.ShapeDtypeStruct((blocks // 2, height, width), BF16)
    return pl.pallas_call(
        functools.partial(split_kernel, bit, inner),
        out_shape=[shape, shape],
        in_specs=[SMEM, HBM, HBM, FREE],
        out_specs=[HBM, HBM],
        scratch_shapes=[pltpu.VMEM(keep.shape, BF16), pltpu.VMEM(keep.shape, BF16),
                        pltpu.SemaphoreType.DMA((3, blocks))],
        compiler_params=pltpu.CompilerParams(vmem_limit_bytes=LAST_LIMIT),
        cost_estimate=NO_COST,
        name="split_sum",
    )(table, keep, recv, token)


def last_kernel(keep, recv, token, out):
    out[...] = keep[...].astype(F32) + recv[...].astype(F32)


def run_last(keep, recv, token):
    _, height, width = keep.shape
    tall = height // 2 if height % 32 == 0 else height
    spec = pl.BlockSpec((None, tall, width), lambda j: (0, j, 0))
    return pl.pallas_call(
        last_kernel,
        out_shape=jax.ShapeDtypeStruct((height, width), F32),
        grid=(height // tall,),
        in_specs=[spec, spec, FREE],
        out_specs=pl.BlockSpec((tall, width), lambda j: (j, 0)),
        compiler_params=pltpu.CompilerParams(vmem_limit_bytes=LAST_LIMIT),
        cost_estimate=NO_COST,
        name="last_sum",
    )(keep, recv, token)


PLAN = (
    "b0", "g0", "g2", "s0", "g1", "s3", "s2", "s1", "b1", "s0", "g3", "s3", "s0", "s2", "s5", "s1", "s4",
    "s3", "s0", "s2", "g4", "s1", "s5", "s3", "s4", "s2", "s6", "s5", "s1", "s4", "s6", "s5", "s6", "s4",
    "s6",
)
TURNS = "AABAABA"


def hop(value, steps):
    count = lax.axis_size("section")
    pairs = [(s, s + steps) for s in range(count) if 0 <= s + steps < count]
    return lax.ppermute(value, "section", pairs) if pairs else jnp.zeros_like(value)


class Piece:
    def __init__(self, send, keep, order, table):
        self.table = table
        self.bits = lax.axis_size("dp").bit_length() - 1
        self.left = list(reversed(range(1, self.bits)))
        self.order = list(order)
        self.send, self.keep = send, keep
        self.recv = None

    def start(self):
        bit = self.order.pop(0)
        pairs = [(device, device ^ (1 << bit)) for device in range(lax.axis_size("dp"))]
        self.recv = lax.ppermute(self.send, "dp", pairs)
        return self.send

    def finish(self, token):
        recv, self.recv = self.recv, None
        if not self.order:
            self.keep = run_last(self.keep, recv, token)
            return self.keep
        bit = self.order[0]
        spot = self.left.index(bit)
        self.left.remove(bit)
        self.send, self.keep = run_split(self.table, bit, self.keep, recv, 2 ** (len(self.left) - spot), token)
        return self.send


def shards(
    section_input, out_cotangent, series_counts, norm_gains, biases,
    qkv_weight, out_weight, up_weight, down_weight,
):
    sections = lax.axis_size("section")
    section = lax.axis_index("section")
    group = lax.axis_size("dp")
    micro_count, per_micro, width = section_input.shape
    layers = qkv_weight.shape[0]
    hidden = up_weight.shape[2]
    total = micro_count * per_micro
    rows = MICROS * per_micro
    chunks = micro_count // MICROS
    ticks = chunks + 2 * (sections - 1)
    weights = (qkv_weight, out_weight, up_weight, down_weight)
    last_weights = weights
    mask = mask_table()
    counts = jnp.broadcast_to(series_counts.reshape(1, micro_count), (ticks, micro_count))
    tick_ids = jnp.arange(ticks, dtype=jnp.int32)
    core = jnp.broadcast_to(lax.axis_index("dp") & 1, (ticks, 1))

    def table(place):
        chunk = tick_ids - 2 * place
        active = (chunk >= 0) & (chunk < chunks)
        edge = jnp.broadcast_to(place == 0, (ticks,))
        columns = [active, jnp.clip(chunk, 0, chunks - 1), edge]
        columns = [column.astype(jnp.int32)[:, None] for column in columns]
        return jnp.concatenate(columns + [counts, core], axis=1)

    own_bits = (lax.axis_index("dp") >> jnp.arange(group.bit_length() - 1, dtype=jnp.int32)) & 1
    tables = (table(section), table(sections - 1 - section), mask, own_bits)
    forward_meta, backward_meta, mask, bit_table = lax.optimization_barrier(tables)
    entering = section_input.reshape(total, width)
    leaving = out_cotangent.reshape(total, width)
    meta = forward_meta
    arrived = [entering] * 2
    kept = []
    for tick in range(ticks):
        sent, kept, weights = run_forward(
            tick, meta, entering, arrived[tick], mask, norm_gains, biases, weights, kept, rows, per_micro)
        if tick + 2 < ticks:
            arrived.append(hop(sent, 1))
    meta = backward_meta
    arrived = [leaving] * 2
    made = []

    def back(tick, top, count, part, recv, token, made, weights):
        return run_backward(tick, top, count, part, meta, token, leaving, recv, mask, norm_gains, weights, kept, made,
                            rows, per_micro)

    final = ticks - 1
    top = layers - 1
    for tick in range(final):
        sent, made, weights = back(tick, top, layers, 0, arrived[tick], arrived[tick], made, weights)
        if tick + 2 < ticks:
            arrived.append(hop(sent, -1))
    e1, attended, e2, hidden_rows, outputs = kept[1], kept[3], kept[5], kept[7], kept[10]
    top = layers - 1
    bits = group.bit_length() - 1
    near = range(bits)

    def gradient(groups, orders, token, small=None, patch=None):
        dqkv, da, du, df = made[:4]
        table_of = {"qkv": (e1, dqkv), "out": (attended, da), "up": (e2, du), "down": (hidden_rows, df)}
        arrays, jobs, cuts = [], [], []
        for members in groups:
            cuts.append(len(jobs))
            for name, level in members:
                arrays += table_of[name]
                jobs.append((len(arrays) - 2, len(arrays) - 1, level, None))
        if patch is not None:
            jobs[-1] = jobs[-1][:3] + (len(arrays),)
            arrays.append(patch)
        out = run_gradient(tuple(jobs), tuple(cuts), final, meta, token, arrays, group, small)
        return [Piece(*out[2 * spot:2 * spot + 2], order, bit_table) for spot, order in enumerate(orders)]

    token = arrived[final]
    pieces = {}

    def begin(names, groups, **more):
        nonlocal token
        fresh = gradient(groups, [orders[name] for name in names], token, **more)
        for name, piece in zip(names, fresh):
            pieces[name] = piece
            token = piece.start()

    def step(*names):
        nonlocal token
        for name in names:
            token = pieces[name].finish(token)
            if pieces[name].order:
                pieces[name].start()

    far = [0, 2, 1] + list(range(3, bits)) if bits > 3 else list(near)
    orders = [near if turn == "A" else far for turn in TURNS]
    calls = {
        0: ([0], [[("down", top)]]),
        1: ([1], [[("up", top), ("out", top)]]),
        2: ([2, 3], [[("qkv", top)], [("down", 0)]]),
        3: ([4, 5], [[("qkv", 0)], [("up", 0)]]),
        4: ([6], [[("out", 0)]]),
    }
    flow = arrived[final]
    for entry in PLAN:
        kind, which = entry[0], int(entry[1:])
        if kind == "b":
            layer, part, now = ((top, 0, weights), (0, 3, last_weights))[which]
            flow, made, _ = back(final, layer, 1, part, flow, token, made, now)
            token = flow
            if which == 1:
                sums, input_grads = made[4:]
                cut = biases.shape[1]
                small = jnp.sum(sums, axis=(0, 2)).astype(BF16)
                small = jnp.concatenate(
                    [small[:, :cut].reshape(layers, group, -1), small[:, cut:].reshape(layers, group, -1)], axis=2)
                used = small.shape[2]
                small = jnp.swapaxes(small, 0, 1).reshape(group, layers * used)
                small = jnp.pad(small, ((0, 0), (0, 8 * TILE - layers * used))).reshape(group // 2, 2, 8, TILE)
        elif kind == "g":
            more = {2: {"patch": flow}, 4: {"small": small} if which == 4 else {}}.get(which, {})
            begin(*calls[which], **more)
        else:
            step(which)
    for piece in pieces.values():
        while piece.order or piece.recv is not None:
            token = piece.finish(token)
            if piece.order:
                piece.start()

    def unpack(packed, at, deep, wide):
        block = deep // group
        tall = block * (wide // TILE)
        return jnp.swapaxes(packed[at:at + tall].reshape(wide // TILE, block, TILE), 0, 1).reshape(block, wide)

    up_rows, out_rows = width // group * (hidden // TILE), width // group
    got = {name: piece.keep for name, piece in pieces.items()}
    grad_down = [unpack(got[3], 0, hidden, width), unpack(got[0], 0, hidden, width)]
    grad_up = [unpack(got[5], 0, width, hidden), unpack(got[1], 0, width, hidden)]
    grad_out = [unpack(got[6], 0, width, width), unpack(got[1], up_rows, width, width)]
    grad_qkv = [unpack(got[4], 0, width, 3 * width), unpack(got[2], 0, width, 3 * width)]
    small = got[6][out_rows:].reshape(-1)[:layers * used].reshape(layers, used)
    return (
        outputs.reshape(1, micro_count, per_micro, width),
        input_grads.reshape(1, micro_count, per_micro, width),
        small[:, cut // group:],
        small[:, :cut // group],
        jnp.stack(grad_qkv), jnp.stack(grad_out), jnp.stack(grad_up), jnp.stack(grad_down),
    )


def solution(mesh):
    stacked = P("section", None, None)
    return jax.shard_map(
        shards,
        mesh=mesh,
        in_specs=(P(None, "dp", None), P(None, "dp", None), P(None, "dp"),
                  P("section", None), P("section", None), stacked, stacked, stacked, stacked),
        out_specs=(P("section", None, "dp", None), P("section", None, "dp", None),
                   P("section", "dp"), P("section", "dp"),
                   P("section", "dp", None), P("section", "dp", None),
                   P("section", "dp", None), P("section", "dp", None)),
        check_vma=False,
    )
```

```python
import functools

import jax
import jax.numpy as jnp
import numpy as np
from jax import lax
from jax.experimental import pallas as pl
from jax.experimental.pallas import tpu as pltpu
from jax.sharding import PartitionSpec as P

HEADS = 8
HEAD_DIM = 128
SEG = 15
LAYERS_DEV = 2
EPSILON = 1e-05
MICROS = 2
NEGATIVE = -1e30
SCALE = HEAD_DIM ** (-0.5)
GELU_A = 0.7978845608028654
GELU_B = 0.044715
TILE = 1024
STEP = 512
F32 = jnp.float32
BF16 = jnp.bfloat16


def dot_nn(left, right):
    return jnp.dot(left, right, preferred_element_type=F32)


def dot_nt(left, right):
    return lax.dot_general(left, right, (((1,), (1,)), ((), ())), preferred_element_type=F32)


def dot_tn(left, right):
    return lax.dot_general(left, right, (((0,), (0,)), ((), ())), preferred_element_type=F32)


def query_blocks(rows):
    blocks = []
    for base in range(0, rows, 240):
        blocks += [(base, 128, base), (base + 128, 112, base + 112)]
    return blocks


def mask_table():
    tables = []
    for query_start, key_start in ((0, 0), (128, 112)):
        query = query_start + np.arange(128)[:, None]
        key = key_start + np.arange(128)[None, :]
        seen = (query // SEG == key // SEG) & (key <= query)
        tables.append(np.where(seen, 0.0, NEGATIVE))
    return jnp.asarray(np.stack(tables), F32)


def fold_rows(values):
    rows, width = values.shape
    return jnp.sum(values.reshape(rows // 8, 8, width), axis=0)


def live_column(meta, tick, rows, per_micro):
    micros = rows // per_micro
    row = lax.broadcasted_iota(jnp.int32, (rows, 1), 0)
    live = None
    for micro in range(micros):
        count = meta[tick, 3 + meta[tick, 1] * micros + micro]
        inside = (row >= micro * per_micro) & (row < micro * per_micro + count * SEG)
        live = inside if live is None else live | inside
    return live.astype(F32)


def exponent(scores, mask):
    scores = scores + mask
    return jnp.exp((scores - jnp.max(scores, axis=-1, keepdims=True)) * SCALE)


def forward_kernel(
    tick, aliased, rows, block, per_micro, unroll,
    meta, first_in, recv, mask, gains, biases, wqkv, wout, wup, wdown,
    *refs,
):
    (y_ref, n1_o, e1_o, qkv_o, o_o, n2_o, e2_o, u_o, h_o, r1_o, r2_o, made_o) = refs[aliased:aliased + 12]
    fresh = tick == 0
    wq, wo, wu, wd = refs[aliased + 12:aliased + 16]
    (xb, xs, qb, n1_s, e1_s, qkv_s, o_s, n2_s, e2_s, u_s, h_s, r1_s, r2_s,
     wsem, ssem, xsem) = refs[aliased + 16:]
    width = xs.shape[1]
    hidden = wu.shape[2]
    layers = wq.shape[0]

    def weight_pieces(layer):
        pieces = []
        for tile in range(3 * width // TILE):
            cut = pl.ds(tile * TILE, TILE)
            pieces.append((wqkv.at[layer, :, cut], wq.at[layer, :, cut]))
        pieces.append((wout.at[layer], wo.at[layer]))
        for tile in range(hidden // TILE):
            cut = pl.ds(tile * TILE, TILE)
            pieces.append((wup.at[layer, :, cut], wu.at[layer, :, cut]))
        for tile in range(hidden // TILE):
            cut = pl.ds(tile * TILE, TILE)
            pieces.append((wdown.at[layer, cut, :], wd.at[layer, cut, :]))
        return pieces

    def each_weight(act):
        for layer in range(layers):
            for spot, (source, target) in enumerate(weight_pieces(layer)):
                act(pltpu.make_async_copy(source, target, wsem.at[layer, spot]))

    def wait_weight(layer, spot, source, target):
        if fresh:
            pltpu.make_async_copy(source, target, wsem.at[layer, spot]).wait()

    if fresh:
        @pl.when(meta[tick, 0] == 1)
        def _():
            copy = pltpu.make_async_copy(first_in.at[pl.ds(0, rows)], xb, xsem)
            copy.start()
            copy.wait()
            each_weight(lambda copy: copy.start())


        @pl.when(meta[tick, 0] != 1)
        def _():
            each_weight(lambda copy: copy.start())
            each_weight(lambda copy: copy.wait())

    n_qkv = 3 * width // TILE
    n_hid = hidden // TILE
    at_out = n_qkv
    at_up = n_qkv + 1
    at_down = at_up + n_hid

    @pl.when(meta[tick, 0] == 1)
    def _():
        row0 = pl.multiple_of(meta[tick, 1] * rows, 16)

        if not fresh:
            @pl.when(meta[tick, 2] == 1)
            def _():
                copy = pltpu.make_async_copy(first_in.at[pl.ds(row0, rows)], xb, xsem)
                copy.start()
                copy.wait()

            @pl.when(meta[tick, 2] != 1)
            def _():
                copy = pltpu.make_async_copy(recv.at[pl.ds(0, rows)], xb, xsem)
                copy.start()
                copy.wait()

        saves = ((n1_s, n1_o), (e1_s, e1_o), (qkv_s, qkv_o), (o_s, o_o), (n2_s, n2_o), (e2_s, e2_o),
                 (u_s, u_o), (h_s, h_o), (r1_s, r1_o), (r2_s, r2_o))

        def save(layer, spot):
            source, target = saves[spot]
            return pltpu.make_async_copy(
                source.at[layer], target.at[layer, pl.ds(row0, rows)], ssem.at[layer, spot])

        @pl.loop(0, rows // block)
        def _(step):
            cut = pl.ds(pl.multiple_of(step * block, 16), block)
            xs[cut, :] = xb[cut, :].astype(F32)

        def norm(layer, gain, shift, n_s, e_s, r_s):
            @pl.loop(0, rows // block)
            def _(step):
                cut = pl.ds(pl.multiple_of(step * block, 16), block)
                values = xs[cut, :]
                centred = values - jnp.mean(values, axis=-1, keepdims=True)
                inverse = lax.rsqrt(jnp.mean(centred * centred, axis=-1, keepdims=True) + EPSILON)
                normed = centred * inverse
                n_s[layer, cut, :] = normed.astype(BF16)
                e_s[layer, cut, :] = (normed * gain + shift).astype(BF16)
                r_s[layer, cut, :] = jnp.broadcast_to(inverse, (block, 128))

        @pl.loop(0, layers)
        def _(layer):
            norm(layer, gains[pl.ds(layer, 1), :width], biases[pl.ds(layer, 1), :width], n1_s, e1_s, r1_s)
            save(layer, 0).start()
            save(layer, 1).start()
            save(layer, 8).start()
            qb[:, :width] = biases[pl.ds(layer, 1), width:2 * width]
            qb[:, width:2 * width] = jnp.zeros((1, width), F32)
            qb[:, 2 * width:] = biases[pl.ds(layer, 1), 2 * width:3 * width]

            for tile in range(n_qkv):
                cut = pl.ds(tile * TILE, TILE)
                wait_weight(layer, tile, wqkv.at[layer, :, cut], wq.at[layer, :, cut])
                for start in range(tile * TILE, (tile + 1) * TILE, STEP):
                    part = pl.ds(start, STEP)
                    qkv_s[layer, :, part] = (dot_nn(e1_s[layer], wq[layer, :, part]) + qb[:, part]).astype(BF16)

            save(layer, 2).start()

            jobs = [(head * HEAD_DIM, spot % 2, q0, nq, k0) for head in range(HEADS)
                    for spot, (q0, nq, k0) in enumerate(query_blocks(rows))]
            scores = []
            for col, _, q0, nq, k0 in jobs:
                query = qkv_s[layer, q0:q0 + nq, col:col + HEAD_DIM]
                key = qkv_s[layer, k0:k0 + 128, width + col:width + col + HEAD_DIM]
                scores.append(dot_nt(query, key))
            soft = []
            for (_, kind, _, nq, _), score in zip(jobs, scores):
                raised = exponent(score, mask[kind, :nq, :])
                soft.append((raised * (1.0 / jnp.sum(raised, axis=-1, keepdims=True))).astype(BF16))
            for (col, _, q0, nq, k0), share in zip(jobs, soft):
                value = qkv_s[layer, k0:k0 + 128, 2 * width + col:2 * width + col + HEAD_DIM]
                o_s[layer, q0:q0 + nq, col:col + HEAD_DIM] = dot_nn(share, value).astype(BF16)

            save(layer, 3).start()
            wait_weight(layer, at_out, wout.at[layer], wo.at[layer])
            for start in range(0, width, STEP):
                part = pl.ds(start, STEP)
                xs[:, part] += dot_nn(o_s[layer], wo[layer, :, part]) + biases[pl.ds(layer, 1), pl.ds(3 * width + start, STEP)]
            norm(layer, gains[pl.ds(layer, 1), width:], biases[pl.ds(layer, 1), 4 * width:5 * width], n2_s, e2_s, r2_s)
            save(layer, 4).start()
            save(layer, 5).start()
            save(layer, 9).start()

            for tile in range(n_hid):
                cut = pl.ds(tile * TILE, TILE)
                wait_weight(layer, at_up + tile, wup.at[layer, :, cut], wu.at[layer, :, cut])
                for start in range(tile * TILE, (tile + 1) * TILE, STEP):
                    part = pl.ds(start, STEP)
                    pre = dot_nn(e2_s[layer], wu[layer, :, part]) + biases[pl.ds(layer, 1), pl.ds(6 * width + start, STEP)]
                    u_s[layer, :, part] = pre.astype(BF16)
                    half = 0.5 * pre
                    turned = jnp.tanh(pre * (GELU_A + (GELU_A * GELU_B) * (pre * pre)))
                    h_s[layer, :, part] = (half + half * turned).astype(BF16)

            save(layer, 6).start()
            save(layer, 7).start()
            for tile in range(n_hid):
                cut = pl.ds(tile * TILE, TILE)
                wait_weight(layer, at_down + tile, wdown.at[layer, cut, :], wd.at[layer, cut, :])
            for start in range(0, width, STEP):
                part = pl.ds(start, STEP)
                xs[:, part] += dot_nn(h_s[layer], wd[layer, :, part]) + biases[pl.ds(layer, 1), pl.ds(5 * width + start, STEP)]

        y_ref[...] = (xs[...] * live_column(meta, tick, rows, per_micro)).astype(BF16)
        made = pltpu.make_async_copy(y_ref, made_o.at[pl.ds(row0, rows)], xsem)
        made.start()
        for layer in range(layers):
            for spot in range(len(saves)):
                save(layer, spot).wait()
        made.wait()


def backward_kernel(
    tick, top, count, part, aliased, rows, block, per_micro, unroll,
    meta, token, last_in, recv, mask, gains, wqkv, wout, wup, wdown,
    n1_i, qkv_i, n2_i, u_i, r1_i, r2_i,
    *refs,
):
    (gx_ref, dqkv_o, da_o, du_o, df_o, sums_o, made_o) = refs[aliased:aliased + 7]
    loaded = part == 3
    wq, wo, wu, wd = refs[-4:] if loaded else refs[aliased + 7:aliased + 11]
    (gb, gs, de_s, do_s, n1_s, qkv_s, n2_s, u_s, r1_s, r2_s,
     dqkv_s, da_s, du_s, df_s, sums_s, lsem, ssem, xsem) = (
         refs[aliased + 7:-5] if loaded else refs[aliased + 11:])
    width = gs.shape[1]
    hidden = wu.shape[2]
    lower, upper = part != 1, part != 2
    first, last = top + 1 == wqkv.shape[0] and upper, top + 1 == count and lower

    def weight(spot):
        pair = ((wdown, wd), (wup, wu), (wout, wo), (wqkv, wq))[spot]
        return pltpu.make_async_copy(pair[0].at[top], pair[1].at[0], refs[-5].at[spot])

    def weight_here(spot):
        if loaded:
            weight(spot).wait()
    HALF = 1024

    @pl.when(meta[tick, 0] == 1)
    def _():
        row0 = pl.multiple_of(meta[tick, 1] * rows, 16)

        if first:
            @pl.when(meta[tick, 2] == 1)
            def _():
                copy = pltpu.make_async_copy(last_in.at[pl.ds(row0, rows)], gb, xsem)
                copy.start()
                copy.wait()

            @pl.when(meta[tick, 2] != 1)
            def _():
                copy = pltpu.make_async_copy(recv.at[pl.ds(0, rows)], gb, xsem)
                copy.start()
                copy.wait()

            gs[...] = gb[...].astype(F32) * live_column(meta, tick, rows, per_micro)
        else:
            copy = pltpu.make_async_copy(recv, gs, xsem)
            copy.start()
            copy.wait()

        loads = ((u_i, u_s), (n2_i, n2_s), (r2_i, r2_s), (qkv_i, qkv_s), (n1_i, n1_s), (r1_i, r1_s))

        def load(layer, spot):
            source, target = loads[spot]
            return pltpu.make_async_copy(
                source.at[layer, pl.ds(row0, rows)], target.at[layer], lsem.at[layer, spot])

        saves = ((df_s, df_o), (du_s, du_o), (da_s, da_o), (dqkv_s, dqkv_o))
        spots = (range(3) if upper else ()), (range(3, 4) if lower else ())
        spots = [spot for group in spots for spot in group]
        spans = ([(3 * width, 6 * width + hidden), (7 * width + hidden, 8 * width + hidden)] if upper else []) + (
            [(0, 3 * width), (6 * width + hidden, 7 * width + hidden)] if lower else [])

        def save(layer, spot):
            source, target = saves[spot]
            return pltpu.make_async_copy(
                source.at[layer], target.at[layer, pl.ds(row0, rows)], ssem.at[layer, spot])

        def save_sums(layer):
            return [pltpu.make_async_copy(
                sums_s.at[layer, :, low:high], sums_o.at[meta[tick, 1], layer, :, low:high], ssem.at[layer, 4 + spot])
                for spot, (low, high) in enumerate(spans)]

        def begin_loads(spots, weights):
            for layer in range(top, top - count, -1):
                for spot in spots:
                    load(layer, spot).start()
            if loaded:
                for spot in weights:
                    weight(spot).start()

        begin_loads((0,) if loaded else range(6), (0,))

        sums_s[...] = jnp.zeros(sums_s.shape, F32)

        def add_sum(layer, start, size, values):
            sums_s[layer, :, pl.ds(start, size)] += fold_rows(values)

        def norm_back(layer, gain, n_s, r_s, shift_at, gain_at, narrow):
            @pl.loop(0, rows // block)
            def _(step):
                cut = pl.ds(pl.multiple_of(step * block, 16), block)
                grad = de_s[cut, :]
                normed = n_s[layer, cut, :].astype(F32)
                scaled = grad * gain
                along = grad * normed
                first = jnp.mean(scaled, axis=-1, keepdims=True)
                second = jnp.mean(along * gain, axis=-1, keepdims=True)
                inverse = r_s[layer, cut, :1]
                fresh = gs[cut, :] + inverse * (scaled - first - normed * second)
                gs[cut, :] = fresh
                add_sum(layer, shift_at, width, grad)
                add_sum(layer, gain_at, width, along)
                if narrow is not None:
                    rounded = fresh.astype(BF16)
                    narrow[layer, cut, :] = rounded
                    add_sum(layer, 3 * width, width, rounded.astype(F32))

        @pl.loop(0, count)
        def _(turn):
            layer = top - turn

            shelf = 0 if loaded else layer
            if upper:
                @pl.loop(0, rows // block)
                def _(step):
                    cut = pl.ds(pl.multiple_of(step * block, 16), block)
                    rounded = gs[cut, :].astype(BF16)
                    df_s[layer, cut, :] = rounded
                    add_sum(layer, 5 * width, width, rounded.astype(F32))

                save(layer, 0).start()
                load(layer, 0).wait()
                weight_here(0)
                if loaded:
                    begin_loads((1, 2), (1,))

                @pl.loop(0, hidden // HALF)
                def _(tile):
                    cut = pl.ds(pl.multiple_of(tile * HALF, HALF), HALF)
                    back = dot_nt(df_s[layer], wd[shelf, cut, :]).astype(BF16).astype(F32)
                    pre = u_s[layer, :, cut].astype(F32)
                    square = pre * pre
                    turned = jnp.tanh(GELU_A * pre * (1.0 + GELU_B * square))
                    slope = 0.5 * (1.0 + turned) + (0.5 * GELU_A) * pre * (1.0 - turned * turned) * (
                        1.0 + (3.0 * GELU_B) * square)
                    rounded = (back * slope).astype(BF16)
                    du_s[layer, :, cut] = rounded
                    add_sum(layer, pl.multiple_of(6 * width + tile * HALF, HALF), HALF, rounded.astype(F32))

                save(layer, 1).start()
                weight_here(1)
                if loaded:
                    begin_loads((3, 4, 5), (2, 3))

                @pl.loop(0, width // HALF)
                def _(tile):
                    cut = pl.ds(pl.multiple_of(tile * HALF, HALF), HALF)
                    de_s[:, cut] = dot_nt(du_s[layer], wu[shelf, cut, :])

                load(layer, 1).wait()
                load(layer, 2).wait()
                norm_back(layer, gains[pl.ds(layer, 1), width:], n2_s, r2_s, 4 * width, 9 * width, da_s)
                save(layer, 2).start()
            if lower:
                if not upper:
                    da_s[layer] = gs[...].astype(BF16)
                weight_here(2)
                do_s[...] = dot_nt(da_s[layer], wo[shelf]).astype(BF16)
                load(layer, 3).wait()

                @pl.loop(0, HEADS // unroll)
                def _(group):
                    jobs = []
                    for inner in range(unroll):
                        col = pl.multiple_of((group * unroll + inner) * HEAD_DIM, HEAD_DIM)
                        cuts = (pl.ds(col, HEAD_DIM), pl.ds(width + col, HEAD_DIM), pl.ds(2 * width + col, HEAD_DIM))
                        jobs += [(cuts, spot % 2, q0, nq, k0) for spot, (q0, nq, k0) in enumerate(query_blocks(rows))]
                    first = []
                    for cuts, _, q0, nq, k0 in jobs:
                        query = qkv_s[layer, q0:q0 + nq, cuts[0]]
                        key = qkv_s[layer, k0:k0 + 128, cuts[1]]
                        value = qkv_s[layer, k0:k0 + 128, cuts[2]]
                        grad = do_s[q0:q0 + nq, cuts[0]]
                        first.append((dot_nt(query, key), dot_nt(grad, value)))
                    second = []
                    for (_, kind, _, nq, _), (score, soft_grad) in zip(jobs, first):
                        raised = exponent(score, mask[kind, :nq, :])
                        soft = raised * (1.0 / jnp.sum(raised, axis=-1, keepdims=True))
                        inner_sum = jnp.sum(soft_grad * soft, axis=-1, keepdims=True)
                        second.append((soft.astype(BF16), (soft * (soft_grad - inner_sum)).astype(BF16)))
                    tail_k = tail_v = None
                    for (cuts, kind, q0, nq, k0), (soft, score_grad) in zip(jobs, second):
                        query = qkv_s[layer, q0:q0 + nq, cuts[0]]
                        key = qkv_s[layer, k0:k0 + 128, cuts[1]]
                        grad = do_s[q0:q0 + nq, cuts[0]]
                        dqkv_s[layer, q0:q0 + nq, cuts[0]] = (dot_nn(score_grad, key) * SCALE).astype(BF16)
                        dk = dot_tn(score_grad, query) * SCALE
                        dv = dot_tn(soft, grad)
                        if kind == 0:
                            tail_k, tail_v = dk[112:], dv[112:]
                            high = 112
                            dk, dv = dk[:112], dv[:112]
                        else:
                            high = 128
                            dk = jnp.concatenate([dk[:16] + tail_k, dk[16:]], axis=0)
                            dv = jnp.concatenate([dv[:16] + tail_v, dv[16:]], axis=0)
                        dqkv_s[layer, k0:k0 + high, cuts[1]] = dk.astype(BF16)
                        dqkv_s[layer, k0:k0 + high, cuts[2]] = dv.astype(BF16)

                sums_s[layer, :, width:2 * width] = fold_rows(dqkv_s[layer, :, :width].astype(F32))
                sums_s[layer, :, 2 * width:3 * width] = fold_rows(dqkv_s[layer, :, 2 * width:].astype(F32))
                save(layer, 3).start()
                weight_here(3)

                @pl.loop(0, width // HALF)
                def _(tile):
                    cut = pl.ds(pl.multiple_of(tile * HALF, HALF), HALF)
                    de_s[:, cut] = dot_nt(dqkv_s[layer], wq[shelf, cut, :])

                load(layer, 4).wait()
                load(layer, 5).wait()
                norm_back(layer, gains[pl.ds(layer, 1), :width], n1_s, r1_s, 0, 8 * width, None)
            for copy in save_sums(layer):
                copy.start()

        if last:
            gx_ref[...] = gs[...].astype(BF16)
            made = pltpu.make_async_copy(gx_ref, made_o.at[pl.ds(row0, rows)], xsem)
            made.start()
        else:
            gx_ref[...] = gs[...]
        for layer in range(top, top - count, -1):
            for spot in spots:
                save(layer, spot).wait()
            for copy in save_sums(layer):
                copy.wait()
        if last:
            made.wait()


def gradient_kernel(
    jobs, cuts, grid, tick, extra,
    meta, token, *refs,
):
    count = 2 * len(cuts)
    inputs, outputs, scratch = refs[:extra], refs[extra:extra + count], refs[extra + count:]
    lefts, rights = scratch[:len(jobs)], scratch[len(jobs):2 * len(jobs)]
    res, patch_s, lsem, osem, psem = scratch[2 * len(jobs):2 * len(jobs) + 5]
    mine = meta[0, meta.shape[1] - 1]
    def tiles_of(spot):
        return lefts[spot].shape[1] // TILE, rights[spot].shape[1] // TILE

    def load(spot, which, tile):
        source, target = ((jobs[spot][0], lefts), (jobs[spot][1], rights))[which]
        cut = pl.ds(pl.multiple_of(tile * TILE, TILE), TILE)
        return pltpu.make_async_copy(
            inputs[source].at[jobs[spot][2], :, cut], target[spot].at[:, cut], lsem.at[spot, which, tile])

    for spot in range(len(jobs)):
        for which in range(2):
            for tile in range(tiles_of(spot)[which]):
                load(spot, which, tile).start()
    sends = []
    at = tile = 0
    for spot, (_, _, _, patch) in enumerate(jobs):
        if spot in cuts:
            at = 0
            send_o, keep_o = outputs[2 * cuts.index(spot):2 * cuts.index(spot) + 2]
        tall, broad = tiles_of(spot)
        if patch is not None:
            load(spot, 1, 0).wait()

            @pl.when(meta[tick, 0] == 1)
            def _():
                rows = patch_s.shape[0]
                copy = pltpu.make_async_copy(inputs[patch], patch_s, psem)
                copy.start()
                copy.wait()
                values = patch_s[...].astype(F32)
                if patch_s.dtype == BF16:
                    values = values * live_column(meta, tick, rows, rows // MICROS)
                cut = pl.ds(pl.multiple_of(meta[tick, 1] * rows, 16), rows)
                rights[spot][cut, :] = values.astype(BF16)

        deep = lefts[spot].shape[1]
        block = deep // grid
        pairs = TILE // (2 * block)

        def send(step, which, send_o=send_o, keep_o=keep_o, at=at, tile=tile):
            output, half = ((send_o, 1 - mine), (keep_o, mine))[which]
            row, col = (step, 0) if tall > 1 else (0, step)
            view = res.at[tile + step].reshape(pairs, 2, block, TILE)
            return pltpu.make_async_copy(
                view.at[:, half], output.at[pl.ds(row * pairs, pairs), pl.ds(at + col * block, block), :],
                osem.at[tile + step, which])

        @pl.loop(0, max(tall, broad))
        def _(step):
            row, col = (step, 0) if tall > 1 else (0, step)
            if tall > 1:
                load(spot, 0, step).wait()
            else:
                @pl.when(step == 0)
                def _():
                    load(spot, 0, 0).wait()

                if patch is None:
                    load(spot, 1, step).wait()
            if tall > 1 and patch is None:
                @pl.when(step == 0)
                def _():
                    load(spot, 1, 0).wait()

            rows_cut = pl.ds(pl.multiple_of(row * TILE, TILE), TILE)
            cols_cut = pl.ds(pl.multiple_of(col * TILE, TILE), TILE)
            res[tile + step] = dot_tn(lefts[spot][:, rows_cut], rights[spot][:, cols_cut]).astype(BF16)
            for which in range(2):
                send(step, which).start()

        for step in range(max(tall, broad)):
            for which in range(2):
                sends.append(send(step, which))
        tile += max(tall, broad)
        at += block * broad
    if send_o.shape[1] > at:
        small_s = scratch[-1]
        copy = pltpu.make_async_copy(inputs[extra - 1], small_s, psem)
        copy.start()
        copy.wait()
        for which, (output, half) in enumerate(((send_o, 1 - mine), (keep_o, mine))):
            copy = pltpu.make_async_copy(small_s.at[:, half], output.at[:, at:, :], osem.at[tile, which])
            copy.start()
            sends.append(copy)
    for copy in sends:
        copy.wait()


HBM = pl.BlockSpec(memory_space=pltpu.HBM)
FREE = pl.BlockSpec(memory_space=pl.ANY)
VMEM = pl.BlockSpec(memory_space=pltpu.VMEM)
SMEM = pl.BlockSpec(memory_space=pltpu.SMEM)
LIMIT = 26 << 20
LAST_LIMIT = 56 << 20
NO_COST = pl.CostEstimate(flops=int(2e11), bytes_accessed=int(5e8), transcendentals=0)


def forward_shapes(layers, total, width, hidden):
    sizes = (width, width, 3 * width, width, width, width, hidden, hidden)
    shapes = [((layers, total, size), BF16) for size in sizes]
    shapes += [((layers, total, 128), F32)] * 2
    shapes.append(((total, width), BF16))
    return shapes


def backward_shapes(layers, total, width, hidden, chunks):
    shapes = [((layers, total, size), BF16) for size in (3 * width, width, hidden, width)]
    shapes.append(((chunks, layers, 8, 8 * width + hidden), F32))
    shapes.append(((total, width), BF16))
    return shapes


def run_forward(tick, meta, first_in, recv, mask, gains, biases, weights, kept, rows, per_micro, block=240, unroll=2):
    wqkv, wout, wup, wdown = weights
    layers, width = wqkv.shape[0], wqkv.shape[1]
    hidden = wup.shape[2]
    sizes = (width, width, 3 * width, width, width, width, hidden, hidden)
    pieces = 3 * width // TILE + 1 + 2 * (hidden // TILE)
    fresh = tick == 0
    scratch = [pltpu.VMEM((rows, width), BF16), pltpu.VMEM((rows, width), F32), pltpu.VMEM((1, 3 * width), F32)]
    scratch += [pltpu.VMEM((layers, rows, size), BF16) for size in sizes]
    scratch += [pltpu.VMEM((layers, rows, 128), F32)] * 2
    scratch += [pltpu.SemaphoreType.DMA((layers, pieces)), pltpu.SemaphoreType.DMA((layers, 10)), pltpu.SemaphoreType.DMA]
    flops = 2 * rows * (wqkv.size + wout.size + wup.size + wdown.size)
    moved = 2 * (wqkv.size + wout.size + wup.size + wdown.size) + 2 * layers * rows * sum(sizes)
    total = first_in.shape[0]
    shapes = [jax.ShapeDtypeStruct(*k) for k in forward_shapes(layers, total, width, hidden)]
    out = pl.pallas_call(
        functools.partial(forward_kernel, tick, len(kept), rows, block, per_micro, unroll),
        out_shape=[jax.ShapeDtypeStruct((rows, width), BF16)] + shapes + [pltpu.VMEM(w.shape, BF16) for w in weights],
        in_specs=[SMEM, HBM, FREE, VMEM, VMEM, VMEM] + [HBM if fresh else VMEM] * 4 + [HBM] * len(kept),
        out_specs=[VMEM] + [HBM] * 11 + [VMEM] * 4,
        scratch_shapes=scratch,
        input_output_aliases={10 + i: 1 + i for i in range(len(kept))} | ({} if fresh else {6 + i: 12 + i for i in range(4)}),
        compiler_params=pltpu.CompilerParams(vmem_limit_bytes=LIMIT),
        cost_estimate=pl.CostEstimate(flops=flops, bytes_accessed=moved, transcendentals=0),
        name="section_forward",
    )(meta, first_in, recv, mask, gains, biases, *weights, *kept)
    return out[0], list(out[1:12]), list(out[12:])


def run_backward(tick, top, count, part, meta, token, last_in, recv, mask, gains, weights, kept, made, rows, per_micro,
                 block=240, unroll=8):
    wqkv, wout, wup, wdown = weights
    layers, width = wqkv.shape[0], wqkv.shape[1]
    hidden = wup.shape[2]
    n1, _, qkv, _, n2, _, u, _, r1, r2, _ = kept
    scratch = [pltpu.VMEM((rows, width), BF16), pltpu.VMEM((rows, width), F32), pltpu.VMEM((rows, width), F32),
               pltpu.VMEM((rows, width), BF16)]
    scratch += [pltpu.VMEM((layers, rows, size), BF16) for size in (width, 3 * width, width, hidden)]
    scratch += [pltpu.VMEM((layers, rows, 128), F32)] * 2
    scratch += [pltpu.VMEM((layers, rows, size), BF16) for size in (3 * width, width, hidden, width)]
    scratch += [pltpu.VMEM((layers, 8, 8 * width + hidden), F32)]
    scratch += [pltpu.SemaphoreType.DMA((layers, 6)), pltpu.SemaphoreType.DMA((layers, 8)), pltpu.SemaphoreType.DMA]
    loaded = part == 3
    if loaded:
        scratch.append(pltpu.SemaphoreType.DMA((4,)))
        scratch += [pltpu.VMEM((1,) + w.shape[1:], BF16) for w in weights]
    total = (wqkv.size + wout.size + wup.size + wdown.size) * count // layers
    shapes = [jax.ShapeDtypeStruct(*k) for k in backward_shapes(
        layers, last_in.shape[0], width, hidden, last_in.shape[0] // rows)]
    out = pl.pallas_call(
        functools.partial(backward_kernel, tick, top, count, part, len(made), rows, block, per_micro, unroll),
        out_shape=[jax.ShapeDtypeStruct((rows, width), BF16 if count == top + 1 and part != 1 else F32)] + shapes
        + ([] if loaded else [pltpu.VMEM(w.shape, BF16) for w in weights]),
        in_specs=[SMEM, FREE, HBM, FREE, VMEM, VMEM] + [HBM if loaded else VMEM] * 4 + [HBM] * 6 + [HBM] * len(made),
        out_specs=[VMEM] + [HBM] * 6 + ([] if loaded else [VMEM] * 4),
        scratch_shapes=scratch,
        input_output_aliases={16 + i: 1 + i for i in range(len(made))} | (
            {} if loaded else {6 + i: 7 + i for i in range(4)}),
        compiler_params=pltpu.CompilerParams(vmem_limit_bytes=LAST_LIMIT if loaded else LIMIT),
        cost_estimate=NO_COST,
        name="section_backward",
    )(meta, token, last_in, recv, mask, gains, *weights, n1, qkv, n2, u, r1, r2, *made)
    return out[0], list(out[1:7]), weights if loaded else list(out[7:])


def run_gradient(jobs, cuts, tick, meta, token, arrays, grid, small=None):
    rows = arrays[jobs[0][0]].shape[1]
    inputs = list(arrays) + ([] if small is None else [small])
    heights = []
    for spot, (left, right, _, _) in enumerate(jobs):
        if spot in cuts:
            heights.append(0)
        heights[-1] += arrays[left].shape[2] // grid * (arrays[right].shape[2] // TILE)
    tiles = sum(arrays[left].shape[2] * arrays[right].shape[2] // TILE ** 2 for left, right, _, _ in jobs)
    flops = 2 * rows * tiles * TILE ** 2
    if small is not None:
        heights[-1] += small.shape[2]
    width = arrays[jobs[0][1]].shape[2]
    patch = next((inputs[job[3]] for job in jobs if job[3] is not None), jax.ShapeDtypeStruct((16, 128), BF16))
    scratch = [pltpu.VMEM(arrays[left].shape[1:], BF16) for left, _, _, _ in jobs]
    scratch += [pltpu.VMEM(arrays[right].shape[1:], BF16) for _, right, _, _ in jobs]
    scratch += [pltpu.VMEM((tiles, TILE, TILE), BF16), pltpu.VMEM(patch.shape, patch.dtype),
                pltpu.SemaphoreType.DMA((len(jobs), 2, 4)), pltpu.SemaphoreType.DMA((tiles + 1, 2)), pltpu.SemaphoreType.DMA]
    if small is not None:
        scratch.append(pltpu.VMEM(small.shape, small.dtype))
    shapes = [jax.ShapeDtypeStruct((grid // 2, height, TILE), BF16) for height in heights for _ in range(2)]
    return pl.pallas_call(
        functools.partial(gradient_kernel, jobs, cuts, grid, tick, len(inputs)),
        out_shape=shapes,
        in_specs=[SMEM, FREE] + [HBM] * len(inputs),
        out_specs=[HBM] * len(shapes),
        scratch_shapes=scratch,
        compiler_params=pltpu.CompilerParams(vmem_limit_bytes=LAST_LIMIT),
        cost_estimate=NO_COST,
        name="weight_gradient",
    )(meta, token, *inputs)


def split_kernel(bit, inner, table, keep, recv, token, send_o, keep_o, keep_s, recv_s, sems):
    blocks = keep.shape[0]
    mine = table[bit]

    def loads(spot):
        half, place = spot // (blocks // 2), spot % (blocks // 2)
        pick = 1 - mine if half == 0 else mine
        source = (place // inner * 2 + pick) * inner + place % inner
        return [pltpu.make_async_copy(origin.at[source], target.at[spot], sems.at[which, spot])
                for which, (origin, target) in enumerate(((keep, keep_s), (recv, recv_s)))]

    def store(spot):
        output = send_o if spot < blocks // 2 else keep_o
        return pltpu.make_async_copy(keep_s.at[spot], output.at[spot % (blocks // 2)], sems.at[2, spot])

    for spot in range(blocks):
        for copy in loads(spot):
            copy.start()
    for spot in range(blocks):
        for copy in loads(spot):
            copy.wait()
        keep_s[spot] = (keep_s[spot].astype(F32) + recv_s[spot].astype(F32)).astype(BF16)
        store(spot).start()
    for spot in range(blocks):
        store(spot).wait()


def run_split(table, bit, keep, recv, inner, token):
    blocks, height, width = keep.shape
    shape = jax.ShapeDtypeStruct((blocks // 2, height, width), BF16)
    return pl.pallas_call(
        functools.partial(split_kernel, bit, inner),
        out_shape=[shape, shape],
        in_specs=[SMEM, HBM, HBM, FREE],
        out_specs=[HBM, HBM],
        scratch_shapes=[pltpu.VMEM(keep.shape, BF16), pltpu.VMEM(keep.shape, BF16),
                        pltpu.SemaphoreType.DMA((3, blocks))],
        compiler_params=pltpu.CompilerParams(vmem_limit_bytes=LAST_LIMIT),
        cost_estimate=NO_COST,
        name="split_sum",
    )(table, keep, recv, token)


def last_kernel(keep, recv, token, out):
    out[...] = keep[...].astype(F32) + recv[...].astype(F32)


def run_last(keep, recv, token):
    _, height, width = keep.shape
    tall = height // 2 if height % 32 == 0 else height
    spec = pl.BlockSpec((None, tall, width), lambda j: (0, j, 0))
    return pl.pallas_call(
        last_kernel,
        out_shape=jax.ShapeDtypeStruct((height, width), F32),
        grid=(height // tall,),
        in_specs=[spec, spec, FREE],
        out_specs=pl.BlockSpec((tall, width), lambda j: (j, 0)),
        compiler_params=pltpu.CompilerParams(vmem_limit_bytes=LAST_LIMIT),
        cost_estimate=NO_COST,
        name="last_sum",
    )(keep, recv, token)


PLAN = (
    "b0", "g1", "g2", "s1", "s2", "b1", "s3", "g3", "s1", "s5", "s3", "s2", "s3", "s1", "s4", "s5", "s3", "s2", "g0", "s1", "s5", "s0", "s4", "s2", "g4", "s5", "s6", "s0", "s4", "s6", "s0", "s4", "s6", "s0", "s6",
)
TURNS = "AABAAAA"


def hop(value, steps):
    count = lax.axis_size("section")
    pairs = [(s, s + steps) for s in range(count) if 0 <= s + steps < count]
    return lax.ppermute(value, "section", pairs) if pairs else jnp.zeros_like(value)


class Piece:
    def __init__(self, send, keep, order, table):
        self.table = table
        self.bits = lax.axis_size("dp").bit_length() - 1
        self.left = list(reversed(range(1, self.bits)))
        self.order = list(order)
        self.send, self.keep = send, keep
        self.recv = None

    def start(self):
        bit = self.order.pop(0)
        pairs = [(device, device ^ (1 << bit)) for device in range(lax.axis_size("dp"))]
        self.recv = lax.ppermute(self.send, "dp", pairs)
        return self.send

    def finish(self, token):
        recv, self.recv = self.recv, None
        if not self.order:
            self.keep = run_last(self.keep, recv, token)
            return self.keep
        bit = self.order[0]
        spot = self.left.index(bit)
        self.left.remove(bit)
        self.send, self.keep = run_split(self.table, bit, self.keep, recv, 2 ** (len(self.left) - spot), token)
        return self.send


def shards(
    section_input, out_cotangent, series_counts, norm_gains, biases,
    qkv_weight, out_weight, up_weight, down_weight,
):
    sections = lax.axis_size("section")
    section = lax.axis_index("section")
    group = lax.axis_size("dp")
    micro_count, per_micro, width = section_input.shape
    layers = qkv_weight.shape[0]
    hidden = up_weight.shape[2]
    total = micro_count * per_micro
    rows = MICROS * per_micro
    chunks = micro_count // MICROS
    ticks = chunks + 2 * (sections - 1)
    weights = (qkv_weight, out_weight, up_weight, down_weight)
    last_weights = weights
    mask = mask_table()
    counts = jnp.broadcast_to(series_counts.reshape(1, micro_count), (ticks, micro_count))
    tick_ids = jnp.arange(ticks, dtype=jnp.int32)
    core = jnp.broadcast_to(lax.axis_index("dp") & 1, (ticks, 1))

    def table(place):
        chunk = tick_ids - 2 * place
        active = (chunk >= 0) & (chunk < chunks)
        edge = jnp.broadcast_to(place == 0, (ticks,))
        columns = [active, jnp.clip(chunk, 0, chunks - 1), edge]
        columns = [column.astype(jnp.int32)[:, None] for column in columns]
        return jnp.concatenate(columns + [counts, core], axis=1)

    own_bits = (lax.axis_index("dp") >> jnp.arange(group.bit_length() - 1, dtype=jnp.int32)) & 1
    tables = (table(section), table(sections - 1 - section), mask, own_bits)
    forward_meta, backward_meta, mask, bit_table = lax.optimization_barrier(tables)
    entering = section_input.reshape(total, width)
    leaving = out_cotangent.reshape(total, width)
    meta = forward_meta
    arrived = [entering] * 2
    kept = []
    for tick in range(ticks):
        sent, kept, weights = run_forward(
            tick, meta, entering, arrived[tick], mask, norm_gains, biases, weights, kept, rows, per_micro)
        if tick + 2 < ticks:
            arrived.append(hop(sent, 1))
    meta = backward_meta
    arrived = [leaving] * 2
    made = []

    def back(tick, top, count, part, recv, token, made, weights):
        return run_backward(tick, top, count, part, meta, token, leaving, recv, mask, norm_gains, weights, kept, made,
                            rows, per_micro)

    final = ticks - 1
    top = layers - 1
    for tick in range(final):
        sent, made, weights = back(tick, top, layers, 0, arrived[tick], arrived[tick], made, weights)
        if tick + 2 < ticks:
            arrived.append(hop(sent, -1))
    e1, attended, e2, hidden_rows, outputs = kept[1], kept[3], kept[5], kept[7], kept[10]
    top = layers - 1
    bits = group.bit_length() - 1
    near = range(bits)

    def gradient(groups, orders, token, small=None, patch=None):
        dqkv, da, du, df = made[:4]
        table_of = {"qkv": (e1, dqkv), "out": (attended, da), "up": (e2, du), "down": (hidden_rows, df)}
        arrays, jobs, cuts = [], [], []
        for members in groups:
            cuts.append(len(jobs))
            for name, level in members:
                arrays += table_of[name]
                jobs.append((len(arrays) - 2, len(arrays) - 1, level, None))
        if patch is not None:
            jobs[-1] = jobs[-1][:3] + (len(arrays),)
            arrays.append(patch)
        out = run_gradient(tuple(jobs), tuple(cuts), final, meta, token, arrays, group, small)
        return [Piece(*out[2 * spot:2 * spot + 2], order, bit_table) for spot, order in enumerate(orders)]

    token = arrived[final]
    pieces = {}

    def begin(names, groups, **more):
        nonlocal token
        fresh = gradient(groups, [orders[name] for name in names], token, **more)
        for name, piece in zip(names, fresh):
            pieces[name] = piece
            token = piece.start()

    def step(*names):
        nonlocal token
        for name in names:
            token = pieces[name].finish(token)
            if pieces[name].order:
                pieces[name].start()

    far = [0, 2, 1] + list(range(3, bits)) if bits > 3 else list(near)
    orders = [near if turn == "A" else far for turn in TURNS]
    calls = {
        0: ([0], [[("down", top)]]),
        1: ([1], [[("up", top), ("out", top)]]),
        2: ([2, 3], [[("qkv", top)], [("down", 0)]]),
        3: ([4, 5], [[("qkv", 0)], [("up", 0)]]),
        4: ([6], [[("out", 0)]]),
    }
    flow = arrived[final]
    for entry in PLAN:
        kind, which = entry[0], int(entry[1:])
        if kind == "b":
            layer, part, now = ((top, 0, weights), (0, 3, last_weights))[which]
            flow, made, _ = back(final, layer, 1, part, flow, token, made, now)
            token = flow
            if which == 1:
                sums, input_grads = made[4:]
                cut = biases.shape[1]
                small = jnp.sum(sums, axis=(0, 2)).astype(BF16)
                small = jnp.concatenate(
                    [small[:, :cut].reshape(layers, group, -1), small[:, cut:].reshape(layers, group, -1)], axis=2)
                used = small.shape[2]
                small = jnp.swapaxes(small, 0, 1).reshape(group, layers * used)
                small = jnp.pad(small, ((0, 0), (0, 8 * TILE - layers * used))).reshape(group // 2, 2, 8, TILE)
        elif kind == "g":
            more = {2: {"patch": flow}, 4: {"small": small} if which == 4 else {}}.get(which, {})
            begin(*calls[which], **more)
        else:
            step(which)
    for piece in pieces.values():
        while piece.order or piece.recv is not None:
            token = piece.finish(token)
            if piece.order:
                piece.start()

    def unpack(packed, at, deep, wide):
        block = deep // group
        tall = block * (wide // TILE)
        return jnp.swapaxes(packed[at:at + tall].reshape(wide // TILE, block, TILE), 0, 1).reshape(block, wide)

    up_rows, out_rows = width // group * (hidden // TILE), width // group
    got = {name: piece.keep for name, piece in pieces.items()}
    grad_down = [unpack(got[3], 0, hidden, width), unpack(got[0], 0, hidden, width)]
    grad_up = [unpack(got[5], 0, width, hidden), unpack(got[1], 0, width, hidden)]
    grad_out = [unpack(got[6], 0, width, width), unpack(got[1], up_rows, width, width)]
    grad_qkv = [unpack(got[4], 0, width, 3 * width), unpack(got[2], 0, width, 3 * width)]
    small = got[6][out_rows:].reshape(-1)[:layers * used].reshape(layers, used)
    return (
        outputs.reshape(1, micro_count, per_micro, width),
        input_grads.reshape(1, micro_count, per_micro, width),
        small[:, cut // group:],
        small[:, :cut // group],
        jnp.stack(grad_qkv), jnp.stack(grad_out), jnp.stack(grad_up), jnp.stack(grad_down),
    )


def solution(mesh):
    stacked = P("section", None, None)
    return jax.shard_map(
        shards,
        mesh=mesh,
        in_specs=(P(None, "dp", None), P(None, "dp", None), P(None, "dp"),
                  P("section", None), P("section", None), stacked, stacked, stacked, stacked),
        out_specs=(P("section", None, "dp", None), P("section", None, "dp", None),
                   P("section", "dp"), P("section", "dp"),
                   P("section", "dp", None), P("section", "dp", None),
                   P("section", "dp", None), P("section", "dp", None)),
        check_vma=False,
    )
```
